128 devices in a mesh: dp: 8 (over x, y_lo), expert: 16 (over z, y_hi, core).
Axes of the slice: x: 4, y: 4 (y_hi: 2, y_lo: 2; y = y_hi * 2 + y_lo), z: 4, core: 2. Of those that a mesh axis runs over, the one named last changes fastest.
Arguments:
- tokens: bfloat16 [32768, 1536], P(('dp', 'expert')), may hold values from -24 to 24
- cotangent: bfloat16 [32768, 1536], P(('dp', 'expert')), may hold values from -0.59765625 to 0.59765625
- chosen: int32 [512, 16, 8], P(('dp', 'expert')), may hold values from 0 to 63, as said below
- w_router: bfloat16 [1536, 16], replicated, may hold values from -0.15625 to 0.15625
- w_gate: bfloat16 [16, 1536, 1024], P('expert', 'dp'), may hold values from -0.15625 to 0.15625
- w_up: bfloat16 [16, 1536, 1024], P('expert', 'dp'), may hold values from -0.15625 to 0.15625
- w_down: bfloat16 [16, 1024, 1536], P('expert', 'dp'), may hold values from -0.1875 to 0.1875
Outputs:
- mixed: bfloat16 [32768, 1536], P(('dp', 'expert'))
- grad_tokens: bfloat16 [32768, 1536], P(('dp', 'expert'))
- grad_gate: float32 [16, 1536, 1024], P('expert', 'dp')
- grad_up: float32 [16, 1536, 1024], P('expert', 'dp')
- down_weight_gradient: float32 [16, 1024, 1536], P('expert', 'dp')
- grad_router: float32 [1536, 16], replicated
The draws below stay inside these ranges and needn't reach their ends.
Inputs may be any that keep to these rules, and one draw needn't show every extreme that they name: `chosen`: for each aligned block of 64 token rows and each expert, 8 different row numbers within the block; so every device has exactly 32 slots for each expert.
All inputs are finite; a program needn't handle non-finite values.
Results may differ from the reference program's by a relative error of at most 0.017.
Values may be sent and summed in bfloat16 or wider, within the bound.
A program may use at most 128 MiB of HBM per device.

```python
import jax
import jax.numpy as jnp
from jax import lax

D = 1536
H = 1024
BLOCK = 64
EXPERTS = 16
PICK = 8
TOKENS = 32768
NBLK = 512


def draw_chosen(key, part):
    scores = jax.random.randint(key, (NBLK, EXPERTS, BLOCK), 0, 1048576, dtype=jnp.int32)
    ranked = scores * BLOCK + lax.broadcasted_iota(jnp.int32, (NBLK, EXPERTS, BLOCK), 2)
    _, indices = lax.top_k(ranked, PICK)
    return indices.astype(jnp.int32)


def raised(array, stream_key, source, target, parts, factor):
    owner, partner = [(jnp.arange(array.shape[position]) // (array.shape[position] // parts)).reshape([-1 if axis == position else 1 for axis in range(array.ndim)]) for position in (source, target)]
    chosen = jax.random.permutation(stream_key, parts)[partner]
    strong = (owner == chosen) | (owner == (partner + parts // 2) % parts)
    return jnp.where(strong, factor * array, array)


def block_scale(stream_key, extent, cuts, smallest, largest):
    factor_of, own = 1.0, jax.random.fold_in(stream_key, 6)
    for dim, blocks in cuts:
        draws = jnp.exp(jax.random.uniform(jax.random.fold_in(own, dim), (blocks,), jnp.float32, smallest / len(cuts), largest / len(cuts)))
        factor_of = factor_of * jnp.repeat(draws, extent[dim] // blocks).reshape([-1 if axis == dim else 1 for axis in range(len(extent))])
    return factor_of


def gaussian(rng, shape, deviation, limit, cuts=(), held_as=jnp.bfloat16):
    result = deviation * jax.random.normal(rng, shape, jnp.float32)
    if cuts:
        result = result * block_scale(rng, shape, cuts, -0.22, 0.18)
    return jnp.clip(result, -limit, limit).astype(held_as)


def heavy_noise(stream_key, extent, deviation, limit, shards, heavy, held_as=jnp.bfloat16):
    result = deviation * jax.random.normal(stream_key, extent, jnp.float32)
    if shards:
        result = result * block_scale(stream_key, extent, shards, -0.22, 0.18)
    return jnp.clip(raised(result, jax.random.fold_in(stream_key, 3), *heavy), -limit, limit).astype(held_as)


def setup_inputs(seed: int = 0) -> dict:
    arg_keys = jax.random.split(jax.random.key(seed), 8)
    tokens = heavy_noise(arg_keys[0], (TOKENS, D), 1.0, 24.0, ((0, 128),), (0, 1, 128, 5.5))
    cotangent = gaussian(arg_keys[1], (TOKENS, D), 0.1, 0.59765625, ((0, 128),))
    chosen = draw_chosen(jax.random.fold_in(arg_keys[7], 71), 0)
    w_router = gaussian(arg_keys[3], (D, EXPERTS), D ** -0.5, 0.15625)
    w_gate = gaussian(arg_keys[4], (EXPERTS, D, H), D ** -0.5, 0.15625, ((0, 16), (1, 8)))
    w_up = gaussian(arg_keys[5], (EXPERTS, D, H), D ** -0.5, 0.15625, ((0, 16), (1, 8)))
    w_down = gaussian(arg_keys[6], (EXPERTS, H, D), H ** -0.5, 0.1875, ((0, 16), (1, 8)))
    return {"tokens": tokens, "cotangent": cotangent, "chosen": chosen, "w_router": w_router, "w_gate": w_gate, "w_up": w_up, "w_down": w_down}


def reference(tokens, cotangent, chosen, w_router, w_gate, w_up, w_down):
    logits = jnp.dot(tokens, w_router, preferred_element_type=jnp.float32)
    gate_values = jax.nn.sigmoid(logits)
    offsets = (jnp.arange(NBLK, dtype=jnp.int32) * BLOCK)[:, None]

    def per_expert(carried, inputs):
        combined_total, gradient_total = carried
        pick_rows, gate_column, gate_w, up_w, down_w = inputs
        slot_rows = (pick_rows + offsets).reshape(-1).astype(jnp.int32)
        chosen_rows = tokens[slot_rows]
        slot_gate_values = gate_column[slot_rows]
        pre_gate = jnp.dot(chosen_rows, gate_w, preferred_element_type=jnp.float32)
        pre_up = jnp.dot(chosen_rows, up_w, preferred_element_type=jnp.float32)
        silu_gate = jax.nn.silu(pre_gate)
        hidden = (silu_gate * pre_up).astype(jnp.bfloat16)
        expert_out = jnp.dot(hidden, down_w, preferred_element_type=jnp.float32).astype(jnp.bfloat16)
        combined_total = combined_total.at[slot_rows].add(slot_gate_values[:, None] * expert_out.astype(jnp.float32))
        cot_rows = cotangent[slot_rows]
        scaled_cot = (slot_gate_values[:, None] * cot_rows.astype(jnp.float32)).astype(jnp.bfloat16)
        slot_dots = jnp.sum(cot_rows.astype(jnp.float32) * expert_out.astype(jnp.float32), axis=1)
        dgate_column = jnp.zeros((TOKENS,), jnp.float32).at[slot_rows].set(slot_dots)
        d_hidden = jnp.dot(scaled_cot, down_w.T, preferred_element_type=jnp.float32)
        gate_sigmoid = jax.nn.sigmoid(pre_gate)
        d_pre_gate = (d_hidden * pre_up * gate_sigmoid * (1.0 + pre_gate * (1.0 - gate_sigmoid))).astype(jnp.bfloat16)
        d_pre_up = (d_hidden * silu_gate).astype(jnp.bfloat16)
        d_rows = (jnp.dot(d_pre_gate, gate_w.T, preferred_element_type=jnp.float32)
                  + jnp.dot(d_pre_up, up_w.T, preferred_element_type=jnp.float32)).astype(jnp.bfloat16)
        gradient_total = gradient_total.at[slot_rows].add(d_rows.astype(jnp.float32))
        gate_grad = jnp.dot(chosen_rows.T, d_pre_gate, preferred_element_type=jnp.float32)
        up_grad = jnp.dot(chosen_rows.T, d_pre_up, preferred_element_type=jnp.float32)
        down_grad = jnp.dot(hidden.T, scaled_cot, preferred_element_type=jnp.float32)
        return (combined_total, gradient_total), (dgate_column, gate_grad, up_grad, down_grad)

    start_sums = (jnp.zeros((TOKENS, D), jnp.float32), jnp.zeros((TOKENS, D), jnp.float32))
    inputs = (jnp.transpose(chosen, (1, 0, 2)), gate_values.T, w_gate, w_up, w_down)
    (combined_total, gradient_total), outputs = lax.scan(per_expert, start_sums, inputs)
    dgate_columns, grad_gate, grad_up, down_weight_gradient = outputs
    dgate = dgate_columns.T
    d_logit = (dgate * gate_values * (1.0 - gate_values)).astype(jnp.bfloat16)
    grad_tokens = (gradient_total + jnp.dot(d_logit, w_router.T, preferred_element_type=jnp.float32)).astype(jnp.bfloat16)
    grad_router = jnp.dot(tokens.T, d_logit, preferred_element_type=jnp.float32)
    return (combined_total.astype(jnp.bfloat16), grad_tokens, grad_gate, grad_up, down_weight_gradient, grad_router)
```

```python
import functools

import jax
import jax.numpy as jnp
from jax import lax
from jax.experimental import pallas as pl
from jax.experimental.pallas import tpu as pltpu
from jax.sharding import PartitionSpec as P

MESH = pl.DeviceIdType.MESH


def _gather_kernel(n, *refs):
    count = (len(refs) - 3) // 2
    srcs, dsts = refs[:count], refs[count : 2 * count]
    send_sem, recv_sem, local_sem = refs[2 * count :]
    me = lax.axis_index("dp")
    ex = lax.axis_index("expert")
    barrier = pltpu.get_barrier_semaphore()
    for k in range(1, n):
        pl.semaphore_signal(barrier, inc=1, device_id=(lax.rem(me + k, n), ex), device_id_type=MESH)
    pl.semaphore_wait(barrier, n - 1)
    copies = []
    for a in range(count):
        rows = srcs[a].shape[0]
        slot = dsts[a].at[pl.ds(me * rows, rows)]
        local = pltpu.make_async_copy(srcs[a], slot, local_sem.at[a])
        local.start()
        copies.append(local)
        for k in range(1, n):
            remote = pltpu.make_async_remote_copy(
                src_ref=srcs[a],
                dst_ref=slot,
                send_sem=send_sem.at[a, k],
                recv_sem=recv_sem.at[a, k],
                device_id=(lax.rem(me + k, n), ex),
                device_id_type=MESH,
            )
            remote.start()
            copies.append(remote)
    for c in copies:
        c.wait()


def dp_all_gather(shards, n):
    count = len(shards)
    return pl.pallas_call(
        functools.partial(_gather_kernel, n),
        out_shape=[jax.ShapeDtypeStruct((n * s.shape[0],) + s.shape[1:], s.dtype) for s in shards],
        in_specs=[pl.BlockSpec(memory_space=pl.ANY)] * count,
        out_specs=[pl.BlockSpec(memory_space=pl.ANY)] * count,
        scratch_shapes=[
            pltpu.SemaphoreType.DMA((count, n)),
            pltpu.SemaphoreType.DMA((count, n)),
            pltpu.SemaphoreType.DMA((count,)),
        ],
        compiler_params=pltpu.CompilerParams(collective_id=0, has_side_effects=True),
    )(*shards)


def _scatter_kernel(n, *refs):
    count = (len(refs) - 3) // 2
    srcs, dsts = refs[:count], refs[count : 2 * count]
    send_sem, recv_sem, local_sem = refs[2 * count :]
    me = lax.axis_index("dp")
    ex = lax.axis_index("expert")
    barrier = pltpu.get_barrier_semaphore()
    for k in range(1, n):
        pl.semaphore_signal(barrier, inc=1, device_id=(lax.rem(me + k, n), ex), device_id_type=MESH)
    pl.semaphore_wait(barrier, n - 1)
    copies = []
    for a in range(count):
        rows = dsts[a].shape[1]
        local = pltpu.make_async_copy(
            srcs[a].at[pl.ds(me * rows, rows)], dsts[a].at[me], local_sem.at[a]
        )
        local.start()
        copies.append(local)
        for k in range(1, n):
            peer = lax.rem(me + k, n)
            remote = pltpu.make_async_remote_copy(
                src_ref=srcs[a].at[pl.ds(peer * rows, rows)],
                dst_ref=dsts[a].at[me],
                send_sem=send_sem.at[a, k],
                recv_sem=recv_sem.at[a, k],
                device_id=(peer, ex),
                device_id_type=MESH,
            )
            remote.start()
            copies.append(remote)
    for c in copies:
        c.wait()


def dp_reduce_scatter(partials, n):
    count = len(partials)
    received = pl.pallas_call(
        functools.partial(_scatter_kernel, n),
        out_shape=[
            jax.ShapeDtypeStruct((n, p.shape[0] // n) + p.shape[1:], p.dtype) for p in partials
        ],
        in_specs=[pl.BlockSpec(memory_space=pl.ANY)] * count,
        out_specs=[pl.BlockSpec(memory_space=pl.ANY)] * count,
        scratch_shapes=[
            pltpu.SemaphoreType.DMA((count, n)),
            pltpu.SemaphoreType.DMA((count, n)),
            pltpu.SemaphoreType.DMA((count,)),
        ],
        compiler_params=pltpu.CompilerParams(collective_id=1, has_side_effects=True),
    )(*partials)
    return [jnp.sum(r.astype(jnp.float32), axis=0) for r in received]


def to_blocks(slot_array, num_blocks, pick_count):
    expert_count = slot_array.shape[0]
    trailing = slot_array.shape[2:]
    grouped = slot_array.reshape((expert_count, num_blocks, pick_count) + trailing)
    axis_order = (1, 0, 2) + tuple(range(3, 3 + len(trailing)))
    return jnp.transpose(grouped, axis_order).reshape(
        (num_blocks, expert_count * pick_count) + trailing
    )


def weight_grads(expert_rows, hidden, expert_cot, d_pre_gate, d_pre_up, n):
    hidden_activations = hidden.shape[2]
    both_grads = jnp.concatenate([d_pre_gate, d_pre_up], axis=2)
    in_part = jnp.einsum(
        "erc,erk->ck", expert_rows, both_grads, preferred_element_type=jnp.float32
    ).astype(jnp.bfloat16)
    out_part = jnp.einsum(
        "erc,erd->cd", hidden, expert_cot, preferred_element_type=jnp.float32
    ).astype(jnp.bfloat16)
    in_share, out_share = dp_reduce_scatter([in_part, out_part], n)
    grad_gate = in_share[None, :, :hidden_activations]
    grad_up = in_share[None, :, hidden_activations:]
    down_weight_gradient = out_share[None]
    return (grad_gate, grad_up, down_weight_gradient)


def body(tokens, cotangent, chosen, w_router, w_gate, w_up, w_down):
    tok_rows, model_width = tokens.shape
    num_blocks, expert_count, pick_count = chosen.shape
    block_rows = tok_rows // num_blocks
    slot_count = num_blocks * pick_count
    logits = jnp.dot(tokens, w_router, preferred_element_type=jnp.float32)
    gate_values = jax.nn.sigmoid(logits)
    offsets = (jnp.arange(num_blocks, dtype=jnp.int32) * block_rows)[:, None, None]
    slot_rows = jnp.transpose(chosen + offsets, (1, 0, 2)).reshape(expert_count, slot_count)
    picked = tokens[slot_rows]
    slot_gate_values = jnp.take_along_axis(gate_values.T, slot_rows, axis=1)
    cot_rows = cotangent[slot_rows]
    scaled_cot = (slot_gate_values[:, :, None] * cot_rows.astype(jnp.float32)).astype(jnp.bfloat16)
    n = lax.axis_size("dp")
    full_gate, full_up, full_down = (
        g[None] for g in dp_all_gather([w_gate[0], w_up[0], w_down[0]], n)
    )
    expert_rows = lax.all_to_all(picked, "expert", split_axis=0, concat_axis=1, tiled=True)
    pre_gate = jnp.einsum(
        "erd,edh->erh", expert_rows, full_gate, preferred_element_type=jnp.float32
    )
    pre_up = jnp.einsum("erd,edh->erh", expert_rows, full_up, preferred_element_type=jnp.float32)
    silu_gate = jax.nn.silu(pre_gate)
    hidden = (silu_gate * pre_up).astype(jnp.bfloat16)
    expert_out = jnp.einsum(
        "erh,ehd->erd", hidden, full_down, preferred_element_type=jnp.float32
    ).astype(jnp.bfloat16)
    returned = lax.all_to_all(expert_out, "expert", split_axis=1, concat_axis=0, tiled=True)
    expert_cot = lax.all_to_all(scaled_cot, "expert", split_axis=0, concat_axis=1, tiled=True)
    back_gate, back_up, back_down = (full_gate, full_up, full_down)
    d_hidden = jnp.einsum("erd,ehd->erh", expert_cot, back_down, preferred_element_type=jnp.float32)
    gate_sigmoid = jax.nn.sigmoid(pre_gate)
    d_pre_gate = (
        d_hidden * pre_up * gate_sigmoid * (1.0 + pre_gate * (1.0 - gate_sigmoid))
    ).astype(jnp.bfloat16)
    d_pre_up = (d_hidden * silu_gate).astype(jnp.bfloat16)
    d_rows = (
        jnp.einsum("erh,edh->erd", d_pre_gate, back_gate, preferred_element_type=jnp.float32)
        + jnp.einsum("erh,edh->erd", d_pre_up, back_up, preferred_element_type=jnp.float32)
    ).astype(jnp.bfloat16)
    row_grads = lax.all_to_all(d_rows, "expert", split_axis=1, concat_axis=0, tiled=True)
    position_hits = chosen[:, :, :, None] == jnp.arange(block_rows, dtype=jnp.int32)
    indicator_matrix = position_hits.reshape(num_blocks, expert_count * pick_count, block_rows)
    gate_weighted_rows = to_blocks(slot_gate_values, num_blocks, pick_count)[
        :, :, None
    ] * to_blocks(returned, num_blocks, pick_count).astype(jnp.float32)
    mixed = (
        jnp.einsum(
            "wze,wzi->wei",
            indicator_matrix.astype(jnp.float32),
            gate_weighted_rows,
            precision=lax.Precision.HIGHEST,
        )
        .reshape(tok_rows, model_width)
        .astype(jnp.bfloat16)
    )
    slot_dots = jnp.sum(cot_rows.astype(jnp.float32) * returned.astype(jnp.float32), axis=2)
    dgate = jnp.einsum(
        "bept,ebp->bte",
        position_hits.astype(jnp.float32),
        slot_dots.reshape(expert_count, num_blocks, pick_count),
        precision=lax.Precision.HIGHEST,
    ).reshape(tok_rows, expert_count)
    d_logit = (dgate * gate_values * (1.0 - gate_values)).astype(jnp.bfloat16)
    gathered_grads = jnp.einsum(
        "wze,wzi->wei",
        indicator_matrix.astype(jnp.bfloat16),
        to_blocks(row_grads, num_blocks, pick_count),
        preferred_element_type=jnp.float32,
    ).reshape(tok_rows, model_width)
    grad_tokens = (
        gathered_grads + jnp.dot(d_logit, w_router.T, preferred_element_type=jnp.float32)
    ).astype(jnp.bfloat16)
    grad_router = lax.psum(
        jnp.dot(tokens.T, d_logit, preferred_element_type=jnp.float32), ("dp", "expert")
    )
    grad_gate, grad_up, down_weight_gradient = weight_grads(
        expert_rows, hidden, expert_cot, d_pre_gate, d_pre_up, n
    )
    return (mixed, grad_tokens, grad_gate, grad_up, down_weight_gradient, grad_router)


def solution(mesh):
    placed = (
        P(("dp", "expert"), None),
        P(("dp", "expert"), None),
        P(("dp", "expert"), None, None),
        P(),
        P("expert", "dp", None),
        P("expert", "dp", None),
        P("expert", "dp", None),
    )
    return jax.shard_map(
        body,
        mesh=mesh,
        in_specs=placed,
        out_specs=(
            P(("dp", "expert"), None),
            P(("dp", "expert"), None),
            P("expert", "dp", None),
            P("expert", "dp", None),
            P("expert", "dp", None),
            P(),
        ),
        check_vma=False,
    )
```

```python
import functools

import jax
import jax.numpy as jnp
from jax import lax
from jax.experimental import pallas as pl
from jax.experimental.pallas import tpu as pltpu
from jax.sharding import PartitionSpec as P

MESH = pl.DeviceIdType.MESH


def _gather_kernel(n, *refs):
    count = (len(refs) - 3) // 2
    srcs, dsts = refs[:count], refs[count : 2 * count]
    send_sem, recv_sem, local_sem = refs[2 * count :]
    me = lax.axis_index("dp")
    ex = lax.axis_index("expert")
    barrier = pltpu.get_barrier_semaphore()
    for k in range(1, n):
        pl.semaphore_signal(barrier, inc=1, device_id=(lax.rem(me + k, n), ex), device_id_type=MESH)
    pl.semaphore_wait(barrier, n - 1)
    copies = []
    for a in range(count):
        rows = srcs[a].shape[0]
        slot = dsts[a].at[pl.ds(me * rows, rows)]
        local = pltpu.make_async_copy(srcs[a], slot, local_sem.at[a])
        local.start()
        copies.append(local)
        for k in range(1, n):
            remote = pltpu.make_async_remote_copy(
                src_ref=srcs[a],
                dst_ref=slot,
                send_sem=send_sem.at[a, k],
                recv_sem=recv_sem.at[a, k],
                device_id=(lax.rem(me + k, n), ex),
                device_id_type=MESH,
            )
            remote.start()
            copies.append(remote)
    for c in copies:
        c.wait()


def dp_all_gather(shards, n):
    count = len(shards)
    return pl.pallas_call(
        functools.partial(_gather_kernel, n),
        out_shape=[jax.ShapeDtypeStruct((n * s.shape[0],) + s.shape[1:], s.dtype) for s in shards],
        in_specs=[pl.BlockSpec(memory_space=pl.ANY)] * count,
        out_specs=[pl.BlockSpec(memory_space=pl.ANY)] * count,
        scratch_shapes=[
            pltpu.SemaphoreType.DMA((count, n)),
            pltpu.SemaphoreType.DMA((count, n)),
            pltpu.SemaphoreType.DMA((count,)),
        ],
        compiler_params=pltpu.CompilerParams(collective_id=0, has_side_effects=True),
    )(*shards)


def _exchange_kernel(n, n_scatter, *refs):
    count = (len(refs) - 3) // 2
    srcs, dsts = refs[:count], refs[count : 2 * count]
    send_sem, recv_sem, local_sem = refs[2 * count :]
    me = lax.axis_index("dp")
    ex = lax.axis_index("expert")
    barrier = pltpu.get_barrier_semaphore()
    for k in range(1, n):
        pl.semaphore_signal(barrier, inc=1, device_id=(lax.rem(me + k, n), ex), device_id_type=MESH)
    pl.semaphore_wait(barrier, n - 1)
    copies = []
    for a in range(count):
        rows = dsts[a].shape[1]
        if a < n_scatter:
            mine = srcs[a].at[pl.ds(me * rows, rows)]
        else:
            mine = srcs[a]
        local = pltpu.make_async_copy(mine, dsts[a].at[me], local_sem.at[a])
        local.start()
        copies.append(local)
        for k in range(1, n):
            peer = lax.rem(me + k, n)
            if a < n_scatter:
                part = srcs[a].at[pl.ds(peer * rows, rows)]
            else:
                part = srcs[a]
            remote = pltpu.make_async_remote_copy(
                src_ref=part,
                dst_ref=dsts[a].at[me],
                send_sem=send_sem.at[a, k],
                recv_sem=recv_sem.at[a, k],
                device_id=(peer, ex),
                device_id_type=MESH,
            )
            remote.start()
            copies.append(remote)
    for c in copies:
        c.wait()


def dp_exchange(partials, replicas, n):
    arrays = list(partials) + list(replicas)
    count = len(arrays)
    shapes = [(n, p.shape[0] // n) + p.shape[1:] for p in partials]
    shapes += [(n,) + r.shape for r in replicas]
    received = pl.pallas_call(
        functools.partial(_exchange_kernel, n, len(partials)),
        out_shape=[jax.ShapeDtypeStruct(s, a.dtype) for s, a in zip(shapes, arrays)],
        in_specs=[pl.BlockSpec(memory_space=pl.ANY)] * count,
        out_specs=[pl.BlockSpec(memory_space=pl.ANY)] * count,
        scratch_shapes=[
            pltpu.SemaphoreType.DMA((count, n)),
            pltpu.SemaphoreType.DMA((count, n)),
            pltpu.SemaphoreType.DMA((count,)),
        ],
        compiler_params=pltpu.CompilerParams(collective_id=1, has_side_effects=True),
    )(*arrays)
    return [jnp.sum(r.astype(jnp.float32), axis=0) for r in received]


def to_blocks(slot_array, num_blocks, pick_count):
    expert_count = slot_array.shape[0]
    trailing = slot_array.shape[2:]
    grouped = slot_array.reshape((expert_count, num_blocks, pick_count) + trailing)
    axis_order = (1, 0, 2) + tuple(range(3, 3 + len(trailing)))
    return jnp.transpose(grouped, axis_order).reshape(
        (num_blocks, expert_count * pick_count) + trailing
    )


def weight_grads(expert_rows, hidden, expert_cot, d_pre_gate, d_pre_up, router_part, n):
    hidden_activations = hidden.shape[2]
    both_grads = jnp.concatenate([d_pre_gate, d_pre_up], axis=2)
    in_part = jnp.einsum(
        "erc,erk->ck", expert_rows, both_grads, preferred_element_type=jnp.float32
    ).astype(jnp.bfloat16)
    out_part = jnp.einsum(
        "erc,erd->cd", hidden, expert_cot, preferred_element_type=jnp.float32
    ).astype(jnp.bfloat16)
    in_share, out_share, grad_router = dp_exchange([in_part, out_part], [router_part], n)
    grad_gate = in_share[None, :, :hidden_activations]
    grad_up = in_share[None, :, hidden_activations:]
    down_weight_gradient = out_share[None]
    return (grad_gate, grad_up, down_weight_gradient, grad_router)


def body(tokens, cotangent, chosen, w_router, w_gate, w_up, w_down):
    tok_rows, model_width = tokens.shape
    num_blocks, expert_count, pick_count = chosen.shape
    block_rows = tok_rows // num_blocks
    slot_count = num_blocks * pick_count
    logits = jnp.dot(tokens, w_router, preferred_element_type=jnp.float32)
    gate_values = jax.nn.sigmoid(logits)
    offsets = (jnp.arange(num_blocks, dtype=jnp.int32) * block_rows)[:, None, None]
    slot_rows = jnp.transpose(chosen + offsets, (1, 0, 2)).reshape(expert_count, slot_count)
    picked = tokens[slot_rows]
    slot_gate_values = jnp.take_along_axis(gate_values.T, slot_rows, axis=1)
    cot_rows = cotangent[slot_rows]
    scaled_cot = (slot_gate_values[:, :, None] * cot_rows.astype(jnp.float32)).astype(jnp.bfloat16)
    n = lax.axis_size("dp")
    full_gate, full_up, full_down = (
        g[None] for g in dp_all_gather([w_gate[0], w_up[0], w_down[0]], n)
    )
    expert_rows = lax.all_to_all(picked, "expert", split_axis=0, concat_axis=1, tiled=True)
    pre_gate = jnp.einsum(
        "erd,edh->erh", expert_rows, full_gate, preferred_element_type=jnp.float32
    )
    pre_up = jnp.einsum("erd,edh->erh", expert_rows, full_up, preferred_element_type=jnp.float32)
    silu_gate = jax.nn.silu(pre_gate)
    hidden = (silu_gate * pre_up).astype(jnp.bfloat16)
    expert_out = jnp.einsum(
        "erh,ehd->erd", hidden, full_down, preferred_element_type=jnp.float32
    ).astype(jnp.bfloat16)
    returned = lax.all_to_all(expert_out, "expert", split_axis=1, concat_axis=0, tiled=True)
    expert_cot = lax.all_to_all(scaled_cot, "expert", split_axis=0, concat_axis=1, tiled=True)
    back_gate, back_up, back_down = (full_gate, full_up, full_down)
    d_hidden = jnp.einsum("erd,ehd->erh", expert_cot, back_down, preferred_element_type=jnp.float32)
    gate_sigmoid = jax.nn.sigmoid(pre_gate)
    d_pre_gate = (
        d_hidden * pre_up * gate_sigmoid * (1.0 + pre_gate * (1.0 - gate_sigmoid))
    ).astype(jnp.bfloat16)
    d_pre_up = (d_hidden * silu_gate).astype(jnp.bfloat16)
    d_rows = (
        jnp.einsum("erh,edh->erd", d_pre_gate, back_gate, preferred_element_type=jnp.float32)
        + jnp.einsum("erh,edh->erd", d_pre_up, back_up, preferred_element_type=jnp.float32)
    ).astype(jnp.bfloat16)
    row_grads = lax.all_to_all(d_rows, "expert", split_axis=1, concat_axis=0, tiled=True)
    position_hits = chosen[:, :, :, None] == jnp.arange(block_rows, dtype=jnp.int32)
    indicator_matrix = position_hits.reshape(num_blocks, expert_count * pick_count, block_rows)
    gate_weighted_rows = to_blocks(slot_gate_values, num_blocks, pick_count)[
        :, :, None
    ] * to_blocks(returned, num_blocks, pick_count).astype(jnp.float32)
    mixed = (
        jnp.einsum(
            "wze,wzi->wei",
            indicator_matrix.astype(jnp.float32),
            gate_weighted_rows,
            precision=lax.Precision.HIGHEST,
        )
        .reshape(tok_rows, model_width)
        .astype(jnp.bfloat16)
    )
    slot_dots = jnp.sum(cot_rows.astype(jnp.float32) * returned.astype(jnp.float32), axis=2)
    dgate = jnp.einsum(
        "bept,ebp->bte",
        position_hits.astype(jnp.float32),
        slot_dots.reshape(expert_count, num_blocks, pick_count),
        precision=lax.Precision.HIGHEST,
    ).reshape(tok_rows, expert_count)
    d_logit = (dgate * gate_values * (1.0 - gate_values)).astype(jnp.bfloat16)
    gathered_grads = jnp.einsum(
        "wze,wzi->wei",
        indicator_matrix.astype(jnp.bfloat16),
        to_blocks(row_grads, num_blocks, pick_count),
        preferred_element_type=jnp.float32,
    ).reshape(tok_rows, model_width)
    grad_tokens = (
        gathered_grads + jnp.dot(d_logit, w_router.T, preferred_element_type=jnp.float32)
    ).astype(jnp.bfloat16)
    router_part = lax.psum(
        jnp.dot(tokens.T, d_logit, preferred_element_type=jnp.float32), "expert"
    )
    grad_gate, grad_up, down_weight_gradient, grad_router = weight_grads(
        expert_rows, hidden, expert_cot, d_pre_gate, d_pre_up, router_part, n
    )
    return (mixed, grad_tokens, grad_gate, grad_up, down_weight_gradient, grad_router)


def solution(mesh):
    placed = (
        P(("dp", "expert"), None),
        P(("dp", "expert"), None),
        P(("dp", "expert"), None, None),
        P(),
        P("expert", "dp", None),
        P("expert", "dp", None),
        P("expert", "dp", None),
    )
    return jax.shard_map(
        body,
        mesh=mesh,
        in_specs=placed,
        out_specs=(
            P(("dp", "expert"), None),
            P(("dp", "expert"), None),
            P("expert", "dp", None),
            P("expert", "dp", None),
            P("expert", "dp", None),
            P(),
        ),
        check_vma=False,
    )
```

```python
import functools

import jax
import jax.numpy as jnp
from jax import lax
from jax.experimental import pallas as pl
from jax.experimental.pallas import tpu as pltpu
from jax.sharding import PartitionSpec as P

MESH = pl.DeviceIdType.MESH


def _gather_kernel(n, *refs):
    count = (len(refs) - 3) // 2
    srcs, dsts = refs[:count], refs[count : 2 * count]
    send_sem, recv_sem, local_sem = refs[2 * count :]
    me = lax.axis_index("dp")
    ex = lax.axis_index("expert")
    barrier = pltpu.get_barrier_semaphore()
    for k in range(1, n):
        pl.semaphore_signal(barrier, inc=1, device_id=(lax.rem(me + k, n), ex), device_id_type=MESH)
    pl.semaphore_wait(barrier, n - 1)
    copies = []
    for a in range(count):
        rows = srcs[a].shape[0]
        slot = dsts[a].at[pl.ds(me * rows, rows)]
        local = pltpu.make_async_copy(srcs[a], slot, local_sem.at[a])
        local.start()
        copies.append(local)
        for k in range(1, n):
            remote = pltpu.make_async_remote_copy(
                src_ref=srcs[a],
                dst_ref=slot,
                send_sem=send_sem.at[a, k],
                recv_sem=recv_sem.at[a, k],
                device_id=(lax.rem(me + k, n), ex),
                device_id_type=MESH,
            )
            remote.start()
            copies.append(remote)
    for c in copies:
        c.wait()


def dp_all_gather(shards, n):
    count = len(shards)
    return pl.pallas_call(
        functools.partial(_gather_kernel, n),
        out_shape=[jax.ShapeDtypeStruct((n * s.shape[0],) + s.shape[1:], s.dtype) for s in shards],
        in_specs=[pl.BlockSpec(memory_space=pl.ANY)] * count,
        out_specs=[pl.BlockSpec(memory_space=pl.ANY)] * count,
        scratch_shapes=[
            pltpu.SemaphoreType.DMA((count, n)),
            pltpu.SemaphoreType.DMA((count, n)),
            pltpu.SemaphoreType.DMA((count,)),
        ],
        compiler_params=pltpu.CompilerParams(collective_id=0, has_side_effects=True),
    )(*shards)


def _exchange_kernel(n, n_scatter, *refs):
    count = (len(refs) - 3) // 2
    srcs, dsts = refs[:count], refs[count : 2 * count]
    send_sem, recv_sem, local_sem = refs[2 * count :]
    me = lax.axis_index("dp")
    ex = lax.axis_index("expert")
    barrier = pltpu.get_barrier_semaphore()
    for k in range(1, n):
        pl.semaphore_signal(barrier, inc=1, device_id=(lax.rem(me + k, n), ex), device_id_type=MESH)
    pl.semaphore_wait(barrier, n - 1)
    copies = []
    for a in range(count):
        rows = dsts[a].shape[1]
        if a < n_scatter:
            mine = srcs[a].at[pl.ds(me * rows, rows)]
        else:
            mine = srcs[a]
        local = pltpu.make_async_copy(mine, dsts[a].at[me], local_sem.at[a])
        local.start()
        copies.append(local)
        for k in range(1, n):
            peer = lax.rem(me + k, n)
            if a < n_scatter:
                part = srcs[a].at[pl.ds(peer * rows, rows)]
            else:
                part = srcs[a]
            remote = pltpu.make_async_remote_copy(
                src_ref=part,
                dst_ref=dsts[a].at[me],
                send_sem=send_sem.at[a, k],
                recv_sem=recv_sem.at[a, k],
                device_id=(peer, ex),
                device_id_type=MESH,
            )
            remote.start()
            copies.append(remote)
    for c in copies:
        c.wait()


def dp_exchange(partials, replicas, n):
    arrays = list(partials) + list(replicas)
    count = len(arrays)
    shapes = [(n, p.shape[0] // n) + p.shape[1:] for p in partials]
    shapes += [(n,) + r.shape for r in replicas]
    received = pl.pallas_call(
        functools.partial(_exchange_kernel, n, len(partials)),
        out_shape=[jax.ShapeDtypeStruct(s, a.dtype) for s, a in zip(shapes, arrays)],
        in_specs=[pl.BlockSpec(memory_space=pl.ANY)] * count,
        out_specs=[pl.BlockSpec(memory_space=pl.ANY)] * count,
        scratch_shapes=[
            pltpu.SemaphoreType.DMA((count, n)),
            pltpu.SemaphoreType.DMA((count, n)),
            pltpu.SemaphoreType.DMA((count,)),
        ],
        compiler_params=pltpu.CompilerParams(collective_id=1, has_side_effects=True),
    )(*arrays)
    return [jnp.sum(r.astype(jnp.float32), axis=0) for r in received]


def to_blocks(slot_array, num_blocks, pick_count):
    expert_count = slot_array.shape[0]
    trailing = slot_array.shape[2:]
    grouped = slot_array.reshape((expert_count, num_blocks, pick_count) + trailing)
    axis_order = (1, 0, 2) + tuple(range(3, 3 + len(trailing)))
    return jnp.transpose(grouped, axis_order).reshape(
        (num_blocks, expert_count * pick_count) + trailing
    )


def weight_grads(expert_rows, hidden, expert_cot, d_pre_gate, d_pre_up, router_part, n):
    hidden_activations = hidden.shape[2]
    both_grads = jnp.concatenate([d_pre_gate, d_pre_up], axis=2)
    in_part = jnp.einsum(
        "erc,erk->ck", expert_rows, both_grads, preferred_element_type=jnp.float32
    ).astype(jnp.bfloat16)
    out_part = jnp.einsum(
        "erc,erd->cd", hidden, expert_cot, preferred_element_type=jnp.float32
    ).astype(jnp.bfloat16)
    in_share, out_share, grad_router = dp_exchange([in_part, out_part], [router_part], n)
    grad_gate = in_share[None, :, :hidden_activations]
    grad_up = in_share[None, :, hidden_activations:]
    down_weight_gradient = out_share[None]
    return (grad_gate, grad_up, down_weight_gradient, grad_router)


def body(tokens, cotangent, chosen, w_router, w_gate, w_up, w_down):
    tok_rows, model_width = tokens.shape
    num_blocks, expert_count, pick_count = chosen.shape
    block_rows = tok_rows // num_blocks
    slot_count = num_blocks * pick_count
    logits = jnp.dot(tokens, w_router, preferred_element_type=jnp.float32)
    gate_values = jax.nn.sigmoid(logits)
    offsets = (jnp.arange(num_blocks, dtype=jnp.int32) * block_rows)[:, None, None]
    slot_rows = jnp.transpose(chosen + offsets, (1, 0, 2)).reshape(expert_count, slot_count)
    picked = tokens[slot_rows]
    slot_gate_values = jnp.take_along_axis(gate_values.T, slot_rows, axis=1)
    cot_rows = cotangent[slot_rows]
    scaled_cot = (slot_gate_values[:, :, None] * cot_rows.astype(jnp.float32)).astype(jnp.bfloat16)
    n = lax.axis_size("dp")
    full_gate, full_up, full_down = (
        g[None] for g in dp_all_gather([w_gate[0], w_up[0], w_down[0]], n)
    )
    expert_count_axis = lax.axis_size("expert")
    expert_rows = lax.all_to_all(picked, "expert", 0, 0, tiled=True).reshape(1, -1, model_width)
    pre_gate = jnp.einsum(
        "erd,edh->erh", expert_rows, full_gate, preferred_element_type=jnp.float32
    )
    pre_up = jnp.einsum("erd,edh->erh", expert_rows, full_up, preferred_element_type=jnp.float32)
    silu_gate = jax.nn.silu(pre_gate)
    hidden = (silu_gate * pre_up).astype(jnp.bfloat16)
    expert_out = jnp.einsum(
        "erh,ehd->erd", hidden, full_down, preferred_element_type=jnp.float32
    ).astype(jnp.bfloat16)
    returned = lax.all_to_all(
        expert_out.reshape(expert_count_axis, -1, model_width), "expert", 0, 0, tiled=True
    )
    expert_cot = lax.all_to_all(scaled_cot, "expert", 0, 0, tiled=True).reshape(1, -1, model_width)
    back_gate, back_up, back_down = (full_gate, full_up, full_down)
    d_hidden = jnp.einsum("erd,ehd->erh", expert_cot, back_down, preferred_element_type=jnp.float32)
    gate_sigmoid = jax.nn.sigmoid(pre_gate)
    d_pre_gate = (
        d_hidden * pre_up * gate_sigmoid * (1.0 + pre_gate * (1.0 - gate_sigmoid))
    ).astype(jnp.bfloat16)
    d_pre_up = (d_hidden * silu_gate).astype(jnp.bfloat16)
    d_rows = (
        jnp.einsum("erh,edh->erd", d_pre_gate, back_gate, preferred_element_type=jnp.float32)
        + jnp.einsum("erh,edh->erd", d_pre_up, back_up, preferred_element_type=jnp.float32)
    ).astype(jnp.bfloat16)
    row_grads = lax.all_to_all(
        d_rows.reshape(expert_count_axis, -1, model_width), "expert", 0, 0, tiled=True
    )
    position_hits = chosen[:, :, :, None] == jnp.arange(block_rows, dtype=jnp.int32)
    indicator_matrix = position_hits.reshape(num_blocks, expert_count * pick_count, block_rows)
    gate_weighted_rows = to_blocks(slot_gate_values, num_blocks, pick_count)[
        :, :, None
    ] * to_blocks(returned, num_blocks, pick_count).astype(jnp.float32)
    mixed = (
        jnp.einsum(
            "wze,wzi->wei",
            indicator_matrix.astype(jnp.float32),
            gate_weighted_rows,
            precision=lax.Precision.HIGHEST,
        )
        .reshape(tok_rows, model_width)
        .astype(jnp.bfloat16)
    )
    slot_dots = jnp.sum(cot_rows.astype(jnp.float32) * returned.astype(jnp.float32), axis=2)
    dgate = jnp.einsum(
        "bept,ebp->bte",
        position_hits.astype(jnp.float32),
        slot_dots.reshape(expert_count, num_blocks, pick_count),
        precision=lax.Precision.HIGHEST,
    ).reshape(tok_rows, expert_count)
    d_logit = (dgate * gate_values * (1.0 - gate_values)).astype(jnp.bfloat16)
    gathered_grads = jnp.einsum(
        "wze,wzi->wei",
        indicator_matrix.astype(jnp.bfloat16),
        to_blocks(row_grads, num_blocks, pick_count),
        preferred_element_type=jnp.float32,
    ).reshape(tok_rows, model_width)
    grad_tokens = (
        gathered_grads + jnp.dot(d_logit, w_router.T, preferred_element_type=jnp.float32)
    ).astype(jnp.bfloat16)
    router_full = jnp.dot(tokens.T, d_logit, preferred_element_type=jnp.float32)
    router_part = jnp.sum(
        lax.all_to_all(router_full.reshape(expert_count_axis, -1, 128), "expert", 0, 0, tiled=True),
        axis=0,
    )
    grad_gate, grad_up, down_weight_gradient, grad_router = weight_grads(
        expert_rows, hidden, expert_cot, d_pre_gate, d_pre_up, router_part, n
    )
    grad_router = lax.all_to_all(
        jnp.broadcast_to(grad_router[None], (expert_count_axis,) + grad_router.shape),
        "expert",
        0,
        0,
        tiled=True,
    ).reshape(router_full.shape)
    return (mixed, grad_tokens, grad_gate, grad_up, down_weight_gradient, grad_router)


def solution(mesh):
    placed = (
        P(("dp", "expert"), None),
        P(("dp", "expert"), None),
        P(("dp", "expert"), None, None),
        P(),
        P("expert", "dp", None),
        P("expert", "dp", None),
        P("expert", "dp", None),
    )
    return jax.shard_map(
        body,
        mesh=mesh,
        in_specs=placed,
        out_specs=(
            P(("dp", "expert"), None),
            P(("dp", "expert"), None),
            P("expert", "dp", None),
            P("expert", "dp", None),
            P("expert", "dp", None),
            P(),
        ),
        check_vma=False,
    )
```

```python
import functools

import jax
import jax.numpy as jnp
from jax import lax
from jax.experimental import pallas as pl
from jax.experimental.pallas import tpu as pltpu
from jax.sharding import PartitionSpec as P

MESH = pl.DeviceIdType.MESH


def _gather_kernel(n, *refs):
    count = (len(refs) - 3) // 2
    srcs, dsts = refs[:count], refs[count : 2 * count]
    send_sem, recv_sem, local_sem = refs[2 * count :]
    me = lax.axis_index("dp")
    ex = lax.axis_index("expert")
    barrier = pltpu.get_barrier_semaphore()
    for k in range(1, n):
        pl.semaphore_signal(barrier, inc=1, device_id=(lax.rem(me + k, n), ex), device_id_type=MESH)
    pl.semaphore_wait(barrier, n - 1)
    copies = []
    for a in range(count):
        rows = srcs[a].shape[0]
        slot = dsts[a].at[pl.ds(me * rows, rows)]
        local = pltpu.make_async_copy(srcs[a], slot, local_sem.at[a])
        local.start()
        copies.append(local)
        for k in range(1, n):
            remote = pltpu.make_async_remote_copy(
                src_ref=srcs[a],
                dst_ref=slot,
                send_sem=send_sem.at[a, k],
                recv_sem=recv_sem.at[a, k],
                device_id=(lax.rem(me + k, n), ex),
                device_id_type=MESH,
            )
            remote.start()
            copies.append(remote)
    for c in copies:
        c.wait()


def dp_all_gather(shards, n):
    count = len(shards)
    return pl.pallas_call(
        functools.partial(_gather_kernel, n),
        out_shape=[jax.ShapeDtypeStruct((n * s.shape[0],) + s.shape[1:], s.dtype) for s in shards],
        in_specs=[pl.BlockSpec(memory_space=pl.ANY)] * count,
        out_specs=[pl.BlockSpec(memory_space=pl.ANY)] * count,
        scratch_shapes=[
            pltpu.SemaphoreType.DMA((count, n)),
            pltpu.SemaphoreType.DMA((count, n)),
            pltpu.SemaphoreType.DMA((count,)),
        ],
        compiler_params=pltpu.CompilerParams(collective_id=0, has_side_effects=True),
    )(*shards)


def _exchange_kernel(n, n_scatter, *refs):
    count = (len(refs) - 3) // 2
    srcs, dsts = refs[:count], refs[count : 2 * count]
    send_sem, recv_sem, local_sem = refs[2 * count :]
    me = lax.axis_index("dp")
    ex = lax.axis_index("expert")
    barrier = pltpu.get_barrier_semaphore()
    for k in range(1, n):
        pl.semaphore_signal(barrier, inc=1, device_id=(lax.rem(me + k, n), ex), device_id_type=MESH)
    pl.semaphore_wait(barrier, n - 1)
    copies = []
    for a in range(count):
        rows = dsts[a].shape[1]
        if a < n_scatter:
            mine = srcs[a].at[pl.ds(me * rows, rows)]
        else:
            mine = srcs[a]
        local = pltpu.make_async_copy(mine, dsts[a].at[me], local_sem.at[a])
        local.start()
        copies.append(local)
        for k in range(1, n):
            peer = lax.rem(me + k, n)
            if a < n_scatter:
                part = srcs[a].at[pl.ds(peer * rows, rows)]
            else:
                part = srcs[a]
            remote = pltpu.make_async_remote_copy(
                src_ref=part,
                dst_ref=dsts[a].at[me],
                send_sem=send_sem.at[a, k],
                recv_sem=recv_sem.at[a, k],
                device_id=(peer, ex),
                device_id_type=MESH,
            )
            remote.start()
            copies.append(remote)
    for c in copies:
        c.wait()


def dp_exchange(partials, replicas, n):
    arrays = list(partials) + list(replicas)
    count = len(arrays)
    shapes = [(n, p.shape[0] // n) + p.shape[1:] for p in partials]
    shapes += [(n,) + r.shape for r in replicas]
    received = pl.pallas_call(
        functools.partial(_exchange_kernel, n, len(partials)),
        out_shape=[jax.ShapeDtypeStruct(s, a.dtype) for s, a in zip(shapes, arrays)],
        in_specs=[pl.BlockSpec(memory_space=pl.ANY)] * count,
        out_specs=[pl.BlockSpec(memory_space=pl.ANY)] * count,
        scratch_shapes=[
            pltpu.SemaphoreType.DMA((count, n)),
            pltpu.SemaphoreType.DMA((count, n)),
            pltpu.SemaphoreType.DMA((count,)),
        ],
        compiler_params=pltpu.CompilerParams(collective_id=1, has_side_effects=True),
    )(*arrays)
    return [jnp.sum(r.astype(jnp.float32), axis=0) for r in received]


def _shift_pairs(n, k):
    return [(i, (i + k) % n) for i in range(n)]


def dp_gather_permute(shard, n):
    me = lax.axis_index("dp")
    full = jnp.zeros((n,) + shard.shape, shard.dtype)
    full = lax.dynamic_update_index_in_dim(full, shard, me, 0)
    for k in range(1, n):
        got = lax.ppermute(shard, "dp", perm=_shift_pairs(n, k))
        full = lax.dynamic_update_index_in_dim(full, got, lax.rem(me + n - k, n), 0)
    return full


def dp_scatter_permute(partial, n):
    me = lax.axis_index("dp")
    blocks = partial.reshape((n, partial.shape[0] // n) + partial.shape[1:])
    total = lax.dynamic_index_in_dim(blocks, me, 0, keepdims=False).astype(jnp.float32)
    for k in range(1, n):
        piece = lax.dynamic_index_in_dim(blocks, lax.rem(me + k, n), 0, keepdims=False)
        got = lax.ppermute(piece, "dp", perm=_shift_pairs(n, k))
        total = total + got.astype(jnp.float32)
    return total


def to_blocks(slot_array, num_blocks, pick_count):
    expert_count = slot_array.shape[0]
    trailing = slot_array.shape[2:]
    grouped = slot_array.reshape((expert_count, num_blocks, pick_count) + trailing)
    axis_order = (1, 0, 2) + tuple(range(3, 3 + len(trailing)))
    return jnp.transpose(grouped, axis_order).reshape(
        (num_blocks, expert_count * pick_count) + trailing
    )


def weight_grads(expert_rows, hidden, expert_cot, d_pre_gate, d_pre_up, router_part, n):
    hidden_activations = hidden.shape[2]
    out_part = jnp.einsum(
        "erc,erd->cd", hidden, expert_cot, preferred_element_type=jnp.float32
    ).astype(jnp.bfloat16)
    out_share = dp_scatter_permute(out_part, n)
    both_grads = jnp.concatenate([d_pre_gate, d_pre_up], axis=2)
    in_part = jnp.einsum(
        "erc,erk->ck", expert_rows, both_grads, preferred_element_type=jnp.float32
    ).astype(jnp.bfloat16)
    in_share = dp_scatter_permute(in_part, n)
    grad_router = jnp.sum(
        lax.all_to_all(
            jnp.broadcast_to(router_part[None], (n,) + router_part.shape), "dp", 0, 0, tiled=True
        ),
        axis=0,
    )
    grad_gate = in_share[None, :, :hidden_activations]
    grad_up = in_share[None, :, hidden_activations:]
    down_weight_gradient = out_share[None]
    return (grad_gate, grad_up, down_weight_gradient, grad_router)


def body(tokens, cotangent, chosen, w_router, w_gate, w_up, w_down):
    tok_rows, model_width = tokens.shape
    num_blocks, expert_count, pick_count = chosen.shape
    block_rows = tok_rows // num_blocks
    slot_count = num_blocks * pick_count
    logits = jnp.dot(tokens, w_router, preferred_element_type=jnp.float32)
    gate_values = jax.nn.sigmoid(logits)
    offsets = (jnp.arange(num_blocks, dtype=jnp.int32) * block_rows)[:, None, None]
    slot_rows = jnp.transpose(chosen + offsets, (1, 0, 2)).reshape(expert_count, slot_count)
    picked = tokens[slot_rows]
    slot_gate_values = jnp.take_along_axis(gate_values.T, slot_rows, axis=1)
    cot_rows = cotangent[slot_rows]
    scaled_cot = (slot_gate_values[:, :, None] * cot_rows.astype(jnp.float32)).astype(jnp.bfloat16)
    n = lax.axis_size("dp")
    gate_up = dp_gather_permute(jnp.stack([w_gate[0], w_up[0]]), n)
    full_gate = gate_up[:, 0].reshape(1, -1, w_gate.shape[2])
    full_up = gate_up[:, 1].reshape(1, -1, w_up.shape[2])
    full_down = dp_gather_permute(w_down[0], n).reshape(1, -1, w_down.shape[2])
    expert_count_axis = lax.axis_size("expert")
    expert_rows = lax.all_to_all(picked, "expert", 0, 0, tiled=True).reshape(1, -1, model_width)
    pre_gate = jnp.einsum(
        "erd,edh->erh", expert_rows, full_gate, preferred_element_type=jnp.float32
    )
    pre_up = jnp.einsum("erd,edh->erh", expert_rows, full_up, preferred_element_type=jnp.float32)
    silu_gate = jax.nn.silu(pre_gate)
    hidden = (silu_gate * pre_up).astype(jnp.bfloat16)
    expert_out = jnp.einsum(
        "erh,ehd->erd", hidden, full_down, preferred_element_type=jnp.float32
    ).astype(jnp.bfloat16)
    returned = lax.all_to_all(
        expert_out.reshape(expert_count_axis, -1, model_width), "expert", 0, 0, tiled=True
    )
    expert_cot = lax.all_to_all(scaled_cot, "expert", 0, 0, tiled=True).reshape(1, -1, model_width)
    back_gate, back_up, back_down = (full_gate, full_up, full_down)
    d_hidden = jnp.einsum("erd,ehd->erh", expert_cot, back_down, preferred_element_type=jnp.float32)
    gate_sigmoid = jax.nn.sigmoid(pre_gate)
    d_pre_gate = (
        d_hidden * pre_up * gate_sigmoid * (1.0 + pre_gate * (1.0 - gate_sigmoid))
    ).astype(jnp.bfloat16)
    d_pre_up = (d_hidden * silu_gate).astype(jnp.bfloat16)
    d_rows = (
        jnp.einsum("erh,edh->erd", d_pre_gate, back_gate, preferred_element_type=jnp.float32)
        + jnp.einsum("erh,edh->erd", d_pre_up, back_up, preferred_element_type=jnp.float32)
    ).astype(jnp.bfloat16)
    row_grads = lax.all_to_all(
        d_rows.reshape(expert_count_axis, -1, model_width), "expert", 0, 0, tiled=True
    )
    position_hits = chosen[:, :, :, None] == jnp.arange(block_rows, dtype=jnp.int32)
    indicator_matrix = position_hits.reshape(num_blocks, expert_count * pick_count, block_rows)
    gate_weighted_rows = to_blocks(slot_gate_values, num_blocks, pick_count)[
        :, :, None
    ] * to_blocks(returned, num_blocks, pick_count).astype(jnp.float32)
    mixed = (
        jnp.einsum(
            "wze,wzi->wei",
            indicator_matrix.astype(jnp.float32),
            gate_weighted_rows,
            precision=lax.Precision.HIGHEST,
        )
        .reshape(tok_rows, model_width)
        .astype(jnp.bfloat16)
    )
    slot_dots = jnp.sum(cot_rows.astype(jnp.float32) * returned.astype(jnp.float32), axis=2)
    dgate = jnp.einsum(
        "bept,ebp->bte",
        position_hits.astype(jnp.float32),
        slot_dots.reshape(expert_count, num_blocks, pick_count),
        precision=lax.Precision.HIGHEST,
    ).reshape(tok_rows, expert_count)
    d_logit = (dgate * gate_values * (1.0 - gate_values)).astype(jnp.bfloat16)
    gathered_grads = jnp.einsum(
        "wze,wzi->wei",
        indicator_matrix.astype(jnp.bfloat16),
        to_blocks(row_grads, num_blocks, pick_count),
        preferred_element_type=jnp.float32,
    ).reshape(tok_rows, model_width)
    grad_tokens = (
        gathered_grads + jnp.dot(d_logit, w_router.T, preferred_element_type=jnp.float32)
    ).astype(jnp.bfloat16)
    router_full = jnp.dot(tokens.T, d_logit, preferred_element_type=jnp.float32)
    router_part = jnp.sum(
        lax.all_to_all(router_full.reshape(expert_count_axis, -1, 128), "expert", 0, 0, tiled=True),
        axis=0,
    )
    grad_gate, grad_up, down_weight_gradient, grad_router = weight_grads(
        expert_rows, hidden, expert_cot, d_pre_gate, d_pre_up, router_part, n
    )
    grad_router = lax.all_to_all(
        jnp.broadcast_to(grad_router[None], (expert_count_axis,) + grad_router.shape),
        "expert",
        0,
        0,
        tiled=True,
    ).reshape(router_full.shape)
    return (mixed, grad_tokens, grad_gate, grad_up, down_weight_gradient, grad_router)


def solution(mesh):
    placed = (
        P(("dp", "expert"), None),
        P(("dp", "expert"), None),
        P(("dp", "expert"), None, None),
        P(),
        P("expert", "dp", None),
        P("expert", "dp", None),
        P("expert", "dp", None),
    )
    return jax.shard_map(
        body,
        mesh=mesh,
        in_specs=placed,
        out_specs=(
            P(("dp", "expert"), None),
            P(("dp", "expert"), None),
            P("expert", "dp", None),
            P("expert", "dp", None),
            P("expert", "dp", None),
            P(),
        ),
        check_vma=False,
    )
```

```python
import functools

import jax
import jax.numpy as jnp
from jax import lax
from jax.experimental import pallas as pl
from jax.experimental.pallas import tpu as pltpu
from jax.sharding import PartitionSpec as P

MESH = pl.DeviceIdType.MESH


def _gather_kernel(n, *refs):
    count = (len(refs) - 3) // 2
    srcs, dsts = refs[:count], refs[count : 2 * count]
    send_sem, recv_sem, local_sem = refs[2 * count :]
    me = lax.axis_index("dp")
    ex = lax.axis_index("expert")
    barrier = pltpu.get_barrier_semaphore()
    for k in range(1, n):
        pl.semaphore_signal(barrier, inc=1, device_id=(lax.rem(me + k, n), ex), device_id_type=MESH)
    pl.semaphore_wait(barrier, n - 1)
    copies = []
    for a in range(count):
        rows = srcs[a].shape[0]
        slot = dsts[a].at[pl.ds(me * rows, rows)]
        local = pltpu.make_async_copy(srcs[a], slot, local_sem.at[a])
        local.start()
        copies.append(local)
        for k in range(1, n):
            remote = pltpu.make_async_remote_copy(
                src_ref=srcs[a],
                dst_ref=slot,
                send_sem=send_sem.at[a, k],
                recv_sem=recv_sem.at[a, k],
                device_id=(lax.rem(me + k, n), ex),
                device_id_type=MESH,
            )
            remote.start()
            copies.append(remote)
    for c in copies:
        c.wait()


def dp_all_gather(shards, n):
    count = len(shards)
    return pl.pallas_call(
        functools.partial(_gather_kernel, n),
        out_shape=[jax.ShapeDtypeStruct((n * s.shape[0],) + s.shape[1:], s.dtype) for s in shards],
        in_specs=[pl.BlockSpec(memory_space=pl.ANY)] * count,
        out_specs=[pl.BlockSpec(memory_space=pl.ANY)] * count,
        scratch_shapes=[
            pltpu.SemaphoreType.DMA((count, n)),
            pltpu.SemaphoreType.DMA((count, n)),
            pltpu.SemaphoreType.DMA((count,)),
        ],
        compiler_params=pltpu.CompilerParams(collective_id=0, has_side_effects=True),
    )(*shards)


def _exchange_kernel(n, n_scatter, *refs):
    count = (len(refs) - 3) // 2
    srcs, dsts = refs[:count], refs[count : 2 * count]
    send_sem, recv_sem, local_sem = refs[2 * count :]
    me = lax.axis_index("dp")
    ex = lax.axis_index("expert")
    barrier = pltpu.get_barrier_semaphore()
    for k in range(1, n):
        pl.semaphore_signal(barrier, inc=1, device_id=(lax.rem(me + k, n), ex), device_id_type=MESH)
    pl.semaphore_wait(barrier, n - 1)
    copies = []
    for a in range(count):
        rows = dsts[a].shape[1]
        if a < n_scatter:
            mine = srcs[a].at[pl.ds(me * rows, rows)]
        else:
            mine = srcs[a]
        local = pltpu.make_async_copy(mine, dsts[a].at[me], local_sem.at[a])
        local.start()
        copies.append(local)
        for k in range(1, n):
            peer = lax.rem(me + k, n)
            if a < n_scatter:
                part = srcs[a].at[pl.ds(peer * rows, rows)]
            else:
                part = srcs[a]
            remote = pltpu.make_async_remote_copy(
                src_ref=part,
                dst_ref=dsts[a].at[me],
                send_sem=send_sem.at[a, k],
                recv_sem=recv_sem.at[a, k],
                device_id=(peer, ex),
                device_id_type=MESH,
            )
            remote.start()
            copies.append(remote)
    for c in copies:
        c.wait()


def dp_exchange(partials, replicas, n):
    arrays = list(partials) + list(replicas)
    count = len(arrays)
    shapes = [(n, p.shape[0] // n) + p.shape[1:] for p in partials]
    shapes += [(n,) + r.shape for r in replicas]
    received = pl.pallas_call(
        functools.partial(_exchange_kernel, n, len(partials)),
        out_shape=[jax.ShapeDtypeStruct(s, a.dtype) for s, a in zip(shapes, arrays)],
        in_specs=[pl.BlockSpec(memory_space=pl.ANY)] * count,
        out_specs=[pl.BlockSpec(memory_space=pl.ANY)] * count,
        scratch_shapes=[
            pltpu.SemaphoreType.DMA((count, n)),
            pltpu.SemaphoreType.DMA((count, n)),
            pltpu.SemaphoreType.DMA((count,)),
        ],
        compiler_params=pltpu.CompilerParams(collective_id=1, has_side_effects=True),
    )(*arrays)
    return [jnp.sum(r.astype(jnp.float32), axis=0) for r in received]


def _shift_pairs(n, k):
    return [(i, (i + k) % n) for i in range(n)]


def dp_gather_permute(shard, n):
    me = lax.axis_index("dp")
    full = jnp.zeros((n,) + shard.shape, shard.dtype)
    full = lax.dynamic_update_index_in_dim(full, shard, me, 0)
    for k in range(1, n):
        got = lax.ppermute(shard, "dp", perm=_shift_pairs(n, k))
        full = lax.dynamic_update_index_in_dim(full, got, lax.rem(me + n - k, n), 0)
    return full


def dp_scatter_permute(partial, n):
    me = lax.axis_index("dp")
    blocks = partial.reshape((n, partial.shape[0] // n) + partial.shape[1:])
    total = lax.dynamic_index_in_dim(blocks, me, 0, keepdims=False).astype(jnp.float32)
    for k in range(1, n):
        piece = lax.dynamic_index_in_dim(blocks, lax.rem(me + k, n), 0, keepdims=False)
        got = lax.ppermute(piece, "dp", perm=_shift_pairs(n, k))
        total = total + got.astype(jnp.float32)
    return total


def _x_shift(n, d):
    return [(i, (i + 2 * d) % n) for i in range(n)]


def _y_pair(n):
    return [(i, i ^ 1) for i in range(n)]


def x_ring_gather(t, n):
    from_left = lax.ppermute(t, "dp", _x_shift(n, 1))
    from_right = lax.ppermute(t, "dp", _x_shift(n, -1))
    h = t.shape[0] // 2
    first = lax.ppermute(from_left[:h], "dp", _x_shift(n, 1))
    second = lax.ppermute(from_right[h:], "dp", _x_shift(n, -1))
    return [t, from_right, jnp.concatenate([first, second], axis=0), from_left]


def dp_gather_2d(t, n):
    assert n == 8
    me = lax.axis_index("dp")
    x, l, nx = me // 2, me % 2, n // 2
    partner = lax.ppermute(t, "dp", _y_pair(n))
    stacked = jnp.stack(x_ring_gather(t, n) + x_ring_gather(partner, n))
    p = jnp.arange(n, dtype=jnp.int32)
    order = (p // 2 - x) % nx + nx * (p % 2 != l).astype(jnp.int32)
    return jnp.take(stacked, order, axis=0)


def x_ring_scatter(blocks, n):
    h = blocks[0].shape[0] // 2
    low = lax.ppermute(blocks[2][:h].astype(jnp.bfloat16), "dp", _x_shift(n, 1))
    high = lax.ppermute(blocks[2][h:].astype(jnp.bfloat16), "dp", _x_shift(n, -1))
    to_right = jnp.concatenate([blocks[1][:h] + low.astype(jnp.float32), blocks[1][h:]], axis=0)
    to_left = jnp.concatenate([blocks[3][:h], blocks[3][h:] + high.astype(jnp.float32)], axis=0)
    from_left = lax.ppermute(to_right.astype(jnp.bfloat16), "dp", _x_shift(n, 1))
    from_right = lax.ppermute(to_left.astype(jnp.bfloat16), "dp", _x_shift(n, -1))
    return blocks[0] + from_left.astype(jnp.float32) + from_right.astype(jnp.float32)


def dp_scatter_2d(partial, n):
    assert n == 8
    me = lax.axis_index("dp")
    x, l, nx = me // 2, me % 2, n // 2
    blocks = partial.reshape((n, partial.shape[0] // n) + partial.shape[1:])

    def pick(m, side):
        index = 2 * ((x + m) % nx) + side
        return lax.dynamic_index_in_dim(blocks, index, 0, keepdims=False).astype(jnp.float32)

    partner_sum = x_ring_scatter([pick(m, 1 - l) for m in range(nx)], n)
    sent = lax.ppermute(partner_sum.astype(jnp.bfloat16), "dp", _y_pair(n))
    own_sum = x_ring_scatter([pick(m, l) for m in range(nx)], n)
    return own_sum + sent.astype(jnp.float32)


def to_blocks(slot_array, num_blocks, pick_count):
    expert_count = slot_array.shape[0]
    trailing = slot_array.shape[2:]
    grouped = slot_array.reshape((expert_count, num_blocks, pick_count) + trailing)
    axis_order = (1, 0, 2) + tuple(range(3, 3 + len(trailing)))
    return jnp.transpose(grouped, axis_order).reshape(
        (num_blocks, expert_count * pick_count) + trailing
    )


def weight_grads(expert_rows, hidden, expert_cot, d_pre_gate, d_pre_up, router_part, n):
    hidden_activations = hidden.shape[2]
    out_part = jnp.einsum(
        "erc,erd->cd", hidden, expert_cot, preferred_element_type=jnp.float32
    ).astype(jnp.bfloat16)
    out_share = dp_scatter_2d(out_part, n)
    both_grads = jnp.concatenate([d_pre_gate, d_pre_up], axis=2)
    in_part = jnp.einsum(
        "erc,erk->ck", expert_rows, both_grads, preferred_element_type=jnp.float32
    ).astype(jnp.bfloat16)
    in_share = dp_scatter_2d(in_part, n)
    grad_router = jnp.sum(
        lax.all_to_all(
            jnp.broadcast_to(router_part[None], (n,) + router_part.shape), "dp", 0, 0, tiled=True
        ),
        axis=0,
    )
    grad_gate = in_share[None, :, :hidden_activations]
    grad_up = in_share[None, :, hidden_activations:]
    down_weight_gradient = out_share[None]
    return (grad_gate, grad_up, down_weight_gradient, grad_router)


def body(tokens, cotangent, chosen, w_router, w_gate, w_up, w_down):
    tok_rows, model_width = tokens.shape
    num_blocks, expert_count, pick_count = chosen.shape
    block_rows = tok_rows // num_blocks
    slot_count = num_blocks * pick_count
    logits = jnp.dot(tokens, w_router, preferred_element_type=jnp.float32)
    gate_values = jax.nn.sigmoid(logits)
    offsets = (jnp.arange(num_blocks, dtype=jnp.int32) * block_rows)[:, None, None]
    slot_rows = jnp.transpose(chosen + offsets, (1, 0, 2)).reshape(expert_count, slot_count)
    picked = tokens[slot_rows]
    slot_gate_values = jnp.take_along_axis(gate_values.T, slot_rows, axis=1)
    cot_rows = cotangent[slot_rows]
    scaled_cot = (slot_gate_values[:, :, None] * cot_rows.astype(jnp.float32)).astype(jnp.bfloat16)
    n = lax.axis_size("dp")
    gate_up = dp_gather_2d(jnp.stack([w_gate[0], w_up[0]]), n)
    full_gate = gate_up[:, 0].reshape(1, -1, w_gate.shape[2])
    full_up = gate_up[:, 1].reshape(1, -1, w_up.shape[2])
    full_down = dp_gather_2d(w_down[0], n).reshape(1, -1, w_down.shape[2])
    expert_count_axis = lax.axis_size("expert")
    expert_rows = lax.all_to_all(picked, "expert", 0, 0, tiled=True).reshape(1, -1, model_width)
    pre_gate = jnp.einsum(
        "erd,edh->erh", expert_rows, full_gate, preferred_element_type=jnp.float32
    )
    pre_up = jnp.einsum("erd,edh->erh", expert_rows, full_up, preferred_element_type=jnp.float32)
    silu_gate = jax.nn.silu(pre_gate)
    hidden = (silu_gate * pre_up).astype(jnp.bfloat16)
    expert_out = jnp.einsum(
        "erh,ehd->erd", hidden, full_down, preferred_element_type=jnp.float32
    ).astype(jnp.bfloat16)
    returned = lax.all_to_all(
        expert_out.reshape(expert_count_axis, -1, model_width), "expert", 0, 0, tiled=True
    )
    expert_cot = lax.all_to_all(scaled_cot, "expert", 0, 0, tiled=True).reshape(1, -1, model_width)
    back_gate, back_up, back_down = (full_gate, full_up, full_down)
    d_hidden = jnp.einsum("erd,ehd->erh", expert_cot, back_down, preferred_element_type=jnp.float32)
    gate_sigmoid = jax.nn.sigmoid(pre_gate)
    d_pre_gate = (
        d_hidden * pre_up * gate_sigmoid * (1.0 + pre_gate * (1.0 - gate_sigmoid))
    ).astype(jnp.bfloat16)
    d_pre_up = (d_hidden * silu_gate).astype(jnp.bfloat16)
    d_rows = (
        jnp.einsum("erh,edh->erd", d_pre_gate, back_gate, preferred_element_type=jnp.float32)
        + jnp.einsum("erh,edh->erd", d_pre_up, back_up, preferred_element_type=jnp.float32)
    ).astype(jnp.bfloat16)
    row_grads = lax.all_to_all(
        d_rows.reshape(expert_count_axis, -1, model_width), "expert", 0, 0, tiled=True
    )
    position_hits = chosen[:, :, :, None] == jnp.arange(block_rows, dtype=jnp.int32)
    indicator_matrix = position_hits.reshape(num_blocks, expert_count * pick_count, block_rows)
    gate_weighted_rows = to_blocks(slot_gate_values, num_blocks, pick_count)[
        :, :, None
    ] * to_blocks(returned, num_blocks, pick_count).astype(jnp.float32)
    mixed = (
        jnp.einsum(
            "wze,wzi->wei",
            indicator_matrix.astype(jnp.float32),
            gate_weighted_rows,
            precision=lax.Precision.HIGHEST,
        )
        .reshape(tok_rows, model_width)
        .astype(jnp.bfloat16)
    )
    slot_dots = jnp.sum(cot_rows.astype(jnp.float32) * returned.astype(jnp.float32), axis=2)
    dgate = jnp.einsum(
        "bept,ebp->bte",
        position_hits.astype(jnp.float32),
        slot_dots.reshape(expert_count, num_blocks, pick_count),
        precision=lax.Precision.HIGHEST,
    ).reshape(tok_rows, expert_count)
    d_logit = (dgate * gate_values * (1.0 - gate_values)).astype(jnp.bfloat16)
    gathered_grads = jnp.einsum(
        "wze,wzi->wei",
        indicator_matrix.astype(jnp.bfloat16),
        to_blocks(row_grads, num_blocks, pick_count),
        preferred_element_type=jnp.float32,
    ).reshape(tok_rows, model_width)
    grad_tokens = (
        gathered_grads + jnp.dot(d_logit, w_router.T, preferred_element_type=jnp.float32)
    ).astype(jnp.bfloat16)
    router_full = jnp.dot(tokens.T, d_logit, preferred_element_type=jnp.float32)
    router_part = jnp.sum(
        lax.all_to_all(router_full.reshape(expert_count_axis, -1, 128), "expert", 0, 0, tiled=True),
        axis=0,
    )
    grad_gate, grad_up, down_weight_gradient, grad_router = weight_grads(
        expert_rows, hidden, expert_cot, d_pre_gate, d_pre_up, router_part, n
    )
    grad_router = lax.all_to_all(
        jnp.broadcast_to(grad_router[None], (expert_count_axis,) + grad_router.shape),
        "expert",
        0,
        0,
        tiled=True,
    ).reshape(router_full.shape)
    return (mixed, grad_tokens, grad_gate, grad_up, down_weight_gradient, grad_router)


def solution(mesh):
    placed = (
        P(("dp", "expert"), None),
        P(("dp", "expert"), None),
        P(("dp", "expert"), None, None),
        P(),
        P("expert", "dp", None),
        P("expert", "dp", None),
        P("expert", "dp", None),
    )
    return jax.shard_map(
        body,
        mesh=mesh,
        in_specs=placed,
        out_specs=(
            P(("dp", "expert"), None),
            P(("dp", "expert"), None),
            P("expert", "dp", None),
            P("expert", "dp", None),
            P("expert", "dp", None),
            P(),
        ),
        check_vma=False,
    )
```

```python
import functools

import jax
import jax.numpy as jnp
from jax import lax
from jax.experimental import pallas as pl
from jax.experimental.pallas import tpu as pltpu
from jax.sharding import PartitionSpec as P

MESH = pl.DeviceIdType.MESH


def _gather_kernel(n, *refs):
    count = (len(refs) - 3) // 2
    srcs, dsts = refs[:count], refs[count : 2 * count]
    send_sem, recv_sem, local_sem = refs[2 * count :]
    me = lax.axis_index("dp")
    ex = lax.axis_index("expert")
    barrier = pltpu.get_barrier_semaphore()
    for k in range(1, n):
        pl.semaphore_signal(barrier, inc=1, device_id=(lax.rem(me + k, n), ex), device_id_type=MESH)
    pl.semaphore_wait(barrier, n - 1)
    copies = []
    for a in range(count):
        rows = srcs[a].shape[0]
        slot = dsts[a].at[pl.ds(me * rows, rows)]
        local = pltpu.make_async_copy(srcs[a], slot, local_sem.at[a])
        local.start()
        copies.append(local)
        for k in range(1, n):
            remote = pltpu.make_async_remote_copy(
                src_ref=srcs[a],
                dst_ref=slot,
                send_sem=send_sem.at[a, k],
                recv_sem=recv_sem.at[a, k],
                device_id=(lax.rem(me + k, n), ex),
                device_id_type=MESH,
            )
            remote.start()
            copies.append(remote)
    for c in copies:
        c.wait()


def dp_all_gather(shards, n):
    count = len(shards)
    return pl.pallas_call(
        functools.partial(_gather_kernel, n),
        out_shape=[jax.ShapeDtypeStruct((n * s.shape[0],) + s.shape[1:], s.dtype) for s in shards],
        in_specs=[pl.BlockSpec(memory_space=pl.ANY)] * count,
        out_specs=[pl.BlockSpec(memory_space=pl.ANY)] * count,
        scratch_shapes=[
            pltpu.SemaphoreType.DMA((count, n)),
            pltpu.SemaphoreType.DMA((count, n)),
            pltpu.SemaphoreType.DMA((count,)),
        ],
        compiler_params=pltpu.CompilerParams(collective_id=0, has_side_effects=True),
    )(*shards)


def _exchange_kernel(n, n_scatter, *refs):
    count = (len(refs) - 3) // 2
    srcs, dsts = refs[:count], refs[count : 2 * count]
    send_sem, recv_sem, local_sem = refs[2 * count :]
    me = lax.axis_index("dp")
    ex = lax.axis_index("expert")
    barrier = pltpu.get_barrier_semaphore()
    for k in range(1, n):
        pl.semaphore_signal(barrier, inc=1, device_id=(lax.rem(me + k, n), ex), device_id_type=MESH)
    pl.semaphore_wait(barrier, n - 1)
    copies = []
    for a in range(count):
        rows = dsts[a].shape[1]
        if a < n_scatter:
            mine = srcs[a].at[pl.ds(me * rows, rows)]
        else:
            mine = srcs[a]
        local = pltpu.make_async_copy(mine, dsts[a].at[me], local_sem.at[a])
        local.start()
        copies.append(local)
        for k in range(1, n):
            peer = lax.rem(me + k, n)
            if a < n_scatter:
                part = srcs[a].at[pl.ds(peer * rows, rows)]
            else:
                part = srcs[a]
            remote = pltpu.make_async_remote_copy(
                src_ref=part,
                dst_ref=dsts[a].at[me],
                send_sem=send_sem.at[a, k],
                recv_sem=recv_sem.at[a, k],
                device_id=(peer, ex),
                device_id_type=MESH,
            )
            remote.start()
            copies.append(remote)
    for c in copies:
        c.wait()


def dp_exchange(partials, replicas, n):
    arrays = list(partials) + list(replicas)
    count = len(arrays)
    shapes = [(n, p.shape[0] // n) + p.shape[1:] for p in partials]
    shapes += [(n,) + r.shape for r in replicas]
    received = pl.pallas_call(
        functools.partial(_exchange_kernel, n, len(partials)),
        out_shape=[jax.ShapeDtypeStruct(s, a.dtype) for s, a in zip(shapes, arrays)],
        in_specs=[pl.BlockSpec(memory_space=pl.ANY)] * count,
        out_specs=[pl.BlockSpec(memory_space=pl.ANY)] * count,
        scratch_shapes=[
            pltpu.SemaphoreType.DMA((count, n)),
            pltpu.SemaphoreType.DMA((count, n)),
            pltpu.SemaphoreType.DMA((count,)),
        ],
        compiler_params=pltpu.CompilerParams(collective_id=1, has_side_effects=True),
    )(*arrays)
    return [jnp.sum(r.astype(jnp.float32), axis=0) for r in received]


def _shift_pairs(n, k):
    return [(i, (i + k) % n) for i in range(n)]


def dp_gather_permute(shard, n):
    me = lax.axis_index("dp")
    full = jnp.zeros((n,) + shard.shape, shard.dtype)
    full = lax.dynamic_update_index_in_dim(full, shard, me, 0)
    for k in range(1, n):
        got = lax.ppermute(shard, "dp", perm=_shift_pairs(n, k))
        full = lax.dynamic_update_index_in_dim(full, got, lax.rem(me + n - k, n), 0)
    return full


def dp_scatter_permute(partial, n):
    me = lax.axis_index("dp")
    blocks = partial.reshape((n, partial.shape[0] // n) + partial.shape[1:])
    total = lax.dynamic_index_in_dim(blocks, me, 0, keepdims=False).astype(jnp.float32)
    for k in range(1, n):
        piece = lax.dynamic_index_in_dim(blocks, lax.rem(me + k, n), 0, keepdims=False)
        got = lax.ppermute(piece, "dp", perm=_shift_pairs(n, k))
        total = total + got.astype(jnp.float32)
    return total


def _x_shift(n, d):
    return [(i, (i + 2 * d) % n) for i in range(n)]


def _y_pair(n):
    return [(i, i ^ 1) for i in range(n)]


def x_ring_gather(t, n):
    from_left = lax.ppermute(t, "dp", _x_shift(n, 1))
    from_right = lax.ppermute(t, "dp", _x_shift(n, -1))
    h = t.shape[0] // 2
    first = lax.ppermute(from_left[:h], "dp", _x_shift(n, 1))
    second = lax.ppermute(from_right[h:], "dp", _x_shift(n, -1))
    return [t, from_right, jnp.concatenate([first, second], axis=0), from_left]


def dp_gather_2d(t, n):
    assert n == 8
    me = lax.axis_index("dp")
    nx = n // 2
    partner = lax.ppermute(t, "dp", _y_pair(n))
    pieces = x_ring_gather(t, n) + x_ring_gather(partner, n)

    def placed(c):
        order = [(p // 2 - c // 2) % nx + nx * int(p % 2 != c % 2) for p in range(n)]
        return lambda parts: jnp.stack([parts[k] for k in order])

    return lax.switch(me, [placed(c) for c in range(n)], pieces)


def x_ring_scatter(blocks, n):
    h = blocks[0].shape[0] // 2
    low = lax.ppermute(blocks[2][:h].astype(jnp.bfloat16), "dp", _x_shift(n, 1))
    high = lax.ppermute(blocks[2][h:].astype(jnp.bfloat16), "dp", _x_shift(n, -1))
    to_right = jnp.concatenate([blocks[1][:h] + low.astype(jnp.float32), blocks[1][h:]], axis=0)
    to_left = jnp.concatenate([blocks[3][:h], blocks[3][h:] + high.astype(jnp.float32)], axis=0)
    from_left = lax.ppermute(to_right.astype(jnp.bfloat16), "dp", _x_shift(n, 1))
    from_right = lax.ppermute(to_left.astype(jnp.bfloat16), "dp", _x_shift(n, -1))
    return blocks[0] + from_left.astype(jnp.float32) + from_right.astype(jnp.float32)


def dp_scatter_2d(partial, n):
    assert n == 8
    me = lax.axis_index("dp")
    x, l, nx = me // 2, me % 2, n // 2
    blocks = partial.reshape((n, partial.shape[0] // n) + partial.shape[1:])

    def pick(m, side):
        index = 2 * ((x + m) % nx) + side
        return lax.dynamic_index_in_dim(blocks, index, 0, keepdims=False).astype(jnp.float32)

    partner_sum = x_ring_scatter([pick(m, 1 - l) for m in range(nx)], n)
    sent = lax.ppermute(partner_sum.astype(jnp.bfloat16), "dp", _y_pair(n))
    own_sum = x_ring_scatter([pick(m, l) for m in range(nx)], n)
    return own_sum + sent.astype(jnp.float32)


def to_blocks(slot_array, num_blocks, pick_count):
    expert_count = slot_array.shape[0]
    trailing = slot_array.shape[2:]
    grouped = slot_array.reshape((expert_count, num_blocks, pick_count) + trailing)
    axis_order = (1, 0, 2) + tuple(range(3, 3 + len(trailing)))
    return jnp.transpose(grouped, axis_order).reshape(
        (num_blocks, expert_count * pick_count) + trailing
    )


def weight_grads(expert_rows, hidden, expert_cot, d_pre_gate, d_pre_up, router_part, n):
    hidden_activations = hidden.shape[2]
    out_part = jnp.einsum(
        "erc,erd->cd", hidden, expert_cot, preferred_element_type=jnp.float32
    ).astype(jnp.bfloat16)
    router_part, out_part = lax.optimization_barrier((router_part, out_part))
    out_share = dp_scatter_2d(out_part, n)
    grad_router = jnp.sum(
        lax.all_to_all(
            jnp.broadcast_to(router_part[None], (n,) + router_part.shape), "dp", 0, 0, tiled=True
        ),
        axis=0,
    )
    both_grads = jnp.concatenate([d_pre_gate, d_pre_up], axis=2)
    in_part = jnp.einsum(
        "erc,erk->ck", expert_rows, both_grads, preferred_element_type=jnp.float32
    ).astype(jnp.bfloat16)
    grad_router, in_part = lax.optimization_barrier((grad_router, in_part))
    in_share = dp_scatter_2d(in_part, n)
    grad_gate = in_share[None, :, :hidden_activations]
    grad_up = in_share[None, :, hidden_activations:]
    down_weight_gradient = out_share[None]
    return (grad_gate, grad_up, down_weight_gradient, grad_router)


def body(tokens, cotangent, chosen, w_router, w_gate, w_up, w_down):
    tok_rows, model_width = tokens.shape
    num_blocks, expert_count, pick_count = chosen.shape
    block_rows = tok_rows // num_blocks
    slot_count = num_blocks * pick_count
    logits = jnp.dot(tokens, w_router, preferred_element_type=jnp.float32)
    gate_values = jax.nn.sigmoid(logits)
    offsets = (jnp.arange(num_blocks, dtype=jnp.int32) * block_rows)[:, None, None]
    slot_rows = jnp.transpose(chosen + offsets, (1, 0, 2)).reshape(expert_count, slot_count)
    picked = tokens[slot_rows]
    slot_gate_values = jnp.take_along_axis(gate_values.T, slot_rows, axis=1)
    cot_rows = cotangent[slot_rows]
    scaled_cot = (slot_gate_values[:, :, None] * cot_rows.astype(jnp.float32)).astype(jnp.bfloat16)
    n = lax.axis_size("dp")
    gate_up = dp_gather_2d(jnp.stack([w_gate[0], w_up[0]]), n)
    full_gate = gate_up[:, 0].reshape(1, -1, w_gate.shape[2])
    full_up = gate_up[:, 1].reshape(1, -1, w_up.shape[2])
    full_down = dp_gather_2d(w_down[0], n).reshape(1, -1, w_down.shape[2])
    expert_count_axis = lax.axis_size("expert")
    expert_rows = lax.all_to_all(picked, "expert", 0, 0, tiled=True).reshape(1, -1, model_width)
    pre_gate = jnp.einsum(
        "erd,edh->erh", expert_rows, full_gate, preferred_element_type=jnp.float32
    )
    pre_up = jnp.einsum("erd,edh->erh", expert_rows, full_up, preferred_element_type=jnp.float32)
    silu_gate = jax.nn.silu(pre_gate)
    hidden = (silu_gate * pre_up).astype(jnp.bfloat16)
    expert_out = jnp.einsum(
        "erh,ehd->erd", hidden, full_down, preferred_element_type=jnp.float32
    ).astype(jnp.bfloat16)
    returned = lax.all_to_all(
        expert_out.reshape(expert_count_axis, -1, model_width), "expert", 0, 0, tiled=True
    )
    expert_cot = lax.all_to_all(scaled_cot, "expert", 0, 0, tiled=True).reshape(1, -1, model_width)
    back_gate, back_up, back_down = (full_gate, full_up, full_down)
    d_hidden = jnp.einsum("erd,ehd->erh", expert_cot, back_down, preferred_element_type=jnp.float32)
    gate_sigmoid = jax.nn.sigmoid(pre_gate)
    d_pre_gate = (
        d_hidden * pre_up * gate_sigmoid * (1.0 + pre_gate * (1.0 - gate_sigmoid))
    ).astype(jnp.bfloat16)
    d_pre_up = (d_hidden * silu_gate).astype(jnp.bfloat16)
    d_rows = (
        jnp.einsum("erh,edh->erd", d_pre_gate, back_gate, preferred_element_type=jnp.float32)
        + jnp.einsum("erh,edh->erd", d_pre_up, back_up, preferred_element_type=jnp.float32)
    ).astype(jnp.bfloat16)
    row_grads = lax.all_to_all(
        d_rows.reshape(expert_count_axis, -1, model_width), "expert", 0, 0, tiled=True
    )
    position_hits = chosen[:, :, :, None] == jnp.arange(block_rows, dtype=jnp.int32)
    indicator_matrix = position_hits.reshape(num_blocks, expert_count * pick_count, block_rows)
    gate_weighted_rows = to_blocks(slot_gate_values, num_blocks, pick_count)[
        :, :, None
    ] * to_blocks(returned, num_blocks, pick_count).astype(jnp.float32)
    mixed = (
        jnp.einsum(
            "wze,wzi->wei",
            indicator_matrix.astype(jnp.float32),
            gate_weighted_rows,
            precision=lax.Precision.HIGHEST,
        )
        .reshape(tok_rows, model_width)
        .astype(jnp.bfloat16)
    )
    slot_dots = jnp.sum(cot_rows.astype(jnp.float32) * returned.astype(jnp.float32), axis=2)
    dgate = jnp.einsum(
        "bept,ebp->bte",
        position_hits.astype(jnp.float32),
        slot_dots.reshape(expert_count, num_blocks, pick_count),
        precision=lax.Precision.HIGHEST,
    ).reshape(tok_rows, expert_count)
    d_logit = (dgate * gate_values * (1.0 - gate_values)).astype(jnp.bfloat16)
    gathered_grads = jnp.einsum(
        "wze,wzi->wei",
        indicator_matrix.astype(jnp.bfloat16),
        to_blocks(row_grads, num_blocks, pick_count),
        preferred_element_type=jnp.float32,
    ).reshape(tok_rows, model_width)
    grad_tokens = (
        gathered_grads + jnp.dot(d_logit, w_router.T, preferred_element_type=jnp.float32)
    ).astype(jnp.bfloat16)
    router_full = jnp.dot(tokens.T, d_logit, preferred_element_type=jnp.float32)
    router_part = jnp.sum(
        lax.all_to_all(router_full.reshape(expert_count_axis, -1, 128), "expert", 0, 0, tiled=True),
        axis=0,
    )
    grad_gate, grad_up, down_weight_gradient, grad_router = weight_grads(
        expert_rows, hidden, expert_cot, d_pre_gate, d_pre_up, router_part, n
    )
    grad_router = lax.all_to_all(
        jnp.broadcast_to(grad_router[None], (expert_count_axis,) + grad_router.shape),
        "expert",
        0,
        0,
        tiled=True,
    ).reshape(router_full.shape)
    return (mixed, grad_tokens, grad_gate, grad_up, down_weight_gradient, grad_router)


def solution(mesh):
    placed = (
        P(("dp", "expert"), None),
        P(("dp", "expert"), None),
        P(("dp", "expert"), None, None),
        P(),
        P("expert", "dp", None),
        P("expert", "dp", None),
        P("expert", "dp", None),
    )
    return jax.shard_map(
        body,
        mesh=mesh,
        in_specs=placed,
        out_specs=(
            P(("dp", "expert"), None),
            P(("dp", "expert"), None),
            P("expert", "dp", None),
            P("expert", "dp", None),
            P("expert", "dp", None),
            P(),
        ),
        check_vma=False,
    )
```

```python
import functools

import jax
import jax.numpy as jnp
from jax import lax
from jax.experimental import pallas as pl
from jax.experimental.pallas import tpu as pltpu
from jax.sharding import PartitionSpec as P

MESH = pl.DeviceIdType.MESH


def _gather_kernel(n, *refs):
    count = (len(refs) - 3) // 2
    srcs, dsts = refs[:count], refs[count : 2 * count]
    send_sem, recv_sem, local_sem = refs[2 * count :]
    me = lax.axis_index("dp")
    ex = lax.axis_index("expert")
    barrier = pltpu.get_barrier_semaphore()
    for k in range(1, n):
        pl.semaphore_signal(barrier, inc=1, device_id=(lax.rem(me + k, n), ex), device_id_type=MESH)
    pl.semaphore_wait(barrier, n - 1)
    copies = []
    for a in range(count):
        rows = srcs[a].shape[0]
        slot = dsts[a].at[pl.ds(me * rows, rows)]
        local = pltpu.make_async_copy(srcs[a], slot, local_sem.at[a])
        local.start()
        copies.append(local)
        for k in range(1, n):
            remote = pltpu.make_async_remote_copy(
                src_ref=srcs[a],
                dst_ref=slot,
                send_sem=send_sem.at[a, k],
                recv_sem=recv_sem.at[a, k],
                device_id=(lax.rem(me + k, n), ex),
                device_id_type=MESH,
            )
            remote.start()
            copies.append(remote)
    for c in copies:
        c.wait()


def dp_all_gather(shards, n):
    count = len(shards)
    return pl.pallas_call(
        functools.partial(_gather_kernel, n),
        out_shape=[jax.ShapeDtypeStruct((n * s.shape[0],) + s.shape[1:], s.dtype) for s in shards],
        in_specs=[pl.BlockSpec(memory_space=pl.ANY)] * count,
        out_specs=[pl.BlockSpec(memory_space=pl.ANY)] * count,
        scratch_shapes=[
            pltpu.SemaphoreType.DMA((count, n)),
            pltpu.SemaphoreType.DMA((count, n)),
            pltpu.SemaphoreType.DMA((count,)),
        ],
        compiler_params=pltpu.CompilerParams(collective_id=0, has_side_effects=True),
    )(*shards)


def _exchange_kernel(n, n_scatter, *refs):
    count = (len(refs) - 3) // 2
    srcs, dsts = refs[:count], refs[count : 2 * count]
    send_sem, recv_sem, local_sem = refs[2 * count :]
    me = lax.axis_index("dp")
    ex = lax.axis_index("expert")
    barrier = pltpu.get_barrier_semaphore()
    for k in range(1, n):
        pl.semaphore_signal(barrier, inc=1, device_id=(lax.rem(me + k, n), ex), device_id_type=MESH)
    pl.semaphore_wait(barrier, n - 1)
    copies = []
    for a in range(count):
        rows = dsts[a].shape[1]
        if a < n_scatter:
            mine = srcs[a].at[pl.ds(me * rows, rows)]
        else:
            mine = srcs[a]
        local = pltpu.make_async_copy(mine, dsts[a].at[me], local_sem.at[a])
        local.start()
        copies.append(local)
        for k in range(1, n):
            peer = lax.rem(me + k, n)
            if a < n_scatter:
                part = srcs[a].at[pl.ds(peer * rows, rows)]
            else:
                part = srcs[a]
            remote = pltpu.make_async_remote_copy(
                src_ref=part,
                dst_ref=dsts[a].at[me],
                send_sem=send_sem.at[a, k],
                recv_sem=recv_sem.at[a, k],
                device_id=(peer, ex),
                device_id_type=MESH,
            )
            remote.start()
            copies.append(remote)
    for c in copies:
        c.wait()


def dp_exchange(partials, replicas, n):
    arrays = list(partials) + list(replicas)
    count = len(arrays)
    shapes = [(n, p.shape[0] // n) + p.shape[1:] for p in partials]
    shapes += [(n,) + r.shape for r in replicas]
    received = pl.pallas_call(
        functools.partial(_exchange_kernel, n, len(partials)),
        out_shape=[jax.ShapeDtypeStruct(s, a.dtype) for s, a in zip(shapes, arrays)],
        in_specs=[pl.BlockSpec(memory_space=pl.ANY)] * count,
        out_specs=[pl.BlockSpec(memory_space=pl.ANY)] * count,
        scratch_shapes=[
            pltpu.SemaphoreType.DMA((count, n)),
            pltpu.SemaphoreType.DMA((count, n)),
            pltpu.SemaphoreType.DMA((count,)),
        ],
        compiler_params=pltpu.CompilerParams(collective_id=1, has_side_effects=True),
    )(*arrays)
    return [jnp.sum(r.astype(jnp.float32), axis=0) for r in received]


def _shift_pairs(n, k):
    return [(i, (i + k) % n) for i in range(n)]


def dp_gather_permute(shard, n):
    me = lax.axis_index("dp")
    full = jnp.zeros((n,) + shard.shape, shard.dtype)
    full = lax.dynamic_update_index_in_dim(full, shard, me, 0)
    for k in range(1, n):
        got = lax.ppermute(shard, "dp", perm=_shift_pairs(n, k))
        full = lax.dynamic_update_index_in_dim(full, got, lax.rem(me + n - k, n), 0)
    return full


def dp_scatter_permute(partial, n):
    me = lax.axis_index("dp")
    blocks = partial.reshape((n, partial.shape[0] // n) + partial.shape[1:])
    total = lax.dynamic_index_in_dim(blocks, me, 0, keepdims=False).astype(jnp.float32)
    for k in range(1, n):
        piece = lax.dynamic_index_in_dim(blocks, lax.rem(me + k, n), 0, keepdims=False)
        got = lax.ppermute(piece, "dp", perm=_shift_pairs(n, k))
        total = total + got.astype(jnp.float32)
    return total


def _x_shift(n, d):
    return [(i, (i + 2 * d) % n) for i in range(n)]


def _y_pair(n):
    return [(i, i ^ 1) for i in range(n)]


def x_ring_gather(t, n):
    from_left = lax.ppermute(t, "dp", _x_shift(n, 1))
    from_right = lax.ppermute(t, "dp", _x_shift(n, -1))
    h = t.shape[0] // 2
    first = lax.ppermute(from_left[:h], "dp", _x_shift(n, 1))
    second = lax.ppermute(from_right[h:], "dp", _x_shift(n, -1))
    return [t, from_right, jnp.concatenate([first, second], axis=0), from_left]


def dp_gather_2d(t, n):
    assert n == 8
    me = lax.axis_index("dp")
    x, l, nx = me // 2, me % 2, n // 2
    partner = lax.ppermute(t, "dp", _y_pair(n))
    stacked = jnp.stack(x_ring_gather(t, n) + x_ring_gather(partner, n))
    p = jnp.arange(n, dtype=jnp.int32)
    order = (p // 2 - x) % nx + nx * (p % 2 != l).astype(jnp.int32)
    return jnp.take(stacked, order, axis=0)


def x_ring_scatter(blocks, n):
    h = blocks[0].shape[0] // 2
    low = lax.ppermute(blocks[2][:h].astype(jnp.bfloat16), "dp", _x_shift(n, 1))
    high = lax.ppermute(blocks[2][h:].astype(jnp.bfloat16), "dp", _x_shift(n, -1))
    to_right = jnp.concatenate([blocks[1][:h] + low.astype(jnp.float32), blocks[1][h:]], axis=0)
    to_left = jnp.concatenate([blocks[3][:h], blocks[3][h:] + high.astype(jnp.float32)], axis=0)
    from_left = lax.ppermute(to_right.astype(jnp.bfloat16), "dp", _x_shift(n, 1))
    from_right = lax.ppermute(to_left.astype(jnp.bfloat16), "dp", _x_shift(n, -1))
    return blocks[0] + from_left.astype(jnp.float32) + from_right.astype(jnp.float32)


def dp_scatter_2d(partial, n):
    assert n == 8
    me = lax.axis_index("dp")
    x, l, nx = me // 2, me % 2, n // 2
    blocks = partial.reshape((n, partial.shape[0] // n) + partial.shape[1:])

    def pick(m, side):
        index = 2 * ((x + m) % nx) + side
        return lax.dynamic_index_in_dim(blocks, index, 0, keepdims=False).astype(jnp.float32)

    partner_sum = x_ring_scatter([pick(m, 1 - l) for m in range(nx)], n)
    sent = lax.ppermute(partner_sum.astype(jnp.bfloat16), "dp", _y_pair(n))
    own_sum = x_ring_scatter([pick(m, l) for m in range(nx)], n)
    return own_sum + sent.astype(jnp.float32)


def to_blocks(slot_array, num_blocks, pick_count):
    expert_count = slot_array.shape[0]
    trailing = slot_array.shape[2:]
    grouped = slot_array.reshape((expert_count, num_blocks, pick_count) + trailing)
    axis_order = (1, 0, 2) + tuple(range(3, 3 + len(trailing)))
    return jnp.transpose(grouped, axis_order).reshape(
        (num_blocks, expert_count * pick_count) + trailing
    )


def weight_grads(expert_rows, hidden, expert_cot, d_pre_gate, d_pre_up, router_part, n):
    hidden_activations = hidden.shape[2]
    out_part = jnp.einsum(
        "erc,erd->cd", hidden, expert_cot, preferred_element_type=jnp.float32
    ).astype(jnp.bfloat16)
    out_share = dp_scatter_2d(out_part, n)
    both_grads = jnp.concatenate([d_pre_gate, d_pre_up], axis=2)
    in_part = jnp.einsum(
        "erc,erk->ck", expert_rows, both_grads, preferred_element_type=jnp.float32
    ).astype(jnp.bfloat16)
    router_part, in_part = lax.optimization_barrier((router_part, in_part))
    in_share = dp_scatter_2d(in_part, n)
    grad_router = jnp.sum(
        lax.all_to_all(
            jnp.broadcast_to(router_part[None], (n,) + router_part.shape), "dp", 0, 0, tiled=True
        ),
        axis=0,
    )
    grad_gate = in_share[None, :, :hidden_activations]
    grad_up = in_share[None, :, hidden_activations:]
    down_weight_gradient = out_share[None]
    return (grad_gate, grad_up, down_weight_gradient, grad_router)


def body(tokens, cotangent, chosen, w_router, w_gate, w_up, w_down):
    tok_rows, model_width = tokens.shape
    num_blocks, expert_count, pick_count = chosen.shape
    block_rows = tok_rows // num_blocks
    slot_count = num_blocks * pick_count
    logits = jnp.dot(tokens, w_router, preferred_element_type=jnp.float32)
    gate_values = jax.nn.sigmoid(logits)
    offsets = (jnp.arange(num_blocks, dtype=jnp.int32) * block_rows)[:, None, None]
    slot_rows = jnp.transpose(chosen + offsets, (1, 0, 2)).reshape(expert_count, slot_count)
    picked = tokens[slot_rows]
    slot_gate_values = jnp.take_along_axis(gate_values.T, slot_rows, axis=1)
    cot_rows = cotangent[slot_rows]
    scaled_cot = (slot_gate_values[:, :, None] * cot_rows.astype(jnp.float32)).astype(jnp.bfloat16)
    n = lax.axis_size("dp")
    shard_rows = w_gate.shape[1]
    packed = jnp.concatenate(
        [w_gate[0], w_up[0], w_down[0].reshape(-1, w_gate.shape[2])], axis=0
    )
    full = dp_gather_2d(packed, n)
    full_gate = full[:, :shard_rows].reshape(1, -1, w_gate.shape[2])
    full_up = full[:, shard_rows : 2 * shard_rows].reshape(1, -1, w_up.shape[2])
    full_down = full[:, 2 * shard_rows :].reshape(1, -1, w_down.shape[2])
    expert_count_axis = lax.axis_size("expert")
    expert_rows = lax.all_to_all(picked, "expert", 0, 0, tiled=True).reshape(1, -1, model_width)
    pre_gate = jnp.einsum(
        "erd,edh->erh", expert_rows, full_gate, preferred_element_type=jnp.float32
    )
    pre_up = jnp.einsum("erd,edh->erh", expert_rows, full_up, preferred_element_type=jnp.float32)
    silu_gate = jax.nn.silu(pre_gate)
    hidden = (silu_gate * pre_up).astype(jnp.bfloat16)
    expert_out = jnp.einsum(
        "erh,ehd->erd", hidden, full_down, preferred_element_type=jnp.float32
    ).astype(jnp.bfloat16)
    returned = lax.all_to_all(
        expert_out.reshape(expert_count_axis, -1, model_width), "expert", 0, 0, tiled=True
    )
    expert_cot = lax.all_to_all(scaled_cot, "expert", 0, 0, tiled=True).reshape(1, -1, model_width)
    back_gate, back_up, back_down = (full_gate, full_up, full_down)
    d_hidden = jnp.einsum("erd,ehd->erh", expert_cot, back_down, preferred_element_type=jnp.float32)
    gate_sigmoid = jax.nn.sigmoid(pre_gate)
    d_pre_gate = (
        d_hidden * pre_up * gate_sigmoid * (1.0 + pre_gate * (1.0 - gate_sigmoid))
    ).astype(jnp.bfloat16)
    d_pre_up = (d_hidden * silu_gate).astype(jnp.bfloat16)
    d_rows = (
        jnp.einsum("erh,edh->erd", d_pre_gate, back_gate, preferred_element_type=jnp.float32)
        + jnp.einsum("erh,edh->erd", d_pre_up, back_up, preferred_element_type=jnp.float32)
    ).astype(jnp.bfloat16)
    row_grads = lax.all_to_all(
        d_rows.reshape(expert_count_axis, -1, model_width), "expert", 0, 0, tiled=True
    )
    position_hits = chosen[:, :, :, None] == jnp.arange(block_rows, dtype=jnp.int32)
    indicator_matrix = position_hits.reshape(num_blocks, expert_count * pick_count, block_rows)
    gate_weighted_rows = to_blocks(slot_gate_values, num_blocks, pick_count)[
        :, :, None
    ] * to_blocks(returned, num_blocks, pick_count).astype(jnp.float32)
    mixed = (
        jnp.einsum(
            "wze,wzi->wei",
            indicator_matrix.astype(jnp.float32),
            gate_weighted_rows,
            precision=lax.Precision.HIGHEST,
        )
        .reshape(tok_rows, model_width)
        .astype(jnp.bfloat16)
    )
    slot_dots = jnp.sum(cot_rows.astype(jnp.float32) * returned.astype(jnp.float32), axis=2)
    dgate = jnp.einsum(
        "bept,ebp->bte",
        position_hits.astype(jnp.float32),
        slot_dots.reshape(expert_count, num_blocks, pick_count),
        precision=lax.Precision.HIGHEST,
    ).reshape(tok_rows, expert_count)
    d_logit = (dgate * gate_values * (1.0 - gate_values)).astype(jnp.bfloat16)
    gathered_grads = jnp.einsum(
        "wze,wzi->wei",
        indicator_matrix.astype(jnp.bfloat16),
        to_blocks(row_grads, num_blocks, pick_count),
        preferred_element_type=jnp.float32,
    ).reshape(tok_rows, model_width)
    grad_tokens = (
        gathered_grads + jnp.dot(d_logit, w_router.T, preferred_element_type=jnp.float32)
    ).astype(jnp.bfloat16)
    router_full = jnp.dot(tokens.T, d_logit, preferred_element_type=jnp.float32)
    router_part = jnp.sum(
        lax.all_to_all(router_full.reshape(expert_count_axis, -1, 128), "expert", 0, 0, tiled=True),
        axis=0,
    )
    grad_gate, grad_up, down_weight_gradient, grad_router = weight_grads(
        expert_rows, hidden, expert_cot, d_pre_gate, d_pre_up, router_part, n
    )
    grad_router = lax.all_to_all(
        jnp.broadcast_to(grad_router[None], (expert_count_axis,) + grad_router.shape),
        "expert",
        0,
        0,
        tiled=True,
    ).reshape(router_full.shape)
    return (mixed, grad_tokens, grad_gate, grad_up, down_weight_gradient, grad_router)


def solution(mesh):
    placed = (
        P(("dp", "expert"), None),
        P(("dp", "expert"), None),
        P(("dp", "expert"), None, None),
        P(),
        P("expert", "dp", None),
        P("expert", "dp", None),
        P("expert", "dp", None),
    )
    return jax.shard_map(
        body,
        mesh=mesh,
        in_specs=placed,
        out_specs=(
            P(("dp", "expert"), None),
            P(("dp", "expert"), None),
            P("expert", "dp", None),
            P("expert", "dp", None),
            P("expert", "dp", None),
            P(),
        ),
        check_vma=False,
    )
```

```python
import functools

import jax
import jax.numpy as jnp
from jax import lax
from jax.experimental import pallas as pl
from jax.experimental.pallas import tpu as pltpu
from jax.sharding import PartitionSpec as P

MESH = pl.DeviceIdType.MESH


def _gather_kernel(n, *refs):
    count = (len(refs) - 3) // 2
    srcs, dsts = refs[:count], refs[count : 2 * count]
    send_sem, recv_sem, local_sem = refs[2 * count :]
    me = lax.axis_index("dp")
    ex = lax.axis_index("expert")
    barrier = pltpu.get_barrier_semaphore()
    for k in range(1, n):
        pl.semaphore_signal(barrier, inc=1, device_id=(lax.rem(me + k, n), ex), device_id_type=MESH)
    pl.semaphore_wait(barrier, n - 1)
    copies = []
    for a in range(count):
        rows = srcs[a].shape[0]
        slot = dsts[a].at[pl.ds(me * rows, rows)]
        local = pltpu.make_async_copy(srcs[a], slot, local_sem.at[a])
        local.start()
        copies.append(local)
        for k in range(1, n):
            remote = pltpu.make_async_remote_copy(
                src_ref=srcs[a],
                dst_ref=slot,
                send_sem=send_sem.at[a, k],
                recv_sem=recv_sem.at[a, k],
                device_id=(lax.rem(me + k, n), ex),
                device_id_type=MESH,
            )
            remote.start()
            copies.append(remote)
    for c in copies:
        c.wait()


def dp_all_gather(shards, n):
    count = len(shards)
    return pl.pallas_call(
        functools.partial(_gather_kernel, n),
        out_shape=[jax.ShapeDtypeStruct((n * s.shape[0],) + s.shape[1:], s.dtype) for s in shards],
        in_specs=[pl.BlockSpec(memory_space=pl.ANY)] * count,
        out_specs=[pl.BlockSpec(memory_space=pl.ANY)] * count,
        scratch_shapes=[
            pltpu.SemaphoreType.DMA((count, n)),
            pltpu.SemaphoreType.DMA((count, n)),
            pltpu.SemaphoreType.DMA((count,)),
        ],
        compiler_params=pltpu.CompilerParams(collective_id=0, has_side_effects=True),
    )(*shards)


def _exchange_kernel(n, n_scatter, *refs):
    count = (len(refs) - 3) // 2
    srcs, dsts = refs[:count], refs[count : 2 * count]
    send_sem, recv_sem, local_sem = refs[2 * count :]
    me = lax.axis_index("dp")
    ex = lax.axis_index("expert")
    barrier = pltpu.get_barrier_semaphore()
    for k in range(1, n):
        pl.semaphore_signal(barrier, inc=1, device_id=(lax.rem(me + k, n), ex), device_id_type=MESH)
    pl.semaphore_wait(barrier, n - 1)
    copies = []
    for a in range(count):
        rows = dsts[a].shape[1]
        if a < n_scatter:
            mine = srcs[a].at[pl.ds(me * rows, rows)]
        else:
            mine = srcs[a]
        local = pltpu.make_async_copy(mine, dsts[a].at[me], local_sem.at[a])
        local.start()
        copies.append(local)
        for k in range(1, n):
            peer = lax.rem(me + k, n)
            if a < n_scatter:
                part = srcs[a].at[pl.ds(peer * rows, rows)]
            else:
                part = srcs[a]
            remote = pltpu.make_async_remote_copy(
                src_ref=part,
                dst_ref=dsts[a].at[me],
                send_sem=send_sem.at[a, k],
                recv_sem=recv_sem.at[a, k],
                device_id=(peer, ex),
                device_id_type=MESH,
            )
            remote.start()
            copies.append(remote)
    for c in copies:
        c.wait()


def dp_exchange(partials, replicas, n):
    arrays = list(partials) + list(replicas)
    count = len(arrays)
    shapes = [(n, p.shape[0] // n) + p.shape[1:] for p in partials]
    shapes += [(n,) + r.shape for r in replicas]
    received = pl.pallas_call(
        functools.partial(_exchange_kernel, n, len(partials)),
        out_shape=[jax.ShapeDtypeStruct(s, a.dtype) for s, a in zip(shapes, arrays)],
        in_specs=[pl.BlockSpec(memory_space=pl.ANY)] * count,
        out_specs=[pl.BlockSpec(memory_space=pl.ANY)] * count,
        scratch_shapes=[
            pltpu.SemaphoreType.DMA((count, n)),
            pltpu.SemaphoreType.DMA((count, n)),
            pltpu.SemaphoreType.DMA((count,)),
        ],
        compiler_params=pltpu.CompilerParams(collective_id=1, has_side_effects=True),
    )(*arrays)
    return [jnp.sum(r.astype(jnp.float32), axis=0) for r in received]


def _shift_pairs(n, k):
    return [(i, (i + k) % n) for i in range(n)]


def dp_gather_permute(shard, n):
    me = lax.axis_index("dp")
    full = jnp.zeros((n,) + shard.shape, shard.dtype)
    full = lax.dynamic_update_index_in_dim(full, shard, me, 0)
    for k in range(1, n):
        got = lax.ppermute(shard, "dp", perm=_shift_pairs(n, k))
        full = lax.dynamic_update_index_in_dim(full, got, lax.rem(me + n - k, n), 0)
    return full


def dp_scatter_permute(partial, n):
    me = lax.axis_index("dp")
    blocks = partial.reshape((n, partial.shape[0] // n) + partial.shape[1:])
    total = lax.dynamic_index_in_dim(blocks, me, 0, keepdims=False).astype(jnp.float32)
    for k in range(1, n):
        piece = lax.dynamic_index_in_dim(blocks, lax.rem(me + k, n), 0, keepdims=False)
        got = lax.ppermute(piece, "dp", perm=_shift_pairs(n, k))
        total = total + got.astype(jnp.float32)
    return total


def _x_shift(n, d):
    return [(i, (i + 2 * d) % n) for i in range(n)]


def _y_pair(n):
    return [(i, i ^ 1) for i in range(n)]


def x_ring_gather(t, n):
    from_left = lax.ppermute(t, "dp", _x_shift(n, 1))
    from_right = lax.ppermute(t, "dp", _x_shift(n, -1))
    h = t.shape[0] // 2
    first = lax.ppermute(from_left[:h], "dp", _x_shift(n, 1))
    second = lax.ppermute(from_right[h:], "dp", _x_shift(n, -1))
    return [t, from_right, jnp.concatenate([first, second], axis=0), from_left]


def dp_gather_2d(t, n):
    assert n == 8
    me = lax.axis_index("dp")
    x, l, nx = me // 2, me % 2, n // 2
    partner = lax.ppermute(t, "dp", _y_pair(n))
    stacked = jnp.stack(x_ring_gather(t, n) + x_ring_gather(partner, n))
    p = jnp.arange(n, dtype=jnp.int32)
    order = (p // 2 - x) % nx + nx * (p % 2 != l).astype(jnp.int32)
    return jnp.take(stacked, order, axis=0)


def x_ring_scatter(blocks, n):
    h = blocks[0].shape[0] // 2
    low = lax.ppermute(blocks[2][:h].astype(jnp.bfloat16), "dp", _x_shift(n, 1))
    high = lax.ppermute(blocks[2][h:].astype(jnp.bfloat16), "dp", _x_shift(n, -1))
    to_right = jnp.concatenate([blocks[1][:h] + low.astype(jnp.float32), blocks[1][h:]], axis=0)
    to_left = jnp.concatenate([blocks[3][:h], blocks[3][h:] + high.astype(jnp.float32)], axis=0)
    from_left = lax.ppermute(to_right.astype(jnp.bfloat16), "dp", _x_shift(n, 1))
    from_right = lax.ppermute(to_left.astype(jnp.bfloat16), "dp", _x_shift(n, -1))
    return blocks[0] + from_left.astype(jnp.float32) + from_right.astype(jnp.float32)


def dp_scatter_2d(partial, n):
    assert n == 8
    me = lax.axis_index("dp")
    x, l, nx = me // 2, me % 2, n // 2
    blocks = partial.reshape((n, partial.shape[0] // n) + partial.shape[1:])

    def pick(m, side):
        index = 2 * ((x + m) % nx) + side
        return lax.dynamic_index_in_dim(blocks, index, 0, keepdims=False).astype(jnp.float32)

    partner_sum = x_ring_scatter([pick(m, 1 - l) for m in range(nx)], n)
    sent = lax.ppermute(partner_sum.astype(jnp.bfloat16), "dp", _y_pair(n))
    own_sum = x_ring_scatter([pick(m, l) for m in range(nx)], n)
    return own_sum + sent.astype(jnp.float32)


def to_blocks(slot_array, num_blocks, pick_count):
    expert_count = slot_array.shape[0]
    trailing = slot_array.shape[2:]
    grouped = slot_array.reshape((expert_count, num_blocks, pick_count) + trailing)
    axis_order = (1, 0, 2) + tuple(range(3, 3 + len(trailing)))
    return jnp.transpose(grouped, axis_order).reshape(
        (num_blocks, expert_count * pick_count) + trailing
    )


def weight_grads(expert_rows, hidden, expert_cot, d_pre_gate, d_pre_up, n):
    hidden_activations = hidden.shape[2]
    out_part = jnp.einsum(
        "erc,erd->cd", hidden, expert_cot, preferred_element_type=jnp.float32
    ).astype(jnp.bfloat16)
    out_share = dp_scatter_2d(out_part, n)
    both_grads = jnp.concatenate([d_pre_gate, d_pre_up], axis=2)
    in_part = jnp.einsum(
        "erc,erk->ck", expert_rows, both_grads, preferred_element_type=jnp.float32
    ).astype(jnp.bfloat16)
    in_share = dp_scatter_2d(in_part, n)
    grad_gate = in_share[None, :, :hidden_activations]
    grad_up = in_share[None, :, hidden_activations:]
    down_weight_gradient = out_share[None]
    return (grad_gate, grad_up, down_weight_gradient)


def body(tokens, cotangent, chosen, w_router, w_gate, w_up, w_down):
    tok_rows, model_width = tokens.shape
    num_blocks, expert_count, pick_count = chosen.shape
    block_rows = tok_rows // num_blocks
    slot_count = num_blocks * pick_count
    logits = jnp.dot(tokens, w_router, preferred_element_type=jnp.float32)
    gate_values = jax.nn.sigmoid(logits)
    offsets = (jnp.arange(num_blocks, dtype=jnp.int32) * block_rows)[:, None, None]
    slot_rows = jnp.transpose(chosen + offsets, (1, 0, 2)).reshape(expert_count, slot_count)
    picked = tokens[slot_rows]
    slot_gate_values = jnp.take_along_axis(gate_values.T, slot_rows, axis=1)
    cot_rows = cotangent[slot_rows]
    scaled_cot = (slot_gate_values[:, :, None] * cot_rows.astype(jnp.float32)).astype(jnp.bfloat16)
    n = lax.axis_size("dp")
    gate_up = dp_gather_2d(jnp.stack([w_gate[0], w_up[0]]), n)
    full_gate = gate_up[:, 0].reshape(1, -1, w_gate.shape[2])
    full_up = gate_up[:, 1].reshape(1, -1, w_up.shape[2])
    full_down = dp_gather_2d(w_down[0], n).reshape(1, -1, w_down.shape[2])
    expert_count_axis = lax.axis_size("expert")
    expert_rows = lax.all_to_all(picked, "expert", 0, 0, tiled=True).reshape(1, -1, model_width)
    pre_gate = jnp.einsum(
        "erd,edh->erh", expert_rows, full_gate, preferred_element_type=jnp.float32
    )
    pre_up = jnp.einsum("erd,edh->erh", expert_rows, full_up, preferred_element_type=jnp.float32)
    silu_gate = jax.nn.silu(pre_gate)
    hidden = (silu_gate * pre_up).astype(jnp.bfloat16)
    expert_out = jnp.einsum(
        "erh,ehd->erd", hidden, full_down, preferred_element_type=jnp.float32
    ).astype(jnp.bfloat16)
    returned = lax.all_to_all(
        expert_out.reshape(expert_count_axis, -1, model_width), "expert", 0, 0, tiled=True
    )
    expert_cot = lax.all_to_all(scaled_cot, "expert", 0, 0, tiled=True).reshape(1, -1, model_width)
    back_gate, back_up, back_down = (full_gate, full_up, full_down)
    d_hidden = jnp.einsum("erd,ehd->erh", expert_cot, back_down, preferred_element_type=jnp.float32)
    gate_sigmoid = jax.nn.sigmoid(pre_gate)
    d_pre_gate = (
        d_hidden * pre_up * gate_sigmoid * (1.0 + pre_gate * (1.0 - gate_sigmoid))
    ).astype(jnp.bfloat16)
    d_pre_up = (d_hidden * silu_gate).astype(jnp.bfloat16)
    d_rows = (
        jnp.einsum("erh,edh->erd", d_pre_gate, back_gate, preferred_element_type=jnp.float32)
        + jnp.einsum("erh,edh->erd", d_pre_up, back_up, preferred_element_type=jnp.float32)
    ).astype(jnp.bfloat16)
    position_hits = chosen[:, :, :, None] == jnp.arange(block_rows, dtype=jnp.int32)
    indicator_matrix = position_hits.reshape(num_blocks, expert_count * pick_count, block_rows)
    gate_weighted_rows = to_blocks(slot_gate_values, num_blocks, pick_count)[
        :, :, None
    ] * to_blocks(returned, num_blocks, pick_count).astype(jnp.float32)
    mixed = (
        jnp.einsum(
            "wze,wzi->wei",
            indicator_matrix.astype(jnp.float32),
            gate_weighted_rows,
            precision=lax.Precision.HIGHEST,
        )
        .reshape(tok_rows, model_width)
        .astype(jnp.bfloat16)
    )
    slot_dots = jnp.sum(cot_rows.astype(jnp.float32) * returned.astype(jnp.float32), axis=2)
    dgate = jnp.einsum(
        "bept,ebp->bte",
        position_hits.astype(jnp.float32),
        slot_dots.reshape(expert_count, num_blocks, pick_count),
        precision=lax.Precision.HIGHEST,
    ).reshape(tok_rows, expert_count)
    d_logit = (dgate * gate_values * (1.0 - gate_values)).astype(jnp.bfloat16)
    router_full = jnp.dot(tokens.T, d_logit, preferred_element_type=jnp.float32)
    router_part = jnp.sum(
        lax.all_to_all(router_full.reshape(expert_count_axis, -1, 128), "expert", 0, 0, tiled=True),
        axis=0,
    )
    router_part = jnp.sum(
        lax.all_to_all(jnp.broadcast_to(router_part[None], (n,) + router_part.shape), "dp", 0, 0, tiled=True),
        axis=0,
    )
    grad_router = lax.all_to_all(
        jnp.broadcast_to(router_part[None], (expert_count_axis,) + router_part.shape),
        "expert",
        0,
        0,
        tiled=True,
    ).reshape(router_full.shape)
    grad_router, d_rows = lax.optimization_barrier((grad_router, d_rows))
    row_grads = lax.all_to_all(
        d_rows.reshape(expert_count_axis, -1, model_width), "expert", 0, 0, tiled=True
    )
    gathered_grads = jnp.einsum(
        "wze,wzi->wei",
        indicator_matrix.astype(jnp.bfloat16),
        to_blocks(row_grads, num_blocks, pick_count),
        preferred_element_type=jnp.float32,
    ).reshape(tok_rows, model_width)
    grad_tokens = (
        gathered_grads + jnp.dot(d_logit, w_router.T, preferred_element_type=jnp.float32)
    ).astype(jnp.bfloat16)
    grad_gate, grad_up, down_weight_gradient = weight_grads(
        expert_rows, hidden, expert_cot, d_pre_gate, d_pre_up, n
    )
    return (mixed, grad_tokens, grad_gate, grad_up, down_weight_gradient, grad_router)


def solution(mesh):
    placed = (
        P(("dp", "expert"), None),
        P(("dp", "expert"), None),
        P(("dp", "expert"), None, None),
        P(),
        P("expert", "dp", None),
        P("expert", "dp", None),
        P("expert", "dp", None),
    )
    return jax.shard_map(
        body,
        mesh=mesh,
        in_specs=placed,
        out_specs=(
            P(("dp", "expert"), None),
            P(("dp", "expert"), None),
            P("expert", "dp", None),
            P("expert", "dp", None),
            P("expert", "dp", None),
            P(),
        ),
        check_vma=False,
    )
```

```python
import functools

import jax
import jax.numpy as jnp
from jax import lax
from jax.experimental import pallas as pl
from jax.experimental.pallas import tpu as pltpu
from jax.sharding import PartitionSpec as P

MESH = pl.DeviceIdType.MESH


def _gather_kernel(n, *refs):
    count = (len(refs) - 3) // 2
    srcs, dsts = refs[:count], refs[count : 2 * count]
    send_sem, recv_sem, local_sem = refs[2 * count :]
    me = lax.axis_index("dp")
    ex = lax.axis_index("expert")
    barrier = pltpu.get_barrier_semaphore()
    for k in range(1, n):
        pl.semaphore_signal(barrier, inc=1, device_id=(lax.rem(me + k, n), ex), device_id_type=MESH)
    pl.semaphore_wait(barrier, n - 1)
    copies = []
    for a in range(count):
        rows = srcs[a].shape[0]
        slot = dsts[a].at[pl.ds(me * rows, rows)]
        local = pltpu.make_async_copy(srcs[a], slot, local_sem.at[a])
        local.start()
        copies.append(local)
        for k in range(1, n):
            remote = pltpu.make_async_remote_copy(
                src_ref=srcs[a],
                dst_ref=slot,
                send_sem=send_sem.at[a, k],
                recv_sem=recv_sem.at[a, k],
                device_id=(lax.rem(me + k, n), ex),
                device_id_type=MESH,
            )
            remote.start()
            copies.append(remote)
    for c in copies:
        c.wait()


def dp_all_gather(shards, n):
    count = len(shards)
    return pl.pallas_call(
        functools.partial(_gather_kernel, n),
        out_shape=[jax.ShapeDtypeStruct((n * s.shape[0],) + s.shape[1:], s.dtype) for s in shards],
        in_specs=[pl.BlockSpec(memory_space=pl.ANY)] * count,
        out_specs=[pl.BlockSpec(memory_space=pl.ANY)] * count,
        scratch_shapes=[
            pltpu.SemaphoreType.DMA((count, n)),
            pltpu.SemaphoreType.DMA((count, n)),
            pltpu.SemaphoreType.DMA((count,)),
        ],
        compiler_params=pltpu.CompilerParams(collective_id=0, has_side_effects=True),
    )(*shards)


def _exchange_kernel(n, n_scatter, *refs):
    count = (len(refs) - 3) // 2
    srcs, dsts = refs[:count], refs[count : 2 * count]
    send_sem, recv_sem, local_sem = refs[2 * count :]
    me = lax.axis_index("dp")
    ex = lax.axis_index("expert")
    barrier = pltpu.get_barrier_semaphore()
    for k in range(1, n):
        pl.semaphore_signal(barrier, inc=1, device_id=(lax.rem(me + k, n), ex), device_id_type=MESH)
    pl.semaphore_wait(barrier, n - 1)
    copies = []
    for a in range(count):
        rows = dsts[a].shape[1]
        if a < n_scatter:
            mine = srcs[a].at[pl.ds(me * rows, rows)]
        else:
            mine = srcs[a]
        local = pltpu.make_async_copy(mine, dsts[a].at[me], local_sem.at[a])
        local.start()
        copies.append(local)
        for k in range(1, n):
            peer = lax.rem(me + k, n)
            if a < n_scatter:
                part = srcs[a].at[pl.ds(peer * rows, rows)]
            else:
                part = srcs[a]
            remote = pltpu.make_async_remote_copy(
                src_ref=part,
                dst_ref=dsts[a].at[me],
                send_sem=send_sem.at[a, k],
                recv_sem=recv_sem.at[a, k],
                device_id=(peer, ex),
                device_id_type=MESH,
            )
            remote.start()
            copies.append(remote)
    for c in copies:
        c.wait()


def dp_exchange(partials, replicas, n):
    arrays = list(partials) + list(replicas)
    count = len(arrays)
    shapes = [(n, p.shape[0] // n) + p.shape[1:] for p in partials]
    shapes += [(n,) + r.shape for r in replicas]
    received = pl.pallas_call(
        functools.partial(_exchange_kernel, n, len(partials)),
        out_shape=[jax.ShapeDtypeStruct(s, a.dtype) for s, a in zip(shapes, arrays)],
        in_specs=[pl.BlockSpec(memory_space=pl.ANY)] * count,
        out_specs=[pl.BlockSpec(memory_space=pl.ANY)] * count,
        scratch_shapes=[
            pltpu.SemaphoreType.DMA((count, n)),
            pltpu.SemaphoreType.DMA((count, n)),
            pltpu.SemaphoreType.DMA((count,)),
        ],
        compiler_params=pltpu.CompilerParams(collective_id=1, has_side_effects=True),
    )(*arrays)
    return [jnp.sum(r.astype(jnp.float32), axis=0) for r in received]


def _shift_pairs(n, k):
    return [(i, (i + k) % n) for i in range(n)]


def dp_gather_permute(shard, n):
    me = lax.axis_index("dp")
    full = jnp.zeros((n,) + shard.shape, shard.dtype)
    full = lax.dynamic_update_index_in_dim(full, shard, me, 0)
    for k in range(1, n):
        got = lax.ppermute(shard, "dp", perm=_shift_pairs(n, k))
        full = lax.dynamic_update_index_in_dim(full, got, lax.rem(me + n - k, n), 0)
    return full


def dp_scatter_permute(partial, n):
    me = lax.axis_index("dp")
    blocks = partial.reshape((n, partial.shape[0] // n) + partial.shape[1:])
    total = lax.dynamic_index_in_dim(blocks, me, 0, keepdims=False).astype(jnp.float32)
    for k in range(1, n):
        piece = lax.dynamic_index_in_dim(blocks, lax.rem(me + k, n), 0, keepdims=False)
        got = lax.ppermute(piece, "dp", perm=_shift_pairs(n, k))
        total = total + got.astype(jnp.float32)
    return total


def _x_shift(n, d):
    return [(i, (i + 2 * d) % n) for i in range(n)]


def _y_pair(n):
    return [(i, i ^ 1) for i in range(n)]


def x_ring_gather(t, n):
    from_left = lax.ppermute(t, "dp", _x_shift(n, 1))
    from_right = lax.ppermute(t, "dp", _x_shift(n, -1))
    h = t.shape[0] // 2
    first = lax.ppermute(from_left[:h], "dp", _x_shift(n, 1))
    second = lax.ppermute(from_right[h:], "dp", _x_shift(n, -1))
    return [t, from_right, jnp.concatenate([first, second], axis=0), from_left]


def dp_gather_2d(t, n):
    assert n == 8
    me = lax.axis_index("dp")
    x, l, nx = me // 2, me % 2, n // 2
    partner = lax.ppermute(t, "dp", _y_pair(n))
    stacked = jnp.stack(x_ring_gather(t, n) + x_ring_gather(partner, n))
    p = jnp.arange(n, dtype=jnp.int32)
    order = (p // 2 - x) % nx + nx * (p % 2 != l).astype(jnp.int32)
    return jnp.take(stacked, order, axis=0)


def x_ring_scatter(blocks, n):
    h = blocks[0].shape[0] // 2
    low = lax.ppermute(blocks[2][:h].astype(jnp.bfloat16), "dp", _x_shift(n, 1))
    high = lax.ppermute(blocks[2][h:].astype(jnp.bfloat16), "dp", _x_shift(n, -1))
    to_right = jnp.concatenate([blocks[1][:h] + low.astype(jnp.float32), blocks[1][h:]], axis=0)
    to_left = jnp.concatenate([blocks[3][:h], blocks[3][h:] + high.astype(jnp.float32)], axis=0)
    from_left = lax.ppermute(to_right.astype(jnp.bfloat16), "dp", _x_shift(n, 1))
    from_right = lax.ppermute(to_left.astype(jnp.bfloat16), "dp", _x_shift(n, -1))
    return blocks[0] + from_left.astype(jnp.float32) + from_right.astype(jnp.float32)


def dp_scatter_2d(partial, n):
    assert n == 8
    me = lax.axis_index("dp")
    x, l, nx = me // 2, me % 2, n // 2
    blocks = partial.reshape((n, partial.shape[0] // n) + partial.shape[1:])

    def pick(m, side):
        index = 2 * ((x + m) % nx) + side
        return lax.dynamic_index_in_dim(blocks, index, 0, keepdims=False).astype(jnp.float32)

    partner_sum = x_ring_scatter([pick(m, 1 - l) for m in range(nx)], n)
    sent = lax.ppermute(partner_sum.astype(jnp.bfloat16), "dp", _y_pair(n))
    own_sum = x_ring_scatter([pick(m, l) for m in range(nx)], n)
    return own_sum + sent.astype(jnp.float32)


def to_blocks(slot_array, num_blocks, pick_count):
    expert_count = slot_array.shape[0]
    trailing = slot_array.shape[2:]
    grouped = slot_array.reshape((expert_count, num_blocks, pick_count) + trailing)
    axis_order = (1, 0, 2) + tuple(range(3, 3 + len(trailing)))
    return jnp.transpose(grouped, axis_order).reshape(
        (num_blocks, expert_count * pick_count) + trailing
    )


def weight_grads(hidden, expert_cot, in_part, n):
    hidden_activations = hidden.shape[2]
    out_part = jnp.einsum(
        "erc,erd->cd", hidden, expert_cot, preferred_element_type=jnp.float32
    ).astype(jnp.bfloat16)
    out_share = dp_scatter_2d(out_part, n)
    in_share = dp_scatter_2d(in_part, n)
    grad_gate = in_share[None, :, :hidden_activations]
    grad_up = in_share[None, :, hidden_activations:]
    down_weight_gradient = out_share[None]
    return (grad_gate, grad_up, down_weight_gradient)


def body(tokens, cotangent, chosen, w_router, w_gate, w_up, w_down):
    tok_rows, model_width = tokens.shape
    num_blocks, expert_count, pick_count = chosen.shape
    block_rows = tok_rows // num_blocks
    slot_count = num_blocks * pick_count
    logits = jnp.dot(tokens, w_router, preferred_element_type=jnp.float32)
    gate_values = jax.nn.sigmoid(logits)
    offsets = (jnp.arange(num_blocks, dtype=jnp.int32) * block_rows)[:, None, None]
    slot_rows = jnp.transpose(chosen + offsets, (1, 0, 2)).reshape(expert_count, slot_count)
    picked = tokens[slot_rows]
    slot_gate_values = jnp.take_along_axis(gate_values.T, slot_rows, axis=1)
    cot_rows = cotangent[slot_rows]
    scaled_cot = (slot_gate_values[:, :, None] * cot_rows.astype(jnp.float32)).astype(jnp.bfloat16)
    n = lax.axis_size("dp")
    gate_up = dp_gather_2d(jnp.stack([w_gate[0], w_up[0]]), n)
    full_gate = gate_up[:, 0].reshape(1, -1, w_gate.shape[2])
    full_up = gate_up[:, 1].reshape(1, -1, w_up.shape[2])
    full_down = dp_gather_2d(w_down[0], n).reshape(1, -1, w_down.shape[2])
    expert_count_axis = lax.axis_size("expert")
    expert_rows = lax.all_to_all(picked, "expert", 0, 0, tiled=True).reshape(1, -1, model_width)
    pre_gate = jnp.einsum(
        "erd,edh->erh", expert_rows, full_gate, preferred_element_type=jnp.float32
    )
    pre_up = jnp.einsum("erd,edh->erh", expert_rows, full_up, preferred_element_type=jnp.float32)
    silu_gate = jax.nn.silu(pre_gate)
    hidden = (silu_gate * pre_up).astype(jnp.bfloat16)
    expert_out = jnp.einsum(
        "erh,ehd->erd", hidden, full_down, preferred_element_type=jnp.float32
    ).astype(jnp.bfloat16)
    returned = lax.all_to_all(
        expert_out.reshape(expert_count_axis, -1, model_width), "expert", 0, 0, tiled=True
    )
    expert_cot = lax.all_to_all(scaled_cot, "expert", 0, 0, tiled=True).reshape(1, -1, model_width)
    back_gate, back_up, back_down = (full_gate, full_up, full_down)
    d_hidden = jnp.einsum("erd,ehd->erh", expert_cot, back_down, preferred_element_type=jnp.float32)
    gate_sigmoid = jax.nn.sigmoid(pre_gate)
    d_pre_gate = (
        d_hidden * pre_up * gate_sigmoid * (1.0 + pre_gate * (1.0 - gate_sigmoid))
    ).astype(jnp.bfloat16)
    d_pre_up = (d_hidden * silu_gate).astype(jnp.bfloat16)
    in_part = jnp.einsum(
        "erc,erk->ck",
        expert_rows,
        jnp.concatenate([d_pre_gate, d_pre_up], axis=2),
        preferred_element_type=jnp.float32,
    ).astype(jnp.bfloat16)
    in_part, d_pre_gate, d_pre_up = lax.optimization_barrier((in_part, d_pre_gate, d_pre_up))
    d_rows = (
        jnp.einsum("erh,edh->erd", d_pre_gate, back_gate, preferred_element_type=jnp.float32)
        + jnp.einsum("erh,edh->erd", d_pre_up, back_up, preferred_element_type=jnp.float32)
    ).astype(jnp.bfloat16)
    position_hits = chosen[:, :, :, None] == jnp.arange(block_rows, dtype=jnp.int32)
    indicator_matrix = position_hits.reshape(num_blocks, expert_count * pick_count, block_rows)
    gate_weighted_rows = to_blocks(slot_gate_values, num_blocks, pick_count)[
        :, :, None
    ] * to_blocks(returned, num_blocks, pick_count).astype(jnp.float32)
    mixed = (
        jnp.einsum(
            "wze,wzi->wei",
            indicator_matrix.astype(jnp.float32),
            gate_weighted_rows,
            precision=lax.Precision.HIGHEST,
        )
        .reshape(tok_rows, model_width)
        .astype(jnp.bfloat16)
    )
    slot_dots = jnp.sum(cot_rows.astype(jnp.float32) * returned.astype(jnp.float32), axis=2)
    dgate = jnp.einsum(
        "bept,ebp->bte",
        position_hits.astype(jnp.float32),
        slot_dots.reshape(expert_count, num_blocks, pick_count),
        precision=lax.Precision.HIGHEST,
    ).reshape(tok_rows, expert_count)
    d_logit = (dgate * gate_values * (1.0 - gate_values)).astype(jnp.bfloat16)
    router_full = jnp.dot(tokens.T, d_logit, preferred_element_type=jnp.float32)
    router_part = jnp.sum(
        lax.all_to_all(router_full.reshape(expert_count_axis, -1, 128), "expert", 0, 0, tiled=True),
        axis=0,
    )
    router_part = jnp.sum(
        lax.all_to_all(jnp.broadcast_to(router_part[None], (n,) + router_part.shape), "dp", 0, 0, tiled=True),
        axis=0,
    )
    grad_router = lax.all_to_all(
        jnp.broadcast_to(router_part[None], (expert_count_axis,) + router_part.shape),
        "expert",
        0,
        0,
        tiled=True,
    ).reshape(router_full.shape)
    grad_router, d_rows = lax.optimization_barrier((grad_router, d_rows))
    row_grads = lax.all_to_all(
        d_rows.reshape(expert_count_axis, -1, model_width), "expert", 0, 0, tiled=True
    )
    gathered_grads = jnp.einsum(
        "wze,wzi->wei",
        indicator_matrix.astype(jnp.bfloat16),
        to_blocks(row_grads, num_blocks, pick_count),
        preferred_element_type=jnp.float32,
    ).reshape(tok_rows, model_width)
    grad_tokens = (
        gathered_grads + jnp.dot(d_logit, w_router.T, preferred_element_type=jnp.float32)
    ).astype(jnp.bfloat16)
    grad_gate, grad_up, down_weight_gradient = weight_grads(hidden, expert_cot, in_part, n)
    return (mixed, grad_tokens, grad_gate, grad_up, down_weight_gradient, grad_router)


def solution(mesh):
    placed = (
        P(("dp", "expert"), None),
        P(("dp", "expert"), None),
        P(("dp", "expert"), None, None),
        P(),
        P("expert", "dp", None),
        P("expert", "dp", None),
        P("expert", "dp", None),
    )
    return jax.shard_map(
        body,
        mesh=mesh,
        in_specs=placed,
        out_specs=(
            P(("dp", "expert"), None),
            P(("dp", "expert"), None),
            P("expert", "dp", None),
            P("expert", "dp", None),
            P("expert", "dp", None),
            P(),
        ),
        check_vma=False,
    )
```

```python
import functools

import jax
import jax.numpy as jnp
from jax import lax
from jax.experimental import pallas as pl
from jax.experimental.pallas import tpu as pltpu
from jax.sharding import PartitionSpec as P

MESH = pl.DeviceIdType.MESH


def _gather_kernel(n, *refs):
    count = (len(refs) - 3) // 2
    srcs, dsts = refs[:count], refs[count : 2 * count]
    send_sem, recv_sem, local_sem = refs[2 * count :]
    me = lax.axis_index("dp")
    ex = lax.axis_index("expert")
    barrier = pltpu.get_barrier_semaphore()
    for k in range(1, n):
        pl.semaphore_signal(barrier, inc=1, device_id=(lax.rem(me + k, n), ex), device_id_type=MESH)
    pl.semaphore_wait(barrier, n - 1)
    copies = []
    for a in range(count):
        rows = srcs[a].shape[0]
        slot = dsts[a].at[pl.ds(me * rows, rows)]
        local = pltpu.make_async_copy(srcs[a], slot, local_sem.at[a])
        local.start()
        copies.append(local)
        for k in range(1, n):
            remote = pltpu.make_async_remote_copy(
                src_ref=srcs[a],
                dst_ref=slot,
                send_sem=send_sem.at[a, k],
                recv_sem=recv_sem.at[a, k],
                device_id=(lax.rem(me + k, n), ex),
                device_id_type=MESH,
            )
            remote.start()
            copies.append(remote)
    for c in copies:
        c.wait()


def dp_all_gather(shards, n):
    count = len(shards)
    return pl.pallas_call(
        functools.partial(_gather_kernel, n),
        out_shape=[jax.ShapeDtypeStruct((n * s.shape[0],) + s.shape[1:], s.dtype) for s in shards],
        in_specs=[pl.BlockSpec(memory_space=pl.ANY)] * count,
        out_specs=[pl.BlockSpec(memory_space=pl.ANY)] * count,
        scratch_shapes=[
            pltpu.SemaphoreType.DMA((count, n)),
            pltpu.SemaphoreType.DMA((count, n)),
            pltpu.SemaphoreType.DMA((count,)),
        ],
        compiler_params=pltpu.CompilerParams(collective_id=0, has_side_effects=True),
    )(*shards)


def _exchange_kernel(n, n_scatter, *refs):
    count = (len(refs) - 3) // 2
    srcs, dsts = refs[:count], refs[count : 2 * count]
    send_sem, recv_sem, local_sem = refs[2 * count :]
    me = lax.axis_index("dp")
    ex = lax.axis_index("expert")
    barrier = pltpu.get_barrier_semaphore()
    for k in range(1, n):
        pl.semaphore_signal(barrier, inc=1, device_id=(lax.rem(me + k, n), ex), device_id_type=MESH)
    pl.semaphore_wait(barrier, n - 1)
    copies = []
    for a in range(count):
        rows = dsts[a].shape[1]
        if a < n_scatter:
            mine = srcs[a].at[pl.ds(me * rows, rows)]
        else:
            mine = srcs[a]
        local = pltpu.make_async_copy(mine, dsts[a].at[me], local_sem.at[a])
        local.start()
        copies.append(local)
        for k in range(1, n):
            peer = lax.rem(me + k, n)
            if a < n_scatter:
                part = srcs[a].at[pl.ds(peer * rows, rows)]
            else:
                part = srcs[a]
            remote = pltpu.make_async_remote_copy(
                src_ref=part,
                dst_ref=dsts[a].at[me],
                send_sem=send_sem.at[a, k],
                recv_sem=recv_sem.at[a, k],
                device_id=(peer, ex),
                device_id_type=MESH,
            )
            remote.start()
            copies.append(remote)
    for c in copies:
        c.wait()


def dp_exchange(partials, replicas, n):
    arrays = list(partials) + list(replicas)
    count = len(arrays)
    shapes = [(n, p.shape[0] // n) + p.shape[1:] for p in partials]
    shapes += [(n,) + r.shape for r in replicas]
    received = pl.pallas_call(
        functools.partial(_exchange_kernel, n, len(partials)),
        out_shape=[jax.ShapeDtypeStruct(s, a.dtype) for s, a in zip(shapes, arrays)],
        in_specs=[pl.BlockSpec(memory_space=pl.ANY)] * count,
        out_specs=[pl.BlockSpec(memory_space=pl.ANY)] * count,
        scratch_shapes=[
            pltpu.SemaphoreType.DMA((count, n)),
            pltpu.SemaphoreType.DMA((count, n)),
            pltpu.SemaphoreType.DMA((count,)),
        ],
        compiler_params=pltpu.CompilerParams(collective_id=1, has_side_effects=True),
    )(*arrays)
    return [jnp.sum(r.astype(jnp.float32), axis=0) for r in received]


def _shift_pairs(n, k):
    return [(i, (i + k) % n) for i in range(n)]


def dp_gather_permute(shard, n):
    me = lax.axis_index("dp")
    full = jnp.zeros((n,) + shard.shape, shard.dtype)
    full = lax.dynamic_update_index_in_dim(full, shard, me, 0)
    for k in range(1, n):
        got = lax.ppermute(shard, "dp", perm=_shift_pairs(n, k))
        full = lax.dynamic_update_index_in_dim(full, got, lax.rem(me + n - k, n), 0)
    return full


def dp_scatter_permute(partial, n):
    me = lax.axis_index("dp")
    blocks = partial.reshape((n, partial.shape[0] // n) + partial.shape[1:])
    total = lax.dynamic_index_in_dim(blocks, me, 0, keepdims=False).astype(jnp.float32)
    for k in range(1, n):
        piece = lax.dynamic_index_in_dim(blocks, lax.rem(me + k, n), 0, keepdims=False)
        got = lax.ppermute(piece, "dp", perm=_shift_pairs(n, k))
        total = total + got.astype(jnp.float32)
    return total


def _x_shift(n, d):
    return [(i, (i + 2 * d) % n) for i in range(n)]


def _y_pair(n):
    return [(i, i ^ 1) for i in range(n)]


def x_ring_gather(t, n):
    from_left = lax.ppermute(t, "dp", _x_shift(n, 1))
    from_right = lax.ppermute(t, "dp", _x_shift(n, -1))
    h = t.shape[0] // 2
    first = lax.ppermute(from_left[:h], "dp", _x_shift(n, 1))
    second = lax.ppermute(from_right[h:], "dp", _x_shift(n, -1))
    return [t, from_right, jnp.concatenate([first, second], axis=0), from_left]


def dp_gather_2d(t, n):
    assert n == 8
    me = lax.axis_index("dp")
    x, l, nx = me // 2, me % 2, n // 2
    partner = lax.ppermute(t, "dp", _y_pair(n))
    stacked = jnp.stack(x_ring_gather(t, n) + x_ring_gather(partner, n))
    p = jnp.arange(n, dtype=jnp.int32)
    order = (p // 2 - x) % nx + nx * (p % 2 != l).astype(jnp.int32)
    return jnp.take(stacked, order, axis=0)


def x_ring_scatter(blocks, n):
    h = blocks[0].shape[0] // 2
    low = lax.ppermute(blocks[2][:h].astype(jnp.bfloat16), "dp", _x_shift(n, 1))
    high = lax.ppermute(blocks[2][h:].astype(jnp.bfloat16), "dp", _x_shift(n, -1))
    to_right = jnp.concatenate([blocks[1][:h] + low.astype(jnp.float32), blocks[1][h:]], axis=0)
    to_left = jnp.concatenate([blocks[3][:h], blocks[3][h:] + high.astype(jnp.float32)], axis=0)
    from_left = lax.ppermute(to_right.astype(jnp.bfloat16), "dp", _x_shift(n, 1))
    from_right = lax.ppermute(to_left.astype(jnp.bfloat16), "dp", _x_shift(n, -1))
    return blocks[0] + from_left.astype(jnp.float32) + from_right.astype(jnp.float32)


def dp_scatter_2d(partial, n):
    assert n == 8
    me = lax.axis_index("dp")
    x, l, nx = me // 2, me % 2, n // 2
    blocks = partial.reshape((n, partial.shape[0] // n) + partial.shape[1:])

    def pick(m, side):
        index = 2 * ((x + m) % nx) + side
        return lax.dynamic_index_in_dim(blocks, index, 0, keepdims=False).astype(jnp.float32)

    partner_sum = x_ring_scatter([pick(m, 1 - l) for m in range(nx)], n)
    sent = lax.ppermute(partner_sum.astype(jnp.bfloat16), "dp", _y_pair(n))
    own_sum = x_ring_scatter([pick(m, l) for m in range(nx)], n)
    return own_sum + sent.astype(jnp.float32)


def _ring_gather_kernel(n, shard_ref, out_ref, send_sem, recv_sem, local_sem):
    me = lax.axis_index("dp")
    ex = lax.axis_index("expert")
    right, left, partner = lax.rem(me + 2, n), lax.rem(me + n - 2, n), me + 1 - 2 * lax.rem(me, 2)
    barrier = pltpu.get_barrier_semaphore()
    for peer in (right, left, partner):
        pl.semaphore_signal(barrier, inc=1, device_id=(peer, ex), device_id_type=MESH)
    pl.semaphore_wait(barrier, 3)
    half = shard_ref.shape[0] // 2

    def send(role, src, slot, rows, peer):
        copy = pltpu.make_async_remote_copy(
            src_ref=src,
            dst_ref=out_ref.at[slot, rows],
            send_sem=send_sem.at[role],
            recv_sem=recv_sem.at[role],
            device_id=(peer, ex),
            device_id_type=MESH,
        )
        copy.start()
        return copy

    whole, low, high = pl.ds(0, 2 * half), pl.ds(0, half), pl.ds(half, half)
    local = pltpu.make_async_copy(shard_ref, out_ref.at[me], local_sem.at[0])
    local.start()
    first = [
        send(0, shard_ref, me, whole, right),
        send(1, shard_ref, me, whole, left),
        send(2, shard_ref, me, whole, partner),
    ]
    for copy in first:
        copy.wait_recv()
    mate = partner
    second = [
        send(3, out_ref.at[left, low], left, low, right),
        send(4, out_ref.at[right, high], right, high, left),
        send(5, out_ref.at[mate], mate, whole, right),
        send(6, out_ref.at[mate], mate, whole, left),
    ]
    second[2].wait_recv()
    second[3].wait_recv()
    mate_left, mate_right = lax.rem(mate + n - 2, n), lax.rem(mate + 2, n)
    third = [
        send(7, out_ref.at[mate_left, low], mate_left, low, right),
        send(8, out_ref.at[mate_right, high], mate_right, high, left),
    ]
    for copy in first:
        copy.wait_send()
    for copy in second[:2]:
        copy.wait_recv()
    for copy in second:
        copy.wait_send()
    for copy in third:
        copy.wait_recv()
        copy.wait_send()
    local.wait()


def dp_gather_kernel(shard, n):
    assert n == 8
    return pl.pallas_call(
        functools.partial(_ring_gather_kernel, n),
        out_shape=jax.ShapeDtypeStruct((n,) + shard.shape, shard.dtype),
        in_specs=[pl.BlockSpec(memory_space=pl.ANY)],
        out_specs=pl.BlockSpec(memory_space=pl.ANY),
        scratch_shapes=[
            pltpu.SemaphoreType.DMA((9,)),
            pltpu.SemaphoreType.DMA((9,)),
            pltpu.SemaphoreType.DMA((1,)),
        ],
        compiler_params=pltpu.CompilerParams(collective_id=2, has_side_effects=True),
    )(shard)


def to_blocks(slot_array, num_blocks, pick_count):
    expert_count = slot_array.shape[0]
    trailing = slot_array.shape[2:]
    grouped = slot_array.reshape((expert_count, num_blocks, pick_count) + trailing)
    axis_order = (1, 0, 2) + tuple(range(3, 3 + len(trailing)))
    return jnp.transpose(grouped, axis_order).reshape(
        (num_blocks, expert_count * pick_count) + trailing
    )


def weight_grads(expert_rows, hidden, expert_cot, d_pre_gate, d_pre_up, router_part, n):
    hidden_activations = hidden.shape[2]
    out_part = jnp.einsum(
        "erc,erd->cd", hidden, expert_cot, preferred_element_type=jnp.float32
    ).astype(jnp.bfloat16)
    out_share = dp_scatter_2d(out_part, n)
    both_grads = jnp.concatenate([d_pre_gate, d_pre_up], axis=2)
    in_part = jnp.einsum(
        "erc,erk->ck", expert_rows, both_grads, preferred_element_type=jnp.float32
    ).astype(jnp.bfloat16)
    in_share = dp_scatter_2d(in_part, n)
    grad_router = jnp.sum(
        lax.all_to_all(
            jnp.broadcast_to(router_part[None], (n,) + router_part.shape), "dp", 0, 0, tiled=True
        ),
        axis=0,
    )
    grad_gate = in_share[None, :, :hidden_activations]
    grad_up = in_share[None, :, hidden_activations:]
    down_weight_gradient = out_share[None]
    return (grad_gate, grad_up, down_weight_gradient, grad_router)


def body(tokens, cotangent, chosen, w_router, w_gate, w_up, w_down):
    tok_rows, model_width = tokens.shape
    num_blocks, expert_count, pick_count = chosen.shape
    block_rows = tok_rows // num_blocks
    slot_count = num_blocks * pick_count
    logits = jnp.dot(tokens, w_router, preferred_element_type=jnp.float32)
    gate_values = jax.nn.sigmoid(logits)
    offsets = (jnp.arange(num_blocks, dtype=jnp.int32) * block_rows)[:, None, None]
    slot_rows = jnp.transpose(chosen + offsets, (1, 0, 2)).reshape(expert_count, slot_count)
    picked = tokens[slot_rows]
    slot_gate_values = jnp.take_along_axis(gate_values.T, slot_rows, axis=1)
    cot_rows = cotangent[slot_rows]
    scaled_cot = (slot_gate_values[:, :, None] * cot_rows.astype(jnp.float32)).astype(jnp.bfloat16)
    n = lax.axis_size("dp")
    shard_rows = w_gate.shape[1]
    packed = jnp.concatenate(
        [w_gate[0], w_up[0], w_down[0].reshape(-1, w_gate.shape[2])], axis=0
    )
    full = dp_gather_kernel(packed, n)
    full_gate = full[:, :shard_rows].reshape(1, -1, w_gate.shape[2])
    full_up = full[:, shard_rows : 2 * shard_rows].reshape(1, -1, w_up.shape[2])
    full_down = full[:, 2 * shard_rows :].reshape(1, -1, w_down.shape[2])
    expert_count_axis = lax.axis_size("expert")
    expert_rows = lax.all_to_all(picked, "expert", 0, 0, tiled=True).reshape(1, -1, model_width)
    pre_gate = jnp.einsum(
        "erd,edh->erh", expert_rows, full_gate, preferred_element_type=jnp.float32
    )
    pre_up = jnp.einsum("erd,edh->erh", expert_rows, full_up, preferred_element_type=jnp.float32)
    silu_gate = jax.nn.silu(pre_gate)
    hidden = (silu_gate * pre_up).astype(jnp.bfloat16)
    expert_out = jnp.einsum(
        "erh,ehd->erd", hidden, full_down, preferred_element_type=jnp.float32
    ).astype(jnp.bfloat16)
    returned = lax.all_to_all(
        expert_out.reshape(expert_count_axis, -1, model_width), "expert", 0, 0, tiled=True
    )
    expert_cot = lax.all_to_all(scaled_cot, "expert", 0, 0, tiled=True).reshape(1, -1, model_width)
    back_gate, back_up, back_down = (full_gate, full_up, full_down)
    d_hidden = jnp.einsum("erd,ehd->erh", expert_cot, back_down, preferred_element_type=jnp.float32)
    gate_sigmoid = jax.nn.sigmoid(pre_gate)
    d_pre_gate = (
        d_hidden * pre_up * gate_sigmoid * (1.0 + pre_gate * (1.0 - gate_sigmoid))
    ).astype(jnp.bfloat16)
    d_pre_up = (d_hidden * silu_gate).astype(jnp.bfloat16)
    d_rows = (
        jnp.einsum("erh,edh->erd", d_pre_gate, back_gate, preferred_element_type=jnp.float32)
        + jnp.einsum("erh,edh->erd", d_pre_up, back_up, preferred_element_type=jnp.float32)
    ).astype(jnp.bfloat16)
    row_grads = lax.all_to_all(
        d_rows.reshape(expert_count_axis, -1, model_width), "expert", 0, 0, tiled=True
    )
    position_hits = chosen[:, :, :, None] == jnp.arange(block_rows, dtype=jnp.int32)
    indicator_matrix = position_hits.reshape(num_blocks, expert_count * pick_count, block_rows)
    gate_weighted_rows = to_blocks(slot_gate_values, num_blocks, pick_count)[
        :, :, None
    ] * to_blocks(returned, num_blocks, pick_count).astype(jnp.float32)
    mixed = (
        jnp.einsum(
            "wze,wzi->wei",
            indicator_matrix.astype(jnp.float32),
            gate_weighted_rows,
            precision=lax.Precision.HIGHEST,
        )
        .reshape(tok_rows, model_width)
        .astype(jnp.bfloat16)
    )
    slot_dots = jnp.sum(cot_rows.astype(jnp.float32) * returned.astype(jnp.float32), axis=2)
    dgate = jnp.einsum(
        "bept,ebp->bte",
        position_hits.astype(jnp.float32),
        slot_dots.reshape(expert_count, num_blocks, pick_count),
        precision=lax.Precision.HIGHEST,
    ).reshape(tok_rows, expert_count)
    d_logit = (dgate * gate_values * (1.0 - gate_values)).astype(jnp.bfloat16)
    gathered_grads = jnp.einsum(
        "wze,wzi->wei",
        indicator_matrix.astype(jnp.bfloat16),
        to_blocks(row_grads, num_blocks, pick_count),
        preferred_element_type=jnp.float32,
    ).reshape(tok_rows, model_width)
    grad_tokens = (
        gathered_grads + jnp.dot(d_logit, w_router.T, preferred_element_type=jnp.float32)
    ).astype(jnp.bfloat16)
    router_full = jnp.dot(tokens.T, d_logit, preferred_element_type=jnp.float32)
    router_part = jnp.sum(
        lax.all_to_all(router_full.reshape(expert_count_axis, -1, 128), "expert", 0, 0, tiled=True),
        axis=0,
    )
    grad_gate, grad_up, down_weight_gradient, grad_router = weight_grads(
        expert_rows, hidden, expert_cot, d_pre_gate, d_pre_up, router_part, n
    )
    grad_router = lax.all_to_all(
        jnp.broadcast_to(grad_router[None], (expert_count_axis,) + grad_router.shape),
        "expert",
        0,
        0,
        tiled=True,
    ).reshape(router_full.shape)
    return (mixed, grad_tokens, grad_gate, grad_up, down_weight_gradient, grad_router)


def solution(mesh):
    placed = (
        P(("dp", "expert"), None),
        P(("dp", "expert"), None),
        P(("dp", "expert"), None, None),
        P(),
        P("expert", "dp", None),
        P("expert", "dp", None),
        P("expert", "dp", None),
    )
    return jax.shard_map(
        body,
        mesh=mesh,
        in_specs=placed,
        out_specs=(
            P(("dp", "expert"), None),
            P(("dp", "expert"), None),
            P("expert", "dp", None),
            P("expert", "dp", None),
            P("expert", "dp", None),
            P(),
        ),
        check_vma=False,
    )
```

```python
import functools

import jax
import jax.numpy as jnp
from jax import lax
from jax.experimental import pallas as pl
from jax.experimental.pallas import tpu as pltpu
from jax.sharding import PartitionSpec as P

MESH = pl.DeviceIdType.MESH


def _gather_kernel(n, *refs):
    count = (len(refs) - 3) // 2
    srcs, dsts = refs[:count], refs[count : 2 * count]
    send_sem, recv_sem, local_sem = refs[2 * count :]
    me = lax.axis_index("dp")
    ex = lax.axis_index("expert")
    barrier = pltpu.get_barrier_semaphore()
    for k in range(1, n):
        pl.semaphore_signal(barrier, inc=1, device_id=(lax.rem(me + k, n), ex), device_id_type=MESH)
    pl.semaphore_wait(barrier, n - 1)
    copies = []
    for a in range(count):
        rows = srcs[a].shape[0]
        slot = dsts[a].at[pl.ds(me * rows, rows)]
        local = pltpu.make_async_copy(srcs[a], slot, local_sem.at[a])
        local.start()
        copies.append(local)
        for k in range(1, n):
            remote = pltpu.make_async_remote_copy(
                src_ref=srcs[a],
                dst_ref=slot,
                send_sem=send_sem.at[a, k],
                recv_sem=recv_sem.at[a, k],
                device_id=(lax.rem(me + k, n), ex),
                device_id_type=MESH,
            )
            remote.start()
            copies.append(remote)
    for c in copies:
        c.wait()


def dp_all_gather(shards, n):
    count = len(shards)
    return pl.pallas_call(
        functools.partial(_gather_kernel, n),
        out_shape=[jax.ShapeDtypeStruct((n * s.shape[0],) + s.shape[1:], s.dtype) for s in shards],
        in_specs=[pl.BlockSpec(memory_space=pl.ANY)] * count,
        out_specs=[pl.BlockSpec(memory_space=pl.ANY)] * count,
        scratch_shapes=[
            pltpu.SemaphoreType.DMA((count, n)),
            pltpu.SemaphoreType.DMA((count, n)),
            pltpu.SemaphoreType.DMA((count,)),
        ],
        compiler_params=pltpu.CompilerParams(collective_id=0, has_side_effects=True),
    )(*shards)


def _exchange_kernel(n, n_scatter, *refs):
    count = (len(refs) - 3) // 2
    srcs, dsts = refs[:count], refs[count : 2 * count]
    send_sem, recv_sem, local_sem = refs[2 * count :]
    me = lax.axis_index("dp")
    ex = lax.axis_index("expert")
    barrier = pltpu.get_barrier_semaphore()
    for k in range(1, n):
        pl.semaphore_signal(barrier, inc=1, device_id=(lax.rem(me + k, n), ex), device_id_type=MESH)
    pl.semaphore_wait(barrier, n - 1)
    copies = []
    for a in range(count):
        rows = dsts[a].shape[1]
        if a < n_scatter:
            mine = srcs[a].at[pl.ds(me * rows, rows)]
        else:
            mine = srcs[a]
        local = pltpu.make_async_copy(mine, dsts[a].at[me], local_sem.at[a])
        local.start()
        copies.append(local)
        for k in range(1, n):
            peer = lax.rem(me + k, n)
            if a < n_scatter:
                part = srcs[a].at[pl.ds(peer * rows, rows)]
            else:
                part = srcs[a]
            remote = pltpu.make_async_remote_copy(
                src_ref=part,
                dst_ref=dsts[a].at[me],
                send_sem=send_sem.at[a, k],
                recv_sem=recv_sem.at[a, k],
                device_id=(peer, ex),
                device_id_type=MESH,
            )
            remote.start()
            copies.append(remote)
    for c in copies:
        c.wait()


def dp_exchange(partials, replicas, n):
    arrays = list(partials) + list(replicas)
    count = len(arrays)
    shapes = [(n, p.shape[0] // n) + p.shape[1:] for p in partials]
    shapes += [(n,) + r.shape for r in replicas]
    received = pl.pallas_call(
        functools.partial(_exchange_kernel, n, len(partials)),
        out_shape=[jax.ShapeDtypeStruct(s, a.dtype) for s, a in zip(shapes, arrays)],
        in_specs=[pl.BlockSpec(memory_space=pl.ANY)] * count,
        out_specs=[pl.BlockSpec(memory_space=pl.ANY)] * count,
        scratch_shapes=[
            pltpu.SemaphoreType.DMA((count, n)),
            pltpu.SemaphoreType.DMA((count, n)),
            pltpu.SemaphoreType.DMA((count,)),
        ],
        compiler_params=pltpu.CompilerParams(collective_id=1, has_side_effects=True),
    )(*arrays)
    return [jnp.sum(r.astype(jnp.float32), axis=0) for r in received]


def _shift_pairs(n, k):
    return [(i, (i + k) % n) for i in range(n)]


def dp_gather_permute(shard, n):
    me = lax.axis_index("dp")
    full = jnp.zeros((n,) + shard.shape, shard.dtype)
    full = lax.dynamic_update_index_in_dim(full, shard, me, 0)
    for k in range(1, n):
        got = lax.ppermute(shard, "dp", perm=_shift_pairs(n, k))
        full = lax.dynamic_update_index_in_dim(full, got, lax.rem(me + n - k, n), 0)
    return full


def dp_scatter_permute(partial, n):
    me = lax.axis_index("dp")
    blocks = partial.reshape((n, partial.shape[0] // n) + partial.shape[1:])
    total = lax.dynamic_index_in_dim(blocks, me, 0, keepdims=False).astype(jnp.float32)
    for k in range(1, n):
        piece = lax.dynamic_index_in_dim(blocks, lax.rem(me + k, n), 0, keepdims=False)
        got = lax.ppermute(piece, "dp", perm=_shift_pairs(n, k))
        total = total + got.astype(jnp.float32)
    return total


def _x_shift(n, d):
    return [(i, (i + 2 * d) % n) for i in range(n)]


def _y_pair(n):
    return [(i, i ^ 1) for i in range(n)]


def x_ring_gather(t, n):
    from_left = lax.ppermute(t, "dp", _x_shift(n, 1))
    from_right = lax.ppermute(t, "dp", _x_shift(n, -1))
    h = t.shape[0] // 2
    first = lax.ppermute(from_left[:h], "dp", _x_shift(n, 1))
    second = lax.ppermute(from_right[h:], "dp", _x_shift(n, -1))
    return [t, from_right, jnp.concatenate([first, second], axis=0), from_left]


def dp_gather_2d(t, n):
    assert n == 8
    me = lax.axis_index("dp")
    x, l, nx = me // 2, me % 2, n // 2
    partner = lax.ppermute(t, "dp", _y_pair(n))
    stacked = jnp.stack(x_ring_gather(t, n) + x_ring_gather(partner, n))
    p = jnp.arange(n, dtype=jnp.int32)
    order = (p // 2 - x) % nx + nx * (p % 2 != l).astype(jnp.int32)
    return jnp.take(stacked, order, axis=0)


def x_ring_scatter(blocks, n):
    h = blocks[0].shape[0] // 2
    low = lax.ppermute(blocks[2][:h].astype(jnp.bfloat16), "dp", _x_shift(n, 1))
    high = lax.ppermute(blocks[2][h:].astype(jnp.bfloat16), "dp", _x_shift(n, -1))
    to_right = jnp.concatenate([blocks[1][:h] + low.astype(jnp.float32), blocks[1][h:]], axis=0)
    to_left = jnp.concatenate([blocks[3][:h], blocks[3][h:] + high.astype(jnp.float32)], axis=0)
    from_left = lax.ppermute(to_right.astype(jnp.bfloat16), "dp", _x_shift(n, 1))
    from_right = lax.ppermute(to_left.astype(jnp.bfloat16), "dp", _x_shift(n, -1))
    return blocks[0] + from_left.astype(jnp.float32) + from_right.astype(jnp.float32)


def dp_scatter_2d(partial, n):
    assert n == 8
    me = lax.axis_index("dp")
    x, l, nx = me // 2, me % 2, n // 2
    blocks = partial.reshape((n, partial.shape[0] // n) + partial.shape[1:])

    def pick(m, side):
        index = 2 * ((x + m) % nx) + side
        return lax.dynamic_index_in_dim(blocks, index, 0, keepdims=False).astype(jnp.float32)

    partner_sum = x_ring_scatter([pick(m, 1 - l) for m in range(nx)], n)
    sent = lax.ppermute(partner_sum.astype(jnp.bfloat16), "dp", _y_pair(n))
    own_sum = x_ring_scatter([pick(m, l) for m in range(nx)], n)
    return own_sum + sent.astype(jnp.float32)


def _ring_gather_kernel(n, shard_ref, out_ref, send_sem, recv_sem, local_sem):
    me = lax.axis_index("dp")
    ex = lax.axis_index("expert")
    right, left, partner = lax.rem(me + 2, n), lax.rem(me + n - 2, n), me + 1 - 2 * lax.rem(me, 2)
    barrier = pltpu.get_barrier_semaphore()
    for peer in (right, left, partner):
        pl.semaphore_signal(barrier, inc=1, device_id=(peer, ex), device_id_type=MESH)
    pl.semaphore_wait(barrier, 3)
    half = shard_ref.shape[0] // 2

    def send(role, src, slot, rows, peer):
        copy = pltpu.make_async_remote_copy(
            src_ref=src,
            dst_ref=out_ref.at[slot, rows],
            send_sem=send_sem.at[role],
            recv_sem=recv_sem.at[role],
            device_id=(peer, ex),
            device_id_type=MESH,
        )
        copy.start()
        return copy

    whole, low, high = pl.ds(0, 2 * half), pl.ds(0, half), pl.ds(half, half)
    local = pltpu.make_async_copy(shard_ref, out_ref.at[me], local_sem.at[0])
    local.start()
    first = [
        send(0, shard_ref, me, whole, right),
        send(1, shard_ref, me, whole, left),
        send(2, shard_ref, me, whole, partner),
    ]
    for copy in first:
        copy.wait_recv()
    mate = partner
    second = [
        send(3, out_ref.at[left, low], left, low, right),
        send(4, out_ref.at[right, high], right, high, left),
        send(5, out_ref.at[mate], mate, whole, right),
        send(6, out_ref.at[mate], mate, whole, left),
    ]
    second[2].wait_recv()
    second[3].wait_recv()
    mate_left, mate_right = lax.rem(mate + n - 2, n), lax.rem(mate + 2, n)
    third = [
        send(7, out_ref.at[mate_left, low], mate_left, low, right),
        send(8, out_ref.at[mate_right, high], mate_right, high, left),
    ]
    for copy in first:
        copy.wait_send()
    for copy in second[:2]:
        copy.wait_recv()
    for copy in second:
        copy.wait_send()
    for copy in third:
        copy.wait_recv()
        copy.wait_send()
    local.wait()


def dp_gather_kernel(shard, n):
    assert n == 8
    return pl.pallas_call(
        functools.partial(_ring_gather_kernel, n),
        out_shape=jax.ShapeDtypeStruct((n,) + shard.shape, shard.dtype),
        in_specs=[pl.BlockSpec(memory_space=pl.ANY)],
        out_specs=pl.BlockSpec(memory_space=pl.ANY),
        scratch_shapes=[
            pltpu.SemaphoreType.DMA((9,)),
            pltpu.SemaphoreType.DMA((9,)),
            pltpu.SemaphoreType.DMA((1,)),
        ],
        compiler_params=pltpu.CompilerParams(collective_id=2, has_side_effects=True),
    )(shard)


def to_blocks(slot_array, num_blocks, pick_count):
    expert_count = slot_array.shape[0]
    trailing = slot_array.shape[2:]
    grouped = slot_array.reshape((expert_count, num_blocks, pick_count) + trailing)
    axis_order = (1, 0, 2) + tuple(range(3, 3 + len(trailing)))
    return jnp.transpose(grouped, axis_order).reshape(
        (num_blocks, expert_count * pick_count) + trailing
    )


def weight_grads(expert_rows, hidden, expert_cot, d_pre_gate, d_pre_up, n):
    hidden_activations = hidden.shape[2]
    out_part = jnp.einsum(
        "erc,erd->cd", hidden, expert_cot, preferred_element_type=jnp.float32
    ).astype(jnp.bfloat16)
    out_share = dp_scatter_2d(out_part, n)
    both_grads = jnp.concatenate([d_pre_gate, d_pre_up], axis=2)
    in_part = jnp.einsum(
        "erc,erk->ck", expert_rows, both_grads, preferred_element_type=jnp.float32
    ).astype(jnp.bfloat16)
    in_share = dp_scatter_2d(in_part, n)
    grad_gate = in_share[None, :, :hidden_activations]
    grad_up = in_share[None, :, hidden_activations:]
    down_weight_gradient = out_share[None]
    return (grad_gate, grad_up, down_weight_gradient)


def body(tokens, cotangent, chosen, w_router, w_gate, w_up, w_down):
    tok_rows, model_width = tokens.shape
    num_blocks, expert_count, pick_count = chosen.shape
    block_rows = tok_rows // num_blocks
    slot_count = num_blocks * pick_count
    logits = jnp.dot(tokens, w_router, preferred_element_type=jnp.float32)
    gate_values = jax.nn.sigmoid(logits)
    offsets = (jnp.arange(num_blocks, dtype=jnp.int32) * block_rows)[:, None, None]
    slot_rows = jnp.transpose(chosen + offsets, (1, 0, 2)).reshape(expert_count, slot_count)
    picked = tokens[slot_rows]
    slot_gate_values = jnp.take_along_axis(gate_values.T, slot_rows, axis=1)
    cot_rows = cotangent[slot_rows]
    scaled_cot = (slot_gate_values[:, :, None] * cot_rows.astype(jnp.float32)).astype(jnp.bfloat16)
    n = lax.axis_size("dp")
    shard_rows = w_gate.shape[1]
    packed = jnp.concatenate(
        [w_gate[0], w_up[0], w_down[0].reshape(-1, w_gate.shape[2])], axis=0
    )
    full = dp_gather_kernel(packed, n)
    full_gate = full[:, :shard_rows].reshape(1, -1, w_gate.shape[2])
    full_up = full[:, shard_rows : 2 * shard_rows].reshape(1, -1, w_up.shape[2])
    full_down = full[:, 2 * shard_rows :].reshape(1, -1, w_down.shape[2])
    expert_count_axis = lax.axis_size("expert")
    expert_rows = lax.all_to_all(picked, "expert", 0, 0, tiled=True).reshape(1, -1, model_width)
    pre_gate = jnp.einsum(
        "erd,edh->erh", expert_rows, full_gate, preferred_element_type=jnp.float32
    )
    pre_up = jnp.einsum("erd,edh->erh", expert_rows, full_up, preferred_element_type=jnp.float32)
    silu_gate = jax.nn.silu(pre_gate)
    hidden = (silu_gate * pre_up).astype(jnp.bfloat16)
    expert_out = jnp.einsum(
        "erh,ehd->erd", hidden, full_down, preferred_element_type=jnp.float32
    ).astype(jnp.bfloat16)
    returned = lax.all_to_all(
        expert_out.reshape(expert_count_axis, -1, model_width), "expert", 0, 0, tiled=True
    )
    expert_cot = lax.all_to_all(scaled_cot, "expert", 0, 0, tiled=True).reshape(1, -1, model_width)
    back_gate, back_up, back_down = (full_gate, full_up, full_down)
    d_hidden = jnp.einsum("erd,ehd->erh", expert_cot, back_down, preferred_element_type=jnp.float32)
    gate_sigmoid = jax.nn.sigmoid(pre_gate)
    d_pre_gate = (
        d_hidden * pre_up * gate_sigmoid * (1.0 + pre_gate * (1.0 - gate_sigmoid))
    ).astype(jnp.bfloat16)
    d_pre_up = (d_hidden * silu_gate).astype(jnp.bfloat16)
    d_rows = (
        jnp.einsum("erh,edh->erd", d_pre_gate, back_gate, preferred_element_type=jnp.float32)
        + jnp.einsum("erh,edh->erd", d_pre_up, back_up, preferred_element_type=jnp.float32)
    ).astype(jnp.bfloat16)
    row_grads = lax.all_to_all(
        d_rows.reshape(expert_count_axis, -1, model_width), "expert", 0, 0, tiled=True
    )
    position_hits = chosen[:, :, :, None] == jnp.arange(block_rows, dtype=jnp.int32)
    indicator_matrix = position_hits.reshape(num_blocks, expert_count * pick_count, block_rows)
    gate_weighted_rows = to_blocks(slot_gate_values, num_blocks, pick_count)[
        :, :, None
    ] * to_blocks(returned, num_blocks, pick_count).astype(jnp.float32)
    mixed = (
        jnp.einsum(
            "wze,wzi->wei",
            indicator_matrix.astype(jnp.float32),
            gate_weighted_rows,
            precision=lax.Precision.HIGHEST,
        )
        .reshape(tok_rows, model_width)
        .astype(jnp.bfloat16)
    )
    slot_dots = jnp.sum(cot_rows.astype(jnp.float32) * returned.astype(jnp.float32), axis=2)
    dgate = jnp.einsum(
        "bept,ebp->bte",
        position_hits.astype(jnp.float32),
        slot_dots.reshape(expert_count, num_blocks, pick_count),
        precision=lax.Precision.HIGHEST,
    ).reshape(tok_rows, expert_count)
    d_logit = (dgate * gate_values * (1.0 - gate_values)).astype(jnp.bfloat16)
    gathered_grads = jnp.einsum(
        "wze,wzi->wei",
        indicator_matrix.astype(jnp.bfloat16),
        to_blocks(row_grads, num_blocks, pick_count),
        preferred_element_type=jnp.float32,
    ).reshape(tok_rows, model_width)
    grad_tokens = (
        gathered_grads + jnp.dot(d_logit, w_router.T, preferred_element_type=jnp.float32)
    ).astype(jnp.bfloat16)
    router_full = jnp.dot(tokens.T, d_logit, preferred_element_type=jnp.float32)
    devices = n * expert_count_axis
    router_part = jnp.sum(
        lax.all_to_all(router_full.reshape(devices, -1), ("dp", "expert"), 0, 0, tiled=True),
        axis=0,
    )
    grad_gate, grad_up, down_weight_gradient = weight_grads(
        expert_rows, hidden, expert_cot, d_pre_gate, d_pre_up, n
    )
    grad_router = lax.all_to_all(
        jnp.broadcast_to(router_part[None], (devices,) + router_part.shape),
        ("dp", "expert"),
        0,
        0,
        tiled=True,
    ).reshape(router_full.shape)
    return (mixed, grad_tokens, grad_gate, grad_up, down_weight_gradient, grad_router)


def solution(mesh):
    placed = (
        P(("dp", "expert"), None),
        P(("dp", "expert"), None),
        P(("dp", "expert"), None, None),
        P(),
        P("expert", "dp", None),
        P("expert", "dp", None),
        P("expert", "dp", None),
    )
    return jax.shard_map(
        body,
        mesh=mesh,
        in_specs=placed,
        out_specs=(
            P(("dp", "expert"), None),
            P(("dp", "expert"), None),
            P("expert", "dp", None),
            P("expert", "dp", None),
            P("expert", "dp", None),
            P(),
        ),
        check_vma=False,
    )
```

```python
import functools

import jax
import jax.numpy as jnp
from jax import lax
from jax.experimental import pallas as pl
from jax.experimental.pallas import tpu as pltpu
from jax.sharding import PartitionSpec as P

MESH = pl.DeviceIdType.MESH


def _gather_kernel(n, *refs):
    count = (len(refs) - 3) // 2
    srcs, dsts = refs[:count], refs[count : 2 * count]
    send_sem, recv_sem, local_sem = refs[2 * count :]
    me = lax.axis_index("dp")
    ex = lax.axis_index("expert")
    barrier = pltpu.get_barrier_semaphore()
    for k in range(1, n):
        pl.semaphore_signal(barrier, inc=1, device_id=(lax.rem(me + k, n), ex), device_id_type=MESH)
    pl.semaphore_wait(barrier, n - 1)
    copies = []
    for a in range(count):
        rows = srcs[a].shape[0]
        slot = dsts[a].at[pl.ds(me * rows, rows)]
        local = pltpu.make_async_copy(srcs[a], slot, local_sem.at[a])
        local.start()
        copies.append(local)
        for k in range(1, n):
            remote = pltpu.make_async_remote_copy(
                src_ref=srcs[a],
                dst_ref=slot,
                send_sem=send_sem.at[a, k],
                recv_sem=recv_sem.at[a, k],
                device_id=(lax.rem(me + k, n), ex),
                device_id_type=MESH,
            )
            remote.start()
            copies.append(remote)
    for c in copies:
        c.wait()


def dp_all_gather(shards, n):
    count = len(shards)
    return pl.pallas_call(
        functools.partial(_gather_kernel, n),
        out_shape=[jax.ShapeDtypeStruct((n * s.shape[0],) + s.shape[1:], s.dtype) for s in shards],
        in_specs=[pl.BlockSpec(memory_space=pl.ANY)] * count,
        out_specs=[pl.BlockSpec(memory_space=pl.ANY)] * count,
        scratch_shapes=[
            pltpu.SemaphoreType.DMA((count, n)),
            pltpu.SemaphoreType.DMA((count, n)),
            pltpu.SemaphoreType.DMA((count,)),
        ],
        compiler_params=pltpu.CompilerParams(collective_id=0, has_side_effects=True),
    )(*shards)


def _exchange_kernel(n, n_scatter, *refs):
    count = (len(refs) - 3) // 2
    srcs, dsts = refs[:count], refs[count : 2 * count]
    send_sem, recv_sem, local_sem = refs[2 * count :]
    me = lax.axis_index("dp")
    ex = lax.axis_index("expert")
    barrier = pltpu.get_barrier_semaphore()
    for k in range(1, n):
        pl.semaphore_signal(barrier, inc=1, device_id=(lax.rem(me + k, n), ex), device_id_type=MESH)
    pl.semaphore_wait(barrier, n - 1)
    copies = []
    for a in range(count):
        rows = dsts[a].shape[1]
        if a < n_scatter:
            mine = srcs[a].at[pl.ds(me * rows, rows)]
        else:
            mine = srcs[a]
        local = pltpu.make_async_copy(mine, dsts[a].at[me], local_sem.at[a])
        local.start()
        copies.append(local)
        for k in range(1, n):
            peer = lax.rem(me + k, n)
            if a < n_scatter:
                part = srcs[a].at[pl.ds(peer * rows, rows)]
            else:
                part = srcs[a]
            remote = pltpu.make_async_remote_copy(
                src_ref=part,
                dst_ref=dsts[a].at[me],
                send_sem=send_sem.at[a, k],
                recv_sem=recv_sem.at[a, k],
                device_id=(peer, ex),
                device_id_type=MESH,
            )
            remote.start()
            copies.append(remote)
    for c in copies:
        c.wait()


def dp_exchange(partials, replicas, n):
    arrays = list(partials) + list(replicas)
    count = len(arrays)
    shapes = [(n, p.shape[0] // n) + p.shape[1:] for p in partials]
    shapes += [(n,) + r.shape for r in replicas]
    received = pl.pallas_call(
        functools.partial(_exchange_kernel, n, len(partials)),
        out_shape=[jax.ShapeDtypeStruct(s, a.dtype) for s, a in zip(shapes, arrays)],
        in_specs=[pl.BlockSpec(memory_space=pl.ANY)] * count,
        out_specs=[pl.BlockSpec(memory_space=pl.ANY)] * count,
        scratch_shapes=[
            pltpu.SemaphoreType.DMA((count, n)),
            pltpu.SemaphoreType.DMA((count, n)),
            pltpu.SemaphoreType.DMA((count,)),
        ],
        compiler_params=pltpu.CompilerParams(collective_id=1, has_side_effects=True),
    )(*arrays)
    return [jnp.sum(r.astype(jnp.float32), axis=0) for r in received]


def _shift_pairs(n, k):
    return [(i, (i + k) % n) for i in range(n)]


def dp_gather_permute(shard, n):
    me = lax.axis_index("dp")
    full = jnp.zeros((n,) + shard.shape, shard.dtype)
    full = lax.dynamic_update_index_in_dim(full, shard, me, 0)
    for k in range(1, n):
        got = lax.ppermute(shard, "dp", perm=_shift_pairs(n, k))
        full = lax.dynamic_update_index_in_dim(full, got, lax.rem(me + n - k, n), 0)
    return full


def dp_scatter_permute(partial, n):
    me = lax.axis_index("dp")
    blocks = partial.reshape((n, partial.shape[0] // n) + partial.shape[1:])
    total = lax.dynamic_index_in_dim(blocks, me, 0, keepdims=False).astype(jnp.float32)
    for k in range(1, n):
        piece = lax.dynamic_index_in_dim(blocks, lax.rem(me + k, n), 0, keepdims=False)
        got = lax.ppermute(piece, "dp", perm=_shift_pairs(n, k))
        total = total + got.astype(jnp.float32)
    return total


def _x_shift(n, d):
    return [(i, (i + 2 * d) % n) for i in range(n)]


def _y_pair(n):
    return [(i, i ^ 1) for i in range(n)]


def x_ring_gather(t, n):
    from_left = lax.ppermute(t, "dp", _x_shift(n, 1))
    from_right = lax.ppermute(t, "dp", _x_shift(n, -1))
    h = t.shape[0] // 2
    first = lax.ppermute(from_left[:h], "dp", _x_shift(n, 1))
    second = lax.ppermute(from_right[h:], "dp", _x_shift(n, -1))
    return [t, from_right, jnp.concatenate([first, second], axis=0), from_left]


def dp_gather_2d(t, n):
    assert n == 8
    me = lax.axis_index("dp")
    x, l, nx = me // 2, me % 2, n // 2
    partner = lax.ppermute(t, "dp", _y_pair(n))
    stacked = jnp.stack(x_ring_gather(t, n) + x_ring_gather(partner, n))
    p = jnp.arange(n, dtype=jnp.int32)
    order = (p // 2 - x) % nx + nx * (p % 2 != l).astype(jnp.int32)
    return jnp.take(stacked, order, axis=0)


def x_ring_scatter(blocks, n):
    h = blocks[0].shape[0] // 2
    low = lax.ppermute(blocks[2][:h].astype(jnp.bfloat16), "dp", _x_shift(n, 1))
    high = lax.ppermute(blocks[2][h:].astype(jnp.bfloat16), "dp", _x_shift(n, -1))
    to_right = jnp.concatenate([blocks[1][:h] + low.astype(jnp.float32), blocks[1][h:]], axis=0)
    to_left = jnp.concatenate([blocks[3][:h], blocks[3][h:] + high.astype(jnp.float32)], axis=0)
    from_left = lax.ppermute(to_right.astype(jnp.bfloat16), "dp", _x_shift(n, 1))
    from_right = lax.ppermute(to_left.astype(jnp.bfloat16), "dp", _x_shift(n, -1))
    return blocks[0] + from_left.astype(jnp.float32) + from_right.astype(jnp.float32)


def dp_scatter_2d(partial, n):
    assert n == 8
    me = lax.axis_index("dp")
    x, l, nx = me // 2, me % 2, n // 2
    blocks = partial.reshape((n, partial.shape[0] // n) + partial.shape[1:])

    def pick(m, side):
        index = 2 * ((x + m) % nx) + side
        return lax.dynamic_index_in_dim(blocks, index, 0, keepdims=False).astype(jnp.float32)

    partner_sum = x_ring_scatter([pick(m, 1 - l) for m in range(nx)], n)
    sent = lax.ppermute(partner_sum.astype(jnp.bfloat16), "dp", _y_pair(n))
    own_sum = x_ring_scatter([pick(m, l) for m in range(nx)], n)
    return own_sum + sent.astype(jnp.float32)


def _ring_gather_kernel(n, shard_ref, out_ref, send_sem, recv_sem, local_sem):
    me = lax.axis_index("dp")
    ex = lax.axis_index("expert")
    right, left, partner = lax.rem(me + 2, n), lax.rem(me + n - 2, n), me + 1 - 2 * lax.rem(me, 2)
    barrier = pltpu.get_barrier_semaphore()
    for peer in (right, left, partner):
        pl.semaphore_signal(barrier, inc=1, device_id=(peer, ex), device_id_type=MESH)
    pl.semaphore_wait(barrier, 3)
    half = shard_ref.shape[0] // 2

    def send(role, src, slot, rows, peer):
        copy = pltpu.make_async_remote_copy(
            src_ref=src,
            dst_ref=out_ref.at[slot, rows],
            send_sem=send_sem.at[role],
            recv_sem=recv_sem.at[role],
            device_id=(peer, ex),
            device_id_type=MESH,
        )
        copy.start()
        return copy

    whole, low, high = pl.ds(0, 2 * half), pl.ds(0, half), pl.ds(half, half)
    local = pltpu.make_async_copy(shard_ref, out_ref.at[me], local_sem.at[0])
    local.start()
    first = [
        send(0, shard_ref, me, whole, right),
        send(1, shard_ref, me, whole, left),
        send(2, shard_ref, me, whole, partner),
    ]
    for copy in first:
        copy.wait_recv()
    mate = partner
    second = [
        send(3, out_ref.at[left, low], left, low, right),
        send(4, out_ref.at[right, high], right, high, left),
        send(5, out_ref.at[mate], mate, whole, right),
        send(6, out_ref.at[mate], mate, whole, left),
    ]
    second[2].wait_recv()
    second[3].wait_recv()
    mate_left, mate_right = lax.rem(mate + n - 2, n), lax.rem(mate + 2, n)
    third = [
        send(7, out_ref.at[mate_left, low], mate_left, low, right),
        send(8, out_ref.at[mate_right, high], mate_right, high, left),
    ]
    for copy in first:
        copy.wait_send()
    for copy in second[:2]:
        copy.wait_recv()
    for copy in second:
        copy.wait_send()
    for copy in third:
        copy.wait_recv()
        copy.wait_send()
    local.wait()


def dp_gather_kernel(shard, n):
    assert n == 8
    return pl.pallas_call(
        functools.partial(_ring_gather_kernel, n),
        out_shape=jax.ShapeDtypeStruct((n,) + shard.shape, shard.dtype),
        in_specs=[pl.BlockSpec(memory_space=pl.ANY)],
        out_specs=pl.BlockSpec(memory_space=pl.ANY),
        scratch_shapes=[
            pltpu.SemaphoreType.DMA((9,)),
            pltpu.SemaphoreType.DMA((9,)),
            pltpu.SemaphoreType.DMA((1,)),
        ],
        compiler_params=pltpu.CompilerParams(collective_id=2, has_side_effects=True),
    )(shard)


def to_blocks(slot_array, num_blocks, pick_count):
    expert_count = slot_array.shape[0]
    trailing = slot_array.shape[2:]
    grouped = slot_array.reshape((expert_count, num_blocks, pick_count) + trailing)
    axis_order = (1, 0, 2) + tuple(range(3, 3 + len(trailing)))
    return jnp.transpose(grouped, axis_order).reshape(
        (num_blocks, expert_count * pick_count) + trailing
    )


def weight_grads(expert_rows, hidden, expert_cot, d_pre_gate, d_pre_up, n):
    hidden_activations = hidden.shape[2]
    out_part = jnp.einsum(
        "erc,erd->cd", hidden, expert_cot, preferred_element_type=jnp.float32
    ).astype(jnp.bfloat16)
    out_share = dp_scatter_2d(out_part, n)
    both_grads = jnp.concatenate([d_pre_gate, d_pre_up], axis=2)
    in_part = jnp.einsum(
        "erc,erk->ck", expert_rows, both_grads, preferred_element_type=jnp.float32
    ).astype(jnp.bfloat16)
    in_share = dp_scatter_2d(in_part, n)
    grad_gate = in_share[None, :, :hidden_activations]
    grad_up = in_share[None, :, hidden_activations:]
    down_weight_gradient = out_share[None]
    return (grad_gate, grad_up, down_weight_gradient)


def body(tokens, cotangent, chosen, w_router, w_gate, w_up, w_down):
    tok_rows, model_width = tokens.shape
    num_blocks, expert_count, pick_count = chosen.shape
    block_rows = tok_rows // num_blocks
    slot_count = num_blocks * pick_count
    logits = jnp.dot(tokens, w_router, preferred_element_type=jnp.float32)
    gate_values = jax.nn.sigmoid(logits)
    offsets = (jnp.arange(num_blocks, dtype=jnp.int32) * block_rows)[:, None, None]
    slot_rows = jnp.transpose(chosen + offsets, (1, 0, 2)).reshape(expert_count, slot_count)
    picked = tokens[slot_rows]
    slot_gate_values = jnp.take_along_axis(gate_values.T, slot_rows, axis=1)
    cot_rows = cotangent[slot_rows]
    scaled_cot = (slot_gate_values[:, :, None] * cot_rows.astype(jnp.float32)).astype(jnp.bfloat16)
    n = lax.axis_size("dp")
    shard_rows = w_gate.shape[1]
    packed = jnp.concatenate(
        [w_gate[0], w_up[0], w_down[0].reshape(-1, w_gate.shape[2])], axis=0
    )
    full = dp_gather_kernel(packed, n)
    full_gate = full[:, :shard_rows].reshape(1, -1, w_gate.shape[2])
    full_up = full[:, shard_rows : 2 * shard_rows].reshape(1, -1, w_up.shape[2])
    full_down = full[:, 2 * shard_rows :].reshape(1, -1, w_down.shape[2])
    expert_count_axis = lax.axis_size("expert")
    expert_rows = lax.all_to_all(picked, "expert", 0, 0, tiled=True).reshape(1, -1, model_width)
    pre_gate = jnp.einsum(
        "erd,edh->erh", expert_rows, full_gate, preferred_element_type=jnp.float32
    )
    pre_up = jnp.einsum("erd,edh->erh", expert_rows, full_up, preferred_element_type=jnp.float32)
    silu_gate = jax.nn.silu(pre_gate)
    hidden = (silu_gate * pre_up).astype(jnp.bfloat16)
    expert_out = jnp.einsum(
        "erh,ehd->erd", hidden, full_down, preferred_element_type=jnp.float32
    ).astype(jnp.bfloat16)
    returned = lax.all_to_all(
        expert_out.reshape(expert_count_axis, -1, model_width), "expert", 0, 0, tiled=True
    )
    expert_cot = lax.all_to_all(scaled_cot, "expert", 0, 0, tiled=True).reshape(1, -1, model_width)
    back_gate, back_up, back_down = (full_gate, full_up, full_down)
    d_hidden = jnp.einsum("erd,ehd->erh", expert_cot, back_down, preferred_element_type=jnp.float32)
    gate_sigmoid = jax.nn.sigmoid(pre_gate)
    d_pre_gate = (
        d_hidden * pre_up * gate_sigmoid * (1.0 + pre_gate * (1.0 - gate_sigmoid))
    ).astype(jnp.bfloat16)
    d_pre_up = (d_hidden * silu_gate).astype(jnp.bfloat16)
    d_rows = (
        jnp.einsum("erh,edh->erd", d_pre_gate, back_gate, preferred_element_type=jnp.float32)
        + jnp.einsum("erh,edh->erd", d_pre_up, back_up, preferred_element_type=jnp.float32)
    ).astype(jnp.bfloat16)
    position_hits = chosen[:, :, :, None] == jnp.arange(block_rows, dtype=jnp.int32)
    indicator_matrix = position_hits.reshape(num_blocks, expert_count * pick_count, block_rows)
    gate_weighted_rows = to_blocks(slot_gate_values, num_blocks, pick_count)[
        :, :, None
    ] * to_blocks(returned, num_blocks, pick_count).astype(jnp.float32)
    mixed = (
        jnp.einsum(
            "wze,wzi->wei",
            indicator_matrix.astype(jnp.float32),
            gate_weighted_rows,
            precision=lax.Precision.HIGHEST,
        )
        .reshape(tok_rows, model_width)
        .astype(jnp.bfloat16)
    )
    slot_dots = jnp.sum(cot_rows.astype(jnp.float32) * returned.astype(jnp.float32), axis=2)
    dgate = jnp.einsum(
        "bept,ebp->bte",
        position_hits.astype(jnp.float32),
        slot_dots.reshape(expert_count, num_blocks, pick_count),
        precision=lax.Precision.HIGHEST,
    ).reshape(tok_rows, expert_count)
    d_logit = (dgate * gate_values * (1.0 - gate_values)).astype(jnp.bfloat16)
    router_full = jnp.dot(tokens.T, d_logit, preferred_element_type=jnp.float32)
    devices = n * expert_count_axis
    router_part = jnp.sum(
        lax.all_to_all(router_full.reshape(devices, -1), ("dp", "expert"), 0, 0, tiled=True),
        axis=0,
    )
    router_part, d_rows = lax.optimization_barrier((router_part, d_rows))
    row_grads = lax.all_to_all(
        d_rows.reshape(expert_count_axis, -1, model_width), "expert", 0, 0, tiled=True
    )
    gathered_grads = jnp.einsum(
        "wze,wzi->wei",
        indicator_matrix.astype(jnp.bfloat16),
        to_blocks(row_grads, num_blocks, pick_count),
        preferred_element_type=jnp.float32,
    ).reshape(tok_rows, model_width)
    grad_tokens = (
        gathered_grads + jnp.dot(d_logit, w_router.T, preferred_element_type=jnp.float32)
    ).astype(jnp.bfloat16)
    grad_gate, grad_up, down_weight_gradient = weight_grads(
        expert_rows, hidden, expert_cot, d_pre_gate, d_pre_up, n
    )
    grad_router = lax.all_to_all(
        jnp.broadcast_to(router_part[None], (devices,) + router_part.shape),
        ("dp", "expert"),
        0,
        0,
        tiled=True,
    ).reshape(router_full.shape)
    return (mixed, grad_tokens, grad_gate, grad_up, down_weight_gradient, grad_router)


def solution(mesh):
    placed = (
        P(("dp", "expert"), None),
        P(("dp", "expert"), None),
        P(("dp", "expert"), None, None),
        P(),
        P("expert", "dp", None),
        P("expert", "dp", None),
        P("expert", "dp", None),
    )
    return jax.shard_map(
        body,
        mesh=mesh,
        in_specs=placed,
        out_specs=(
            P(("dp", "expert"), None),
            P(("dp", "expert"), None),
            P("expert", "dp", None),
            P("expert", "dp", None),
            P("expert", "dp", None),
            P(),
        ),
        check_vma=False,
    )
```

```python
import functools

import jax
import jax.numpy as jnp
from jax import lax
from jax.experimental import pallas as pl
from jax.experimental.pallas import tpu as pltpu
from jax.sharding import PartitionSpec as P

MESH = pl.DeviceIdType.MESH


def _gather_kernel(n, *refs):
    count = (len(refs) - 3) // 2
    srcs, dsts = refs[:count], refs[count : 2 * count]
    send_sem, recv_sem, local_sem = refs[2 * count :]
    me = lax.axis_index("dp")
    ex = lax.axis_index("expert")
    barrier = pltpu.get_barrier_semaphore()
    for k in range(1, n):
        pl.semaphore_signal(barrier, inc=1, device_id=(lax.rem(me + k, n), ex), device_id_type=MESH)
    pl.semaphore_wait(barrier, n - 1)
    copies = []
    for a in range(count):
        rows = srcs[a].shape[0]
        slot = dsts[a].at[pl.ds(me * rows, rows)]
        local = pltpu.make_async_copy(srcs[a], slot, local_sem.at[a])
        local.start()
        copies.append(local)
        for k in range(1, n):
            remote = pltpu.make_async_remote_copy(
                src_ref=srcs[a],
                dst_ref=slot,
                send_sem=send_sem.at[a, k],
                recv_sem=recv_sem.at[a, k],
                device_id=(lax.rem(me + k, n), ex),
                device_id_type=MESH,
            )
            remote.start()
            copies.append(remote)
    for c in copies:
        c.wait()


def dp_all_gather(shards, n):
    count = len(shards)
    return pl.pallas_call(
        functools.partial(_gather_kernel, n),
        out_shape=[jax.ShapeDtypeStruct((n * s.shape[0],) + s.shape[1:], s.dtype) for s in shards],
        in_specs=[pl.BlockSpec(memory_space=pl.ANY)] * count,
        out_specs=[pl.BlockSpec(memory_space=pl.ANY)] * count,
        scratch_shapes=[
            pltpu.SemaphoreType.DMA((count, n)),
            pltpu.SemaphoreType.DMA((count, n)),
            pltpu.SemaphoreType.DMA((count,)),
        ],
        compiler_params=pltpu.CompilerParams(collective_id=0, has_side_effects=True),
    )(*shards)


def _exchange_kernel(n, n_scatter, *refs):
    count = (len(refs) - 3) // 2
    srcs, dsts = refs[:count], refs[count : 2 * count]
    send_sem, recv_sem, local_sem = refs[2 * count :]
    me = lax.axis_index("dp")
    ex = lax.axis_index("expert")
    barrier = pltpu.get_barrier_semaphore()
    for k in range(1, n):
        pl.semaphore_signal(barrier, inc=1, device_id=(lax.rem(me + k, n), ex), device_id_type=MESH)
    pl.semaphore_wait(barrier, n - 1)
    copies = []
    for a in range(count):
        rows = dsts[a].shape[1]
        if a < n_scatter:
            mine = srcs[a].at[pl.ds(me * rows, rows)]
        else:
            mine = srcs[a]
        local = pltpu.make_async_copy(mine, dsts[a].at[me], local_sem.at[a])
        local.start()
        copies.append(local)
        for k in range(1, n):
            peer = lax.rem(me + k, n)
            if a < n_scatter:
                part = srcs[a].at[pl.ds(peer * rows, rows)]
            else:
                part = srcs[a]
            remote = pltpu.make_async_remote_copy(
                src_ref=part,
                dst_ref=dsts[a].at[me],
                send_sem=send_sem.at[a, k],
                recv_sem=recv_sem.at[a, k],
                device_id=(peer, ex),
                device_id_type=MESH,
            )
            remote.start()
            copies.append(remote)
    for c in copies:
        c.wait()


def dp_exchange(partials, replicas, n):
    arrays = list(partials) + list(replicas)
    count = len(arrays)
    shapes = [(n, p.shape[0] // n) + p.shape[1:] for p in partials]
    shapes += [(n,) + r.shape for r in replicas]
    received = pl.pallas_call(
        functools.partial(_exchange_kernel, n, len(partials)),
        out_shape=[jax.ShapeDtypeStruct(s, a.dtype) for s, a in zip(shapes, arrays)],
        in_specs=[pl.BlockSpec(memory_space=pl.ANY)] * count,
        out_specs=[pl.BlockSpec(memory_space=pl.ANY)] * count,
        scratch_shapes=[
            pltpu.SemaphoreType.DMA((count, n)),
            pltpu.SemaphoreType.DMA((count, n)),
            pltpu.SemaphoreType.DMA((count,)),
        ],
        compiler_params=pltpu.CompilerParams(collective_id=1, has_side_effects=True),
    )(*arrays)
    return [jnp.sum(r.astype(jnp.float32), axis=0) for r in received]


def _shift_pairs(n, k):
    return [(i, (i + k) % n) for i in range(n)]


def dp_gather_permute(shard, n):
    me = lax.axis_index("dp")
    full = jnp.zeros((n,) + shard.shape, shard.dtype)
    full = lax.dynamic_update_index_in_dim(full, shard, me, 0)
    for k in range(1, n):
        got = lax.ppermute(shard, "dp", perm=_shift_pairs(n, k))
        full = lax.dynamic_update_index_in_dim(full, got, lax.rem(me + n - k, n), 0)
    return full


def dp_scatter_permute(partial, n):
    me = lax.axis_index("dp")
    blocks = partial.reshape((n, partial.shape[0] // n) + partial.shape[1:])
    total = lax.dynamic_index_in_dim(blocks, me, 0, keepdims=False).astype(jnp.float32)
    for k in range(1, n):
        piece = lax.dynamic_index_in_dim(blocks, lax.rem(me + k, n), 0, keepdims=False)
        got = lax.ppermute(piece, "dp", perm=_shift_pairs(n, k))
        total = total + got.astype(jnp.float32)
    return total


def _x_shift(n, d):
    return [(i, (i + 2 * d) % n) for i in range(n)]


def _y_pair(n):
    return [(i, i ^ 1) for i in range(n)]


def x_ring_gather(t, n):
    from_left = lax.ppermute(t, "dp", _x_shift(n, 1))
    from_right = lax.ppermute(t, "dp", _x_shift(n, -1))
    h = t.shape[0] // 2
    first = lax.ppermute(from_left[:h], "dp", _x_shift(n, 1))
    second = lax.ppermute(from_right[h:], "dp", _x_shift(n, -1))
    return [t, from_right, jnp.concatenate([first, second], axis=0), from_left]


def dp_gather_2d(t, n):
    assert n == 8
    me = lax.axis_index("dp")
    x, l, nx = me // 2, me % 2, n // 2
    partner = lax.ppermute(t, "dp", _y_pair(n))
    stacked = jnp.stack(x_ring_gather(t, n) + x_ring_gather(partner, n))
    p = jnp.arange(n, dtype=jnp.int32)
    order = (p // 2 - x) % nx + nx * (p % 2 != l).astype(jnp.int32)
    return jnp.take(stacked, order, axis=0)


def x_ring_scatter(blocks, n):
    h = blocks[0].shape[0] // 2
    low = lax.ppermute(blocks[2][:h].astype(jnp.bfloat16), "dp", _x_shift(n, 1))
    high = lax.ppermute(blocks[2][h:].astype(jnp.bfloat16), "dp", _x_shift(n, -1))
    to_right = jnp.concatenate([blocks[1][:h] + low.astype(jnp.float32), blocks[1][h:]], axis=0)
    to_left = jnp.concatenate([blocks[3][:h], blocks[3][h:] + high.astype(jnp.float32)], axis=0)
    from_left = lax.ppermute(to_right.astype(jnp.bfloat16), "dp", _x_shift(n, 1))
    from_right = lax.ppermute(to_left.astype(jnp.bfloat16), "dp", _x_shift(n, -1))
    return blocks[0] + from_left.astype(jnp.float32) + from_right.astype(jnp.float32)


def dp_scatter_2d(partial, n):
    assert n == 8
    me = lax.axis_index("dp")
    x, l, nx = me // 2, me % 2, n // 2
    blocks = partial.reshape((n, partial.shape[0] // n) + partial.shape[1:])

    def pick(m, side):
        index = 2 * ((x + m) % nx) + side
        return lax.dynamic_index_in_dim(blocks, index, 0, keepdims=False).astype(jnp.float32)

    partner_sum = x_ring_scatter([pick(m, 1 - l) for m in range(nx)], n)
    sent = lax.ppermute(partner_sum.astype(jnp.bfloat16), "dp", _y_pair(n))
    own_sum = x_ring_scatter([pick(m, l) for m in range(nx)], n)
    return own_sum + sent.astype(jnp.float32)


def _ring_gather_kernel(n, *refs):
    count = (len(refs) - 3) // 2
    shards, outs = refs[:count], refs[count : 2 * count]
    send_sem, recv_sem, local_sem = refs[2 * count :]
    me = lax.axis_index("dp")
    ex = lax.axis_index("expert")
    right, left, partner = lax.rem(me + 2, n), lax.rem(me + n - 2, n), me + 1 - 2 * lax.rem(me, 2)
    barrier = pltpu.get_barrier_semaphore()
    for peer in (right, left, partner):
        pl.semaphore_signal(barrier, inc=1, device_id=(peer, ex), device_id_type=MESH)
    pl.semaphore_wait(barrier, 3)

    def send(a, role, src, slot, rows, peer):
        copy = pltpu.make_async_remote_copy(
            src_ref=src,
            dst_ref=outs[a].at[slot, rows],
            send_sem=send_sem.at[a, role],
            recv_sem=recv_sem.at[a, role],
            device_id=(peer, ex),
            device_id_type=MESH,
        )
        copy.start()
        return copy

    spans = []
    for a in range(count):
        half = shards[a].shape[0] // 2
        spans.append((pl.ds(0, 2 * half), pl.ds(0, half), pl.ds(half, half)))
    locals_, first, second, third = [], [], [], []
    for a in range(count):
        local = pltpu.make_async_copy(shards[a], outs[a].at[me], local_sem.at[a])
        local.start()
        locals_.append(local)
        whole = spans[a][0]
        first += [
            send(a, 0, shards[a], me, whole, right),
            send(a, 1, shards[a], me, whole, left),
            send(a, 2, shards[a], me, whole, partner),
        ]
    for copy in first:
        copy.wait_recv()
    mate = partner
    for a in range(count):
        whole, low, high = spans[a]
        second += [
            send(a, 3, outs[a].at[left, low], left, low, right),
            send(a, 4, outs[a].at[right, high], right, high, left),
            send(a, 5, outs[a].at[mate], mate, whole, right),
            send(a, 6, outs[a].at[mate], mate, whole, left),
        ]
    for a in range(count):
        second[4 * a + 2].wait_recv()
        second[4 * a + 3].wait_recv()
    mate_left, mate_right = lax.rem(mate + n - 2, n), lax.rem(mate + 2, n)
    for a in range(count):
        whole, low, high = spans[a]
        third += [
            send(a, 7, outs[a].at[mate_left, low], mate_left, low, right),
            send(a, 8, outs[a].at[mate_right, high], mate_right, high, left),
        ]
    for copy in first:
        copy.wait_send()
    for a in range(count):
        second[4 * a].wait_recv()
        second[4 * a + 1].wait_recv()
    for copy in second:
        copy.wait_send()
    for copy in third:
        copy.wait_recv()
        copy.wait_send()
    for local in locals_:
        local.wait()


def dp_gather_kernel(shards, n):
    assert n == 8
    count = len(shards)
    return pl.pallas_call(
        functools.partial(_ring_gather_kernel, n),
        out_shape=[jax.ShapeDtypeStruct((n,) + s.shape, s.dtype) for s in shards],
        in_specs=[pl.BlockSpec(memory_space=pl.ANY)] * count,
        out_specs=[pl.BlockSpec(memory_space=pl.ANY)] * count,
        scratch_shapes=[
            pltpu.SemaphoreType.DMA((count, 9)),
            pltpu.SemaphoreType.DMA((count, 9)),
            pltpu.SemaphoreType.DMA((count,)),
        ],
        compiler_params=pltpu.CompilerParams(collective_id=2, has_side_effects=True),
    )(*shards)


def to_blocks(slot_array, num_blocks, pick_count):
    expert_count = slot_array.shape[0]
    trailing = slot_array.shape[2:]
    grouped = slot_array.reshape((expert_count, num_blocks, pick_count) + trailing)
    axis_order = (1, 0, 2) + tuple(range(3, 3 + len(trailing)))
    return jnp.transpose(grouped, axis_order).reshape(
        (num_blocks, expert_count * pick_count) + trailing
    )


def weight_grads(expert_rows, hidden, expert_cot, d_pre_gate, d_pre_up, n):
    hidden_activations = hidden.shape[2]
    out_part = jnp.einsum(
        "erc,erd->cd", hidden, expert_cot, preferred_element_type=jnp.float32
    ).astype(jnp.bfloat16)
    out_share = dp_scatter_2d(out_part, n)
    both_grads = jnp.concatenate([d_pre_gate, d_pre_up], axis=2)
    in_part = jnp.einsum(
        "erc,erk->ck", expert_rows, both_grads, preferred_element_type=jnp.float32
    ).astype(jnp.bfloat16)
    in_share = dp_scatter_2d(in_part, n)
    grad_gate = in_share[None, :, :hidden_activations]
    grad_up = in_share[None, :, hidden_activations:]
    down_weight_gradient = out_share[None]
    return (grad_gate, grad_up, down_weight_gradient)


def body(tokens, cotangent, chosen, w_router, w_gate, w_up, w_down):
    tok_rows, model_width = tokens.shape
    num_blocks, expert_count, pick_count = chosen.shape
    block_rows = tok_rows // num_blocks
    slot_count = num_blocks * pick_count
    logits = jnp.dot(tokens, w_router, preferred_element_type=jnp.float32)
    gate_values = jax.nn.sigmoid(logits)
    offsets = (jnp.arange(num_blocks, dtype=jnp.int32) * block_rows)[:, None, None]
    slot_rows = jnp.transpose(chosen + offsets, (1, 0, 2)).reshape(expert_count, slot_count)
    picked = tokens[slot_rows]
    slot_gate_values = jnp.take_along_axis(gate_values.T, slot_rows, axis=1)
    cot_rows = cotangent[slot_rows]
    scaled_cot = (slot_gate_values[:, :, None] * cot_rows.astype(jnp.float32)).astype(jnp.bfloat16)
    n = lax.axis_size("dp")
    full_gate, full_up, full_down = (
        g.reshape((1, -1) + g.shape[2:])
        for g in dp_gather_kernel([w_gate[0], w_up[0], w_down[0]], n)
    )
    expert_count_axis = lax.axis_size("expert")
    expert_rows = lax.all_to_all(picked, "expert", 0, 0, tiled=True).reshape(1, -1, model_width)
    pre_gate = jnp.einsum(
        "erd,edh->erh", expert_rows, full_gate, preferred_element_type=jnp.float32
    )
    pre_up = jnp.einsum("erd,edh->erh", expert_rows, full_up, preferred_element_type=jnp.float32)
    silu_gate = jax.nn.silu(pre_gate)
    hidden = (silu_gate * pre_up).astype(jnp.bfloat16)
    expert_out = jnp.einsum(
        "erh,ehd->erd", hidden, full_down, preferred_element_type=jnp.float32
    ).astype(jnp.bfloat16)
    returned = lax.all_to_all(
        expert_out.reshape(expert_count_axis, -1, model_width), "expert", 0, 0, tiled=True
    )
    expert_cot = lax.all_to_all(scaled_cot, "expert", 0, 0, tiled=True).reshape(1, -1, model_width)
    back_gate, back_up, back_down = (full_gate, full_up, full_down)
    d_hidden = jnp.einsum("erd,ehd->erh", expert_cot, back_down, preferred_element_type=jnp.float32)
    gate_sigmoid = jax.nn.sigmoid(pre_gate)
    d_pre_gate = (
        d_hidden * pre_up * gate_sigmoid * (1.0 + pre_gate * (1.0 - gate_sigmoid))
    ).astype(jnp.bfloat16)
    d_pre_up = (d_hidden * silu_gate).astype(jnp.bfloat16)
    d_rows = (
        jnp.einsum("erh,edh->erd", d_pre_gate, back_gate, preferred_element_type=jnp.float32)
        + jnp.einsum("erh,edh->erd", d_pre_up, back_up, preferred_element_type=jnp.float32)
    ).astype(jnp.bfloat16)
    row_grads = lax.all_to_all(
        d_rows.reshape(expert_count_axis, -1, model_width), "expert", 0, 0, tiled=True
    )
    position_hits = chosen[:, :, :, None] == jnp.arange(block_rows, dtype=jnp.int32)
    indicator_matrix = position_hits.reshape(num_blocks, expert_count * pick_count, block_rows)
    gate_weighted_rows = to_blocks(slot_gate_values, num_blocks, pick_count)[
        :, :, None
    ] * to_blocks(returned, num_blocks, pick_count).astype(jnp.float32)
    mixed = (
        jnp.einsum(
            "wze,wzi->wei",
            indicator_matrix.astype(jnp.float32),
            gate_weighted_rows,
            precision=lax.Precision.HIGHEST,
        )
        .reshape(tok_rows, model_width)
        .astype(jnp.bfloat16)
    )
    slot_dots = jnp.sum(cot_rows.astype(jnp.float32) * returned.astype(jnp.float32), axis=2)
    dgate = jnp.einsum(
        "bept,ebp->bte",
        position_hits.astype(jnp.float32),
        slot_dots.reshape(expert_count, num_blocks, pick_count),
        precision=lax.Precision.HIGHEST,
    ).reshape(tok_rows, expert_count)
    d_logit = (dgate * gate_values * (1.0 - gate_values)).astype(jnp.bfloat16)
    gathered_grads = jnp.einsum(
        "wze,wzi->wei",
        indicator_matrix.astype(jnp.bfloat16),
        to_blocks(row_grads, num_blocks, pick_count),
        preferred_element_type=jnp.float32,
    ).reshape(tok_rows, model_width)
    grad_tokens = (
        gathered_grads + jnp.dot(d_logit, w_router.T, preferred_element_type=jnp.float32)
    ).astype(jnp.bfloat16)
    router_full = jnp.dot(tokens.T, d_logit, preferred_element_type=jnp.float32)
    devices = n * expert_count_axis
    router_part = jnp.sum(
        lax.all_to_all(router_full.reshape(devices, -1), ("dp", "expert"), 0, 0, tiled=True),
        axis=0,
    )
    grad_gate, grad_up, down_weight_gradient = weight_grads(
        expert_rows, hidden, expert_cot, d_pre_gate, d_pre_up, n
    )
    grad_router = lax.all_to_all(
        jnp.broadcast_to(router_part[None], (devices,) + router_part.shape),
        ("dp", "expert"),
        0,
        0,
        tiled=True,
    ).reshape(router_full.shape)
    return (mixed, grad_tokens, grad_gate, grad_up, down_weight_gradient, grad_router)


def solution(mesh):
    placed = (
        P(("dp", "expert"), None),
        P(("dp", "expert"), None),
        P(("dp", "expert"), None, None),
        P(),
        P("expert", "dp", None),
        P("expert", "dp", None),
        P("expert", "dp", None),
    )
    return jax.shard_map(
        body,
        mesh=mesh,
        in_specs=placed,
        out_specs=(
            P(("dp", "expert"), None),
            P(("dp", "expert"), None),
            P("expert", "dp", None),
            P("expert", "dp", None),
            P("expert", "dp", None),
            P(),
        ),
        check_vma=False,
    )
```

```python
import functools

import jax
import jax.numpy as jnp
from jax import lax
from jax.experimental import pallas as pl
from jax.experimental.pallas import tpu as pltpu
from jax.sharding import PartitionSpec as P

MESH = pl.DeviceIdType.MESH


def _gather_kernel(n, *refs):
    count = (len(refs) - 3) // 2
    srcs, dsts = refs[:count], refs[count : 2 * count]
    send_sem, recv_sem, local_sem = refs[2 * count :]
    me = lax.axis_index("dp")
    ex = lax.axis_index("expert")
    barrier = pltpu.get_barrier_semaphore()
    for k in range(1, n):
        pl.semaphore_signal(barrier, inc=1, device_id=(lax.rem(me + k, n), ex), device_id_type=MESH)
    pl.semaphore_wait(barrier, n - 1)
    copies = []
    for a in range(count):
        rows = srcs[a].shape[0]
        slot = dsts[a].at[pl.ds(me * rows, rows)]
        local = pltpu.make_async_copy(srcs[a], slot, local_sem.at[a])
        local.start()
        copies.append(local)
        for k in range(1, n):
            remote = pltpu.make_async_remote_copy(
                src_ref=srcs[a],
                dst_ref=slot,
                send_sem=send_sem.at[a, k],
                recv_sem=recv_sem.at[a, k],
                device_id=(lax.rem(me + k, n), ex),
                device_id_type=MESH,
            )
            remote.start()
            copies.append(remote)
    for c in copies:
        c.wait()


def dp_all_gather(shards, n):
    count = len(shards)
    return pl.pallas_call(
        functools.partial(_gather_kernel, n),
        out_shape=[jax.ShapeDtypeStruct((n * s.shape[0],) + s.shape[1:], s.dtype) for s in shards],
        in_specs=[pl.BlockSpec(memory_space=pl.ANY)] * count,
        out_specs=[pl.BlockSpec(memory_space=pl.ANY)] * count,
        scratch_shapes=[
            pltpu.SemaphoreType.DMA((count, n)),
            pltpu.SemaphoreType.DMA((count, n)),
            pltpu.SemaphoreType.DMA((count,)),
        ],
        compiler_params=pltpu.CompilerParams(collective_id=0, has_side_effects=True),
    )(*shards)


def _exchange_kernel(n, n_scatter, *refs):
    count = (len(refs) - 3) // 2
    srcs, dsts = refs[:count], refs[count : 2 * count]
    send_sem, recv_sem, local_sem = refs[2 * count :]
    me = lax.axis_index("dp")
    ex = lax.axis_index("expert")
    barrier = pltpu.get_barrier_semaphore()
    for k in range(1, n):
        pl.semaphore_signal(barrier, inc=1, device_id=(lax.rem(me + k, n), ex), device_id_type=MESH)
    pl.semaphore_wait(barrier, n - 1)
    copies = []
    for a in range(count):
        rows = dsts[a].shape[1]
        if a < n_scatter:
            mine = srcs[a].at[pl.ds(me * rows, rows)]
        else:
            mine = srcs[a]
        local = pltpu.make_async_copy(mine, dsts[a].at[me], local_sem.at[a])
        local.start()
        copies.append(local)
        for k in range(1, n):
            peer = lax.rem(me + k, n)
            if a < n_scatter:
                part = srcs[a].at[pl.ds(peer * rows, rows)]
            else:
                part = srcs[a]
            remote = pltpu.make_async_remote_copy(
                src_ref=part,
                dst_ref=dsts[a].at[me],
                send_sem=send_sem.at[a, k],
                recv_sem=recv_sem.at[a, k],
                device_id=(peer, ex),
                device_id_type=MESH,
            )
            remote.start()
            copies.append(remote)
    for c in copies:
        c.wait()


def dp_exchange(partials, replicas, n):
    arrays = list(partials) + list(replicas)
    count = len(arrays)
    shapes = [(n, p.shape[0] // n) + p.shape[1:] for p in partials]
    shapes += [(n,) + r.shape for r in replicas]
    received = pl.pallas_call(
        functools.partial(_exchange_kernel, n, len(partials)),
        out_shape=[jax.ShapeDtypeStruct(s, a.dtype) for s, a in zip(shapes, arrays)],
        in_specs=[pl.BlockSpec(memory_space=pl.ANY)] * count,
        out_specs=[pl.BlockSpec(memory_space=pl.ANY)] * count,
        scratch_shapes=[
            pltpu.SemaphoreType.DMA((count, n)),
            pltpu.SemaphoreType.DMA((count, n)),
            pltpu.SemaphoreType.DMA((count,)),
        ],
        compiler_params=pltpu.CompilerParams(collective_id=1, has_side_effects=True),
    )(*arrays)
    return [jnp.sum(r.astype(jnp.float32), axis=0) for r in received]


def _shift_pairs(n, k):
    return [(i, (i + k) % n) for i in range(n)]


def dp_gather_permute(shard, n):
    me = lax.axis_index("dp")
    full = jnp.zeros((n,) + shard.shape, shard.dtype)
    full = lax.dynamic_update_index_in_dim(full, shard, me, 0)
    for k in range(1, n):
        got = lax.ppermute(shard, "dp", perm=_shift_pairs(n, k))
        full = lax.dynamic_update_index_in_dim(full, got, lax.rem(me + n - k, n), 0)
    return full


def dp_scatter_permute(partial, n):
    me = lax.axis_index("dp")
    blocks = partial.reshape((n, partial.shape[0] // n) + partial.shape[1:])
    total = lax.dynamic_index_in_dim(blocks, me, 0, keepdims=False).astype(jnp.float32)
    for k in range(1, n):
        piece = lax.dynamic_index_in_dim(blocks, lax.rem(me + k, n), 0, keepdims=False)
        got = lax.ppermute(piece, "dp", perm=_shift_pairs(n, k))
        total = total + got.astype(jnp.float32)
    return total


def _x_shift(n, d):
    return [(i, (i + 2 * d) % n) for i in range(n)]


def _y_pair(n):
    return [(i, i ^ 1) for i in range(n)]


def x_ring_gather(t, n):
    from_left = lax.ppermute(t, "dp", _x_shift(n, 1))
    from_right = lax.ppermute(t, "dp", _x_shift(n, -1))
    h = t.shape[0] // 2
    first = lax.ppermute(from_left[:h], "dp", _x_shift(n, 1))
    second = lax.ppermute(from_right[h:], "dp", _x_shift(n, -1))
    return [t, from_right, jnp.concatenate([first, second], axis=0), from_left]


def dp_gather_2d(t, n):
    assert n == 8
    me = lax.axis_index("dp")
    x, l, nx = me // 2, me % 2, n // 2
    partner = lax.ppermute(t, "dp", _y_pair(n))
    stacked = jnp.stack(x_ring_gather(t, n) + x_ring_gather(partner, n))
    p = jnp.arange(n, dtype=jnp.int32)
    order = (p // 2 - x) % nx + nx * (p % 2 != l).astype(jnp.int32)
    return jnp.take(stacked, order, axis=0)


def x_ring_scatter(blocks, n):
    h = blocks[0].shape[0] // 2
    low = lax.ppermute(blocks[2][:h].astype(jnp.bfloat16), "dp", _x_shift(n, 1))
    high = lax.ppermute(blocks[2][h:].astype(jnp.bfloat16), "dp", _x_shift(n, -1))
    to_right = jnp.concatenate([blocks[1][:h] + low.astype(jnp.float32), blocks[1][h:]], axis=0)
    to_left = jnp.concatenate([blocks[3][:h], blocks[3][h:] + high.astype(jnp.float32)], axis=0)
    from_left = lax.ppermute(to_right.astype(jnp.bfloat16), "dp", _x_shift(n, 1))
    from_right = lax.ppermute(to_left.astype(jnp.bfloat16), "dp", _x_shift(n, -1))
    return blocks[0] + from_left.astype(jnp.float32) + from_right.astype(jnp.float32)


def dp_scatter_2d(partial, n):
    assert n == 8
    me = lax.axis_index("dp")
    x, l, nx = me // 2, me % 2, n // 2
    blocks = partial.reshape((n, partial.shape[0] // n) + partial.shape[1:])

    def pick(m, side):
        index = 2 * ((x + m) % nx) + side
        return lax.dynamic_index_in_dim(blocks, index, 0, keepdims=False).astype(jnp.float32)

    partner_sum = x_ring_scatter([pick(m, 1 - l) for m in range(nx)], n)
    sent = lax.ppermute(partner_sum.astype(jnp.bfloat16), "dp", _y_pair(n))
    own_sum = x_ring_scatter([pick(m, l) for m in range(nx)], n)
    return own_sum + sent.astype(jnp.float32)


def _ring_gather_kernel(n, *refs):
    count = (len(refs) - 3) // 2
    shards, outs = refs[:count], refs[count : 2 * count]
    send_sem, recv_sem, local_sem = refs[2 * count :]
    me = lax.axis_index("dp")
    ex = lax.axis_index("expert")
    right, left, partner = lax.rem(me + 2, n), lax.rem(me + n - 2, n), me + 1 - 2 * lax.rem(me, 2)
    barrier = pltpu.get_barrier_semaphore()
    for peer in (right, left, partner):
        pl.semaphore_signal(barrier, inc=1, device_id=(peer, ex), device_id_type=MESH)
    pl.semaphore_wait(barrier, 3)

    def send(a, role, src, slot, rows, peer):
        copy = pltpu.make_async_remote_copy(
            src_ref=src,
            dst_ref=outs[a].at[slot, rows],
            send_sem=send_sem.at[a, role],
            recv_sem=recv_sem.at[a, role],
            device_id=(peer, ex),
            device_id_type=MESH,
        )
        copy.start()
        return copy

    spans = []
    for a in range(count):
        half = shards[a].shape[0] // 2
        spans.append((pl.ds(0, 2 * half), pl.ds(0, half), pl.ds(half, half)))
    locals_, first, second, third = [], [], [], []
    for a in range(count):
        local = pltpu.make_async_copy(shards[a], outs[a].at[me], local_sem.at[a])
        local.start()
        locals_.append(local)
        whole = spans[a][0]
        first += [
            send(a, 0, shards[a], me, whole, right),
            send(a, 1, shards[a], me, whole, left),
            send(a, 2, shards[a], me, whole, partner),
        ]
    for copy in first:
        copy.wait_recv()
    mate = partner
    for a in range(count):
        whole, low, high = spans[a]
        second += [
            send(a, 3, outs[a].at[left, low], left, low, right),
            send(a, 4, outs[a].at[right, high], right, high, left),
            send(a, 5, outs[a].at[mate], mate, whole, right),
            send(a, 6, outs[a].at[mate], mate, whole, left),
        ]
    for a in range(count):
        second[4 * a + 2].wait_recv()
        second[4 * a + 3].wait_recv()
    mate_left, mate_right = lax.rem(mate + n - 2, n), lax.rem(mate + 2, n)
    for a in range(count):
        whole, low, high = spans[a]
        third += [
            send(a, 7, outs[a].at[mate_left, low], mate_left, low, right),
            send(a, 8, outs[a].at[mate_right, high], mate_right, high, left),
        ]
    for copy in first:
        copy.wait_send()
    for a in range(count):
        second[4 * a].wait_recv()
        second[4 * a + 1].wait_recv()
    for copy in second:
        copy.wait_send()
    for copy in third:
        copy.wait_recv()
        copy.wait_send()
    for local in locals_:
        local.wait()


def dp_gather_kernel(shards, n):
    assert n == 8
    count = len(shards)
    return pl.pallas_call(
        functools.partial(_ring_gather_kernel, n),
        out_shape=[jax.ShapeDtypeStruct((n,) + s.shape, s.dtype) for s in shards],
        in_specs=[pl.BlockSpec(memory_space=pl.ANY)] * count,
        out_specs=[pl.BlockSpec(memory_space=pl.ANY)] * count,
        scratch_shapes=[
            pltpu.SemaphoreType.DMA((count, 9)),
            pltpu.SemaphoreType.DMA((count, 9)),
            pltpu.SemaphoreType.DMA((count,)),
        ],
        compiler_params=pltpu.CompilerParams(collective_id=2, has_side_effects=True),
    )(*shards)


def to_blocks(slot_array, num_blocks, pick_count):
    expert_count = slot_array.shape[0]
    trailing = slot_array.shape[2:]
    grouped = slot_array.reshape((expert_count, num_blocks, pick_count) + trailing)
    axis_order = (1, 0, 2) + tuple(range(3, 3 + len(trailing)))
    return jnp.transpose(grouped, axis_order).reshape(
        (num_blocks, expert_count * pick_count) + trailing
    )


def weight_grads(expert_rows, hidden, expert_cot, d_pre_gate, d_pre_up, n):
    hidden_activations = hidden.shape[2]
    out_part = jnp.einsum(
        "erc,erd->cd", hidden, expert_cot, preferred_element_type=jnp.float32
    ).astype(jnp.bfloat16)
    out_share = dp_scatter_2d(out_part, n)
    both_grads = jnp.concatenate([d_pre_gate, d_pre_up], axis=2)
    in_part = jnp.einsum(
        "erc,erk->ck", expert_rows, both_grads, preferred_element_type=jnp.float32
    ).astype(jnp.bfloat16)
    in_share = dp_scatter_2d(in_part, n)
    grad_gate = in_share[None, :, :hidden_activations]
    grad_up = in_share[None, :, hidden_activations:]
    down_weight_gradient = out_share[None]
    return (grad_gate, grad_up, down_weight_gradient)


def body(tokens, cotangent, chosen, w_router, w_gate, w_up, w_down):
    tok_rows, model_width = tokens.shape
    num_blocks, expert_count, pick_count = chosen.shape
    block_rows = tok_rows // num_blocks
    slot_count = num_blocks * pick_count
    logits = jnp.dot(tokens, w_router, preferred_element_type=jnp.float32)
    gate_values = jax.nn.sigmoid(logits)
    offsets = (jnp.arange(num_blocks, dtype=jnp.int32) * block_rows)[:, None, None]
    slot_rows = jnp.transpose(chosen + offsets, (1, 0, 2)).reshape(expert_count, slot_count)
    picked = tokens[slot_rows]
    slot_gate_values = jnp.take_along_axis(gate_values.T, slot_rows, axis=1)
    cot_rows = cotangent[slot_rows]
    scaled_cot = (slot_gate_values[:, :, None] * cot_rows.astype(jnp.float32)).astype(jnp.bfloat16)
    n = lax.axis_size("dp")
    full_gate, full_up, full_down = (
        g.reshape((1, -1) + g.shape[2:])
        for g in dp_gather_kernel([w_gate[0], w_up[0], w_down[0]], n)
    )
    expert_count_axis = lax.axis_size("expert")
    dispatched = lax.all_to_all(
        jnp.concatenate([picked, scaled_cot], axis=1), "expert", 0, 0, tiled=True
    )
    slot_width = picked.shape[1]
    expert_rows = dispatched[:, :slot_width].reshape(1, -1, model_width)
    pre_gate = jnp.einsum(
        "erd,edh->erh", expert_rows, full_gate, preferred_element_type=jnp.float32
    )
    pre_up = jnp.einsum("erd,edh->erh", expert_rows, full_up, preferred_element_type=jnp.float32)
    silu_gate = jax.nn.silu(pre_gate)
    hidden = (silu_gate * pre_up).astype(jnp.bfloat16)
    expert_out = jnp.einsum(
        "erh,ehd->erd", hidden, full_down, preferred_element_type=jnp.float32
    ).astype(jnp.bfloat16)
    returned = lax.all_to_all(
        expert_out.reshape(expert_count_axis, -1, model_width), "expert", 0, 0, tiled=True
    )
    expert_cot = dispatched[:, slot_width:].reshape(1, -1, model_width)
    back_gate, back_up, back_down = (full_gate, full_up, full_down)
    d_hidden = jnp.einsum("erd,ehd->erh", expert_cot, back_down, preferred_element_type=jnp.float32)
    gate_sigmoid = jax.nn.sigmoid(pre_gate)
    d_pre_gate = (
        d_hidden * pre_up * gate_sigmoid * (1.0 + pre_gate * (1.0 - gate_sigmoid))
    ).astype(jnp.bfloat16)
    d_pre_up = (d_hidden * silu_gate).astype(jnp.bfloat16)
    d_rows = (
        jnp.einsum("erh,edh->erd", d_pre_gate, back_gate, preferred_element_type=jnp.float32)
        + jnp.einsum("erh,edh->erd", d_pre_up, back_up, preferred_element_type=jnp.float32)
    ).astype(jnp.bfloat16)
    row_grads = lax.all_to_all(
        d_rows.reshape(expert_count_axis, -1, model_width), "expert", 0, 0, tiled=True
    )
    position_hits = chosen[:, :, :, None] == jnp.arange(block_rows, dtype=jnp.int32)
    indicator_matrix = position_hits.reshape(num_blocks, expert_count * pick_count, block_rows)
    gate_weighted_rows = to_blocks(slot_gate_values, num_blocks, pick_count)[
        :, :, None
    ] * to_blocks(returned, num_blocks, pick_count).astype(jnp.float32)
    mixed = (
        jnp.einsum(
            "wze,wzi->wei",
            indicator_matrix.astype(jnp.float32),
            gate_weighted_rows,
            precision=lax.Precision.HIGHEST,
        )
        .reshape(tok_rows, model_width)
        .astype(jnp.bfloat16)
    )
    slot_dots = jnp.sum(cot_rows.astype(jnp.float32) * returned.astype(jnp.float32), axis=2)
    dgate = jnp.einsum(
        "bept,ebp->bte",
        position_hits.astype(jnp.float32),
        slot_dots.reshape(expert_count, num_blocks, pick_count),
        precision=lax.Precision.HIGHEST,
    ).reshape(tok_rows, expert_count)
    d_logit = (dgate * gate_values * (1.0 - gate_values)).astype(jnp.bfloat16)
    gathered_grads = jnp.einsum(
        "wze,wzi->wei",
        indicator_matrix.astype(jnp.bfloat16),
        to_blocks(row_grads, num_blocks, pick_count),
        preferred_element_type=jnp.float32,
    ).reshape(tok_rows, model_width)
    grad_tokens = (
        gathered_grads + jnp.dot(d_logit, w_router.T, preferred_element_type=jnp.float32)
    ).astype(jnp.bfloat16)
    router_full = jnp.dot(tokens.T, d_logit, preferred_element_type=jnp.float32)
    devices = n * expert_count_axis
    router_part = jnp.sum(
        lax.all_to_all(router_full.reshape(devices, -1), ("dp", "expert"), 0, 0, tiled=True),
        axis=0,
    )
    grad_gate, grad_up, down_weight_gradient = weight_grads(
        expert_rows, hidden, expert_cot, d_pre_gate, d_pre_up, n
    )
    grad_router = lax.all_to_all(
        jnp.broadcast_to(router_part[None], (devices,) + router_part.shape),
        ("dp", "expert"),
        0,
        0,
        tiled=True,
    ).reshape(router_full.shape)
    return (mixed, grad_tokens, grad_gate, grad_up, down_weight_gradient, grad_router)


def solution(mesh):
    placed = (
        P(("dp", "expert"), None),
        P(("dp", "expert"), None),
        P(("dp", "expert"), None, None),
        P(),
        P("expert", "dp", None),
        P("expert", "dp", None),
        P("expert", "dp", None),
    )
    return jax.shard_map(
        body,
        mesh=mesh,
        in_specs=placed,
        out_specs=(
            P(("dp", "expert"), None),
            P(("dp", "expert"), None),
            P("expert", "dp", None),
            P("expert", "dp", None),
            P("expert", "dp", None),
            P(),
        ),
        check_vma=False,
    )
```

```python
import functools

import jax
import jax.numpy as jnp
from jax import lax
from jax.experimental import pallas as pl
from jax.experimental.pallas import tpu as pltpu
from jax.sharding import PartitionSpec as P

MESH = pl.DeviceIdType.MESH


def _gather_kernel(n, *refs):
    count = (len(refs) - 3) // 2
    srcs, dsts = refs[:count], refs[count : 2 * count]
    send_sem, recv_sem, local_sem = refs[2 * count :]
    me = lax.axis_index("dp")
    ex = lax.axis_index("expert")
    barrier = pltpu.get_barrier_semaphore()
    for k in range(1, n):
        pl.semaphore_signal(barrier, inc=1, device_id=(lax.rem(me + k, n), ex), device_id_type=MESH)
    pl.semaphore_wait(barrier, n - 1)
    copies = []
    for a in range(count):
        rows = srcs[a].shape[0]
        slot = dsts[a].at[pl.ds(me * rows, rows)]
        local = pltpu.make_async_copy(srcs[a], slot, local_sem.at[a])
        local.start()
        copies.append(local)
        for k in range(1, n):
            remote = pltpu.make_async_remote_copy(
                src_ref=srcs[a],
                dst_ref=slot,
                send_sem=send_sem.at[a, k],
                recv_sem=recv_sem.at[a, k],
                device_id=(lax.rem(me + k, n), ex),
                device_id_type=MESH,
            )
            remote.start()
            copies.append(remote)
    for c in copies:
        c.wait()


def dp_all_gather(shards, n):
    count = len(shards)
    return pl.pallas_call(
        functools.partial(_gather_kernel, n),
        out_shape=[jax.ShapeDtypeStruct((n * s.shape[0],) + s.shape[1:], s.dtype) for s in shards],
        in_specs=[pl.BlockSpec(memory_space=pl.ANY)] * count,
        out_specs=[pl.BlockSpec(memory_space=pl.ANY)] * count,
        scratch_shapes=[
            pltpu.SemaphoreType.DMA((count, n)),
            pltpu.SemaphoreType.DMA((count, n)),
            pltpu.SemaphoreType.DMA((count,)),
        ],
        compiler_params=pltpu.CompilerParams(collective_id=0, has_side_effects=True),
    )(*shards)


def _exchange_kernel(n, n_scatter, *refs):
    count = (len(refs) - 3) // 2
    srcs, dsts = refs[:count], refs[count : 2 * count]
    send_sem, recv_sem, local_sem = refs[2 * count :]
    me = lax.axis_index("dp")
    ex = lax.axis_index("expert")
    barrier = pltpu.get_barrier_semaphore()
    for k in range(1, n):
        pl.semaphore_signal(barrier, inc=1, device_id=(lax.rem(me + k, n), ex), device_id_type=MESH)
    pl.semaphore_wait(barrier, n - 1)
    copies = []
    for a in range(count):
        rows = dsts[a].shape[1]
        if a < n_scatter:
            mine = srcs[a].at[pl.ds(me * rows, rows)]
        else:
            mine = srcs[a]
        local = pltpu.make_async_copy(mine, dsts[a].at[me], local_sem.at[a])
        local.start()
        copies.append(local)
        for k in range(1, n):
            peer = lax.rem(me + k, n)
            if a < n_scatter:
                part = srcs[a].at[pl.ds(peer * rows, rows)]
            else:
                part = srcs[a]
            remote = pltpu.make_async_remote_copy(
                src_ref=part,
                dst_ref=dsts[a].at[me],
                send_sem=send_sem.at[a, k],
                recv_sem=recv_sem.at[a, k],
                device_id=(peer, ex),
                device_id_type=MESH,
            )
            remote.start()
            copies.append(remote)
    for c in copies:
        c.wait()


def dp_exchange(partials, replicas, n):
    arrays = list(partials) + list(replicas)
    count = len(arrays)
    shapes = [(n, p.shape[0] // n) + p.shape[1:] for p in partials]
    shapes += [(n,) + r.shape for r in replicas]
    received = pl.pallas_call(
        functools.partial(_exchange_kernel, n, len(partials)),
        out_shape=[jax.ShapeDtypeStruct(s, a.dtype) for s, a in zip(shapes, arrays)],
        in_specs=[pl.BlockSpec(memory_space=pl.ANY)] * count,
        out_specs=[pl.BlockSpec(memory_space=pl.ANY)] * count,
        scratch_shapes=[
            pltpu.SemaphoreType.DMA((count, n)),
            pltpu.SemaphoreType.DMA((count, n)),
            pltpu.SemaphoreType.DMA((count,)),
        ],
        compiler_params=pltpu.CompilerParams(collective_id=1, has_side_effects=True),
    )(*arrays)
    return [jnp.sum(r.astype(jnp.float32), axis=0) for r in received]


def _shift_pairs(n, k):
    return [(i, (i + k) % n) for i in range(n)]


def dp_gather_permute(shard, n):
    me = lax.axis_index("dp")
    full = jnp.zeros((n,) + shard.shape, shard.dtype)
    full = lax.dynamic_update_index_in_dim(full, shard, me, 0)
    for k in range(1, n):
        got = lax.ppermute(shard, "dp", perm=_shift_pairs(n, k))
        full = lax.dynamic_update_index_in_dim(full, got, lax.rem(me + n - k, n), 0)
    return full


def dp_scatter_permute(partial, n):
    me = lax.axis_index("dp")
    blocks = partial.reshape((n, partial.shape[0] // n) + partial.shape[1:])
    total = lax.dynamic_index_in_dim(blocks, me, 0, keepdims=False).astype(jnp.float32)
    for k in range(1, n):
        piece = lax.dynamic_index_in_dim(blocks, lax.rem(me + k, n), 0, keepdims=False)
        got = lax.ppermute(piece, "dp", perm=_shift_pairs(n, k))
        total = total + got.astype(jnp.float32)
    return total


def _x_shift(n, d):
    return [(i, (i + 2 * d) % n) for i in range(n)]


def _y_pair(n):
    return [(i, i ^ 1) for i in range(n)]


def x_ring_gather(t, n):
    from_left = lax.ppermute(t, "dp", _x_shift(n, 1))
    from_right = lax.ppermute(t, "dp", _x_shift(n, -1))
    h = t.shape[0] // 2
    first = lax.ppermute(from_left[:h], "dp", _x_shift(n, 1))
    second = lax.ppermute(from_right[h:], "dp", _x_shift(n, -1))
    return [t, from_right, jnp.concatenate([first, second], axis=0), from_left]


def dp_gather_2d(t, n):
    assert n == 8
    me = lax.axis_index("dp")
    x, l, nx = me // 2, me % 2, n // 2
    partner = lax.ppermute(t, "dp", _y_pair(n))
    stacked = jnp.stack(x_ring_gather(t, n) + x_ring_gather(partner, n))
    p = jnp.arange(n, dtype=jnp.int32)
    order = (p // 2 - x) % nx + nx * (p % 2 != l).astype(jnp.int32)
    return jnp.take(stacked, order, axis=0)


def x_ring_scatter(blocks, n):
    h = blocks[0].shape[0] // 2
    low = lax.ppermute(blocks[2][:h].astype(jnp.bfloat16), "dp", _x_shift(n, 1))
    high = lax.ppermute(blocks[2][h:].astype(jnp.bfloat16), "dp", _x_shift(n, -1))
    to_right = jnp.concatenate([blocks[1][:h] + low.astype(jnp.float32), blocks[1][h:]], axis=0)
    to_left = jnp.concatenate([blocks[3][:h], blocks[3][h:] + high.astype(jnp.float32)], axis=0)
    from_left = lax.ppermute(to_right.astype(jnp.bfloat16), "dp", _x_shift(n, 1))
    from_right = lax.ppermute(to_left.astype(jnp.bfloat16), "dp", _x_shift(n, -1))
    return blocks[0] + from_left.astype(jnp.float32) + from_right.astype(jnp.float32)


def dp_scatter_2d(partial, n):
    assert n == 8
    me = lax.axis_index("dp")
    x, l, nx = me // 2, me % 2, n // 2
    blocks = partial.reshape((n, partial.shape[0] // n) + partial.shape[1:])

    def pick(m, side):
        index = 2 * ((x + m) % nx) + side
        return lax.dynamic_index_in_dim(blocks, index, 0, keepdims=False).astype(jnp.float32)

    partner_sum = x_ring_scatter([pick(m, 1 - l) for m in range(nx)], n)
    sent = lax.ppermute(partner_sum.astype(jnp.bfloat16), "dp", _y_pair(n))
    own_sum = x_ring_scatter([pick(m, l) for m in range(nx)], n)
    return own_sum + sent.astype(jnp.float32)


def _ring_gather_kernel(n, *refs):
    count = (len(refs) - 3) // 2
    shards, outs = refs[:count], refs[count : 2 * count]
    send_sem, recv_sem, local_sem = refs[2 * count :]
    me = lax.axis_index("dp")
    ex = lax.axis_index("expert")
    right, left, partner = lax.rem(me + 2, n), lax.rem(me + n - 2, n), me + 1 - 2 * lax.rem(me, 2)
    barrier = pltpu.get_barrier_semaphore()
    for peer in (right, left, partner):
        pl.semaphore_signal(barrier, inc=1, device_id=(peer, ex), device_id_type=MESH)
    pl.semaphore_wait(barrier, 3)

    def send(a, role, src, slot, rows, peer):
        copy = pltpu.make_async_remote_copy(
            src_ref=src,
            dst_ref=outs[a].at[slot, rows],
            send_sem=send_sem.at[a, role],
            recv_sem=recv_sem.at[a, role],
            device_id=(peer, ex),
            device_id_type=MESH,
        )
        copy.start()
        return copy

    spans = []
    for a in range(count):
        half = shards[a].shape[0] // 2
        spans.append((pl.ds(0, 2 * half), pl.ds(0, half), pl.ds(half, half)))
    locals_, first, second, third = [], [], [], []
    for a in range(count):
        local = pltpu.make_async_copy(shards[a], outs[a].at[me], local_sem.at[a])
        local.start()
        locals_.append(local)
        whole = spans[a][0]
        first += [
            send(a, 0, shards[a], me, whole, right),
            send(a, 1, shards[a], me, whole, left),
            send(a, 2, shards[a], me, whole, partner),
        ]
    for copy in first:
        copy.wait_recv()
    mate = partner
    for a in range(count):
        whole, low, high = spans[a]
        second += [
            send(a, 3, outs[a].at[left, low], left, low, right),
            send(a, 4, outs[a].at[right, high], right, high, left),
            send(a, 5, outs[a].at[mate], mate, whole, right),
            send(a, 6, outs[a].at[mate], mate, whole, left),
        ]
    for a in range(count):
        second[4 * a + 2].wait_recv()
        second[4 * a + 3].wait_recv()
    mate_left, mate_right = lax.rem(mate + n - 2, n), lax.rem(mate + 2, n)
    for a in range(count):
        whole, low, high = spans[a]
        third += [
            send(a, 7, outs[a].at[mate_left, low], mate_left, low, right),
            send(a, 8, outs[a].at[mate_right, high], mate_right, high, left),
        ]
    for copy in first:
        copy.wait_send()
    for a in range(count):
        second[4 * a].wait_recv()
        second[4 * a + 1].wait_recv()
    for copy in second:
        copy.wait_send()
    for copy in third:
        copy.wait_recv()
        copy.wait_send()
    for local in locals_:
        local.wait()


def dp_gather_kernel(shards, n):
    assert n == 8
    count = len(shards)
    return pl.pallas_call(
        functools.partial(_ring_gather_kernel, n),
        out_shape=[jax.ShapeDtypeStruct((n,) + s.shape, s.dtype) for s in shards],
        in_specs=[pl.BlockSpec(memory_space=pl.ANY)] * count,
        out_specs=[pl.BlockSpec(memory_space=pl.ANY)] * count,
        scratch_shapes=[
            pltpu.SemaphoreType.DMA((count, 9)),
            pltpu.SemaphoreType.DMA((count, 9)),
            pltpu.SemaphoreType.DMA((count,)),
        ],
        compiler_params=pltpu.CompilerParams(collective_id=2, has_side_effects=True),
    )(*shards)


def to_blocks(slot_array, num_blocks, pick_count):
    expert_count = slot_array.shape[0]
    trailing = slot_array.shape[2:]
    grouped = slot_array.reshape((expert_count, num_blocks, pick_count) + trailing)
    axis_order = (1, 0, 2) + tuple(range(3, 3 + len(trailing)))
    return jnp.transpose(grouped, axis_order).reshape(
        (num_blocks, expert_count * pick_count) + trailing
    )


def weight_grads(expert_rows, hidden, expert_cot, d_pre_gate, d_pre_up, n):
    hidden_activations = hidden.shape[2]
    out_part = jnp.einsum(
        "erc,erd->cd", hidden, expert_cot, preferred_element_type=jnp.float32
    ).astype(jnp.bfloat16)
    out_share = dp_scatter_2d(out_part, n)
    both_grads = jnp.concatenate([d_pre_gate, d_pre_up], axis=2)
    in_part = jnp.einsum(
        "erc,erk->ck", expert_rows, both_grads, preferred_element_type=jnp.float32
    ).astype(jnp.bfloat16)
    in_share = dp_scatter_2d(in_part, n)
    grad_gate = in_share[None, :, :hidden_activations]
    grad_up = in_share[None, :, hidden_activations:]
    down_weight_gradient = out_share[None]
    return (grad_gate, grad_up, down_weight_gradient)


def body(tokens, cotangent, chosen, w_router, w_gate, w_up, w_down):
    tok_rows, model_width = tokens.shape
    num_blocks, expert_count, pick_count = chosen.shape
    block_rows = tok_rows // num_blocks
    slot_count = num_blocks * pick_count
    logits = jnp.dot(tokens, w_router, preferred_element_type=jnp.float32)
    gate_values = jax.nn.sigmoid(logits)
    offsets = (jnp.arange(num_blocks, dtype=jnp.int32) * block_rows)[:, None, None]
    slot_rows = jnp.transpose(chosen + offsets, (1, 0, 2)).reshape(expert_count, slot_count)
    picked = tokens[slot_rows]
    slot_gate_values = jnp.take_along_axis(gate_values.T, slot_rows, axis=1)
    cot_rows = cotangent[slot_rows]
    scaled_cot = (slot_gate_values[:, :, None] * cot_rows.astype(jnp.float32)).astype(jnp.bfloat16)
    n = lax.axis_size("dp")
    full_gate, full_up, full_down = (
        g.reshape((1, -1) + g.shape[2:])
        for g in dp_gather_kernel([w_gate[0], w_up[0], w_down[0]], n)
    )
    expert_count_axis = lax.axis_size("expert")
    dispatched = lax.all_to_all(
        jnp.concatenate([picked, scaled_cot], axis=1), "expert", 0, 0, tiled=True
    )
    slot_width = picked.shape[1]
    expert_rows = dispatched[:, :slot_width].reshape(1, -1, model_width)
    pre_gate = jnp.einsum(
        "erd,edh->erh", expert_rows, full_gate, preferred_element_type=jnp.float32
    )
    pre_up = jnp.einsum("erd,edh->erh", expert_rows, full_up, preferred_element_type=jnp.float32)
    silu_gate = jax.nn.silu(pre_gate)
    hidden = (silu_gate * pre_up).astype(jnp.bfloat16)
    expert_out = jnp.einsum(
        "erh,ehd->erd", hidden, full_down, preferred_element_type=jnp.float32
    ).astype(jnp.bfloat16)
    returned = lax.all_to_all(
        expert_out.reshape(expert_count_axis, -1, model_width), "expert", 0, 0, tiled=True
    )
    expert_cot = dispatched[:, slot_width:].reshape(1, -1, model_width)
    back_gate, back_up, back_down = (full_gate, full_up, full_down)
    d_hidden = jnp.einsum("erd,ehd->erh", expert_cot, back_down, preferred_element_type=jnp.float32)
    gate_sigmoid = jax.nn.sigmoid(pre_gate)
    d_pre_gate = (
        d_hidden * pre_up * gate_sigmoid * (1.0 + pre_gate * (1.0 - gate_sigmoid))
    ).astype(jnp.bfloat16)
    d_pre_up = (d_hidden * silu_gate).astype(jnp.bfloat16)
    d_rows = (
        jnp.einsum("erh,edh->erd", d_pre_gate, back_gate, preferred_element_type=jnp.float32)
        + jnp.einsum("erh,edh->erd", d_pre_up, back_up, preferred_element_type=jnp.float32)
    ).astype(jnp.bfloat16)
    position_hits = chosen[:, :, :, None] == jnp.arange(block_rows, dtype=jnp.int32)
    indicator_matrix = position_hits.reshape(num_blocks, expert_count * pick_count, block_rows)
    gate_weighted_rows = to_blocks(slot_gate_values, num_blocks, pick_count)[
        :, :, None
    ] * to_blocks(returned, num_blocks, pick_count).astype(jnp.float32)
    mixed = (
        jnp.einsum(
            "wze,wzi->wei",
            indicator_matrix.astype(jnp.float32),
            gate_weighted_rows,
            precision=lax.Precision.HIGHEST,
        )
        .reshape(tok_rows, model_width)
        .astype(jnp.bfloat16)
    )
    slot_dots = jnp.sum(cot_rows.astype(jnp.float32) * returned.astype(jnp.float32), axis=2)
    dgate = jnp.einsum(
        "bept,ebp->bte",
        position_hits.astype(jnp.float32),
        slot_dots.reshape(expert_count, num_blocks, pick_count),
        precision=lax.Precision.HIGHEST,
    ).reshape(tok_rows, expert_count)
    d_logit = (dgate * gate_values * (1.0 - gate_values)).astype(jnp.bfloat16)
    router_full = jnp.dot(tokens.T, d_logit, preferred_element_type=jnp.float32)
    router_full, d_rows = lax.optimization_barrier((router_full, d_rows))
    devices = n * expert_count_axis
    router_part = jnp.sum(
        lax.all_to_all(router_full.reshape(devices, -1), ("dp", "expert"), 0, 0, tiled=True),
        axis=0,
    )
    row_grads = lax.all_to_all(
        d_rows.reshape(expert_count_axis, -1, model_width), "expert", 0, 0, tiled=True
    )
    gathered_grads = jnp.einsum(
        "wze,wzi->wei",
        indicator_matrix.astype(jnp.bfloat16),
        to_blocks(row_grads, num_blocks, pick_count),
        preferred_element_type=jnp.float32,
    ).reshape(tok_rows, model_width)
    grad_tokens = (
        gathered_grads + jnp.dot(d_logit, w_router.T, preferred_element_type=jnp.float32)
    ).astype(jnp.bfloat16)
    grad_gate, grad_up, down_weight_gradient = weight_grads(
        expert_rows, hidden, expert_cot, d_pre_gate, d_pre_up, n
    )
    grad_router = lax.all_to_all(
        jnp.broadcast_to(router_part[None], (devices,) + router_part.shape),
        ("dp", "expert"),
        0,
        0,
        tiled=True,
    ).reshape(router_full.shape)
    return (mixed, grad_tokens, grad_gate, grad_up, down_weight_gradient, grad_router)


def solution(mesh):
    placed = (
        P(("dp", "expert"), None),
        P(("dp", "expert"), None),
        P(("dp", "expert"), None, None),
        P(),
        P("expert", "dp", None),
        P("expert", "dp", None),
        P("expert", "dp", None),
    )
    return jax.shard_map(
        body,
        mesh=mesh,
        in_specs=placed,
        out_specs=(
            P(("dp", "expert"), None),
            P(("dp", "expert"), None),
            P("expert", "dp", None),
            P("expert", "dp", None),
            P("expert", "dp", None),
            P(),
        ),
        check_vma=False,
    )
```

```python
import functools

import jax
import jax.numpy as jnp
from jax import lax
from jax.experimental import pallas as pl
from jax.experimental.pallas import tpu as pltpu
from jax.sharding import PartitionSpec as P

MESH = pl.DeviceIdType.MESH


def _gather_kernel(n, *refs):
    count = (len(refs) - 3) // 2
    srcs, dsts = refs[:count], refs[count : 2 * count]
    send_sem, recv_sem, local_sem = refs[2 * count :]
    me = lax.axis_index("dp")
    ex = lax.axis_index("expert")
    barrier = pltpu.get_barrier_semaphore()
    for k in range(1, n):
        pl.semaphore_signal(barrier, inc=1, device_id=(lax.rem(me + k, n), ex), device_id_type=MESH)
    pl.semaphore_wait(barrier, n - 1)
    copies = []
    for a in range(count):
        rows = srcs[a].shape[0]
        slot = dsts[a].at[pl.ds(me * rows, rows)]
        local = pltpu.make_async_copy(srcs[a], slot, local_sem.at[a])
        local.start()
        copies.append(local)
        for k in range(1, n):
            remote = pltpu.make_async_remote_copy(
                src_ref=srcs[a],
                dst_ref=slot,
                send_sem=send_sem.at[a, k],
                recv_sem=recv_sem.at[a, k],
                device_id=(lax.rem(me + k, n), ex),
                device_id_type=MESH,
            )
            remote.start()
            copies.append(remote)
    for c in copies:
        c.wait()


def dp_all_gather(shards, n):
    count = len(shards)
    return pl.pallas_call(
        functools.partial(_gather_kernel, n),
        out_shape=[jax.ShapeDtypeStruct((n * s.shape[0],) + s.shape[1:], s.dtype) for s in shards],
        in_specs=[pl.BlockSpec(memory_space=pl.ANY)] * count,
        out_specs=[pl.BlockSpec(memory_space=pl.ANY)] * count,
        scratch_shapes=[
            pltpu.SemaphoreType.DMA((count, n)),
            pltpu.SemaphoreType.DMA((count, n)),
            pltpu.SemaphoreType.DMA((count,)),
        ],
        compiler_params=pltpu.CompilerParams(collective_id=0, has_side_effects=True),
    )(*shards)


def _exchange_kernel(n, n_scatter, *refs):
    count = (len(refs) - 3) // 2
    srcs, dsts = refs[:count], refs[count : 2 * count]
    send_sem, recv_sem, local_sem = refs[2 * count :]
    me = lax.axis_index("dp")
    ex = lax.axis_index("expert")
    barrier = pltpu.get_barrier_semaphore()
    for k in range(1, n):
        pl.semaphore_signal(barrier, inc=1, device_id=(lax.rem(me + k, n), ex), device_id_type=MESH)
    pl.semaphore_wait(barrier, n - 1)
    copies = []
    for a in range(count):
        rows = dsts[a].shape[1]
        if a < n_scatter:
            mine = srcs[a].at[pl.ds(me * rows, rows)]
        else:
            mine = srcs[a]
        local = pltpu.make_async_copy(mine, dsts[a].at[me], local_sem.at[a])
        local.start()
        copies.append(local)
        for k in range(1, n):
            peer = lax.rem(me + k, n)
            if a < n_scatter:
                part = srcs[a].at[pl.ds(peer * rows, rows)]
            else:
                part = srcs[a]
            remote = pltpu.make_async_remote_copy(
                src_ref=part,
                dst_ref=dsts[a].at[me],
                send_sem=send_sem.at[a, k],
                recv_sem=recv_sem.at[a, k],
                device_id=(peer, ex),
                device_id_type=MESH,
            )
            remote.start()
            copies.append(remote)
    for c in copies:
        c.wait()


def dp_exchange(partials, replicas, n):
    arrays = list(partials) + list(replicas)
    count = len(arrays)
    shapes = [(n, p.shape[0] // n) + p.shape[1:] for p in partials]
    shapes += [(n,) + r.shape for r in replicas]
    received = pl.pallas_call(
        functools.partial(_exchange_kernel, n, len(partials)),
        out_shape=[jax.ShapeDtypeStruct(s, a.dtype) for s, a in zip(shapes, arrays)],
        in_specs=[pl.BlockSpec(memory_space=pl.ANY)] * count,
        out_specs=[pl.BlockSpec(memory_space=pl.ANY)] * count,
        scratch_shapes=[
            pltpu.SemaphoreType.DMA((count, n)),
            pltpu.SemaphoreType.DMA((count, n)),
            pltpu.SemaphoreType.DMA((count,)),
        ],
        compiler_params=pltpu.CompilerParams(collective_id=1, has_side_effects=True),
    )(*arrays)
    return [jnp.sum(r.astype(jnp.float32), axis=0) for r in received]


def _shift_pairs(n, k):
    return [(i, (i + k) % n) for i in range(n)]


def dp_gather_permute(shard, n):
    me = lax.axis_index("dp")
    full = jnp.zeros((n,) + shard.shape, shard.dtype)
    full = lax.dynamic_update_index_in_dim(full, shard, me, 0)
    for k in range(1, n):
        got = lax.ppermute(shard, "dp", perm=_shift_pairs(n, k))
        full = lax.dynamic_update_index_in_dim(full, got, lax.rem(me + n - k, n), 0)
    return full


def dp_scatter_permute(partial, n):
    me = lax.axis_index("dp")
    blocks = partial.reshape((n, partial.shape[0] // n) + partial.shape[1:])
    total = lax.dynamic_index_in_dim(blocks, me, 0, keepdims=False).astype(jnp.float32)
    for k in range(1, n):
        piece = lax.dynamic_index_in_dim(blocks, lax.rem(me + k, n), 0, keepdims=False)
        got = lax.ppermute(piece, "dp", perm=_shift_pairs(n, k))
        total = total + got.astype(jnp.float32)
    return total


def _x_shift(n, d):
    return [(i, (i + 2 * d) % n) for i in range(n)]


def _y_pair(n):
    return [(i, i ^ 1) for i in range(n)]


def x_ring_gather(t, n):
    from_left = lax.ppermute(t, "dp", _x_shift(n, 1))
    from_right = lax.ppermute(t, "dp", _x_shift(n, -1))
    h = t.shape[0] // 2
    first = lax.ppermute(from_left[:h], "dp", _x_shift(n, 1))
    second = lax.ppermute(from_right[h:], "dp", _x_shift(n, -1))
    return [t, from_right, jnp.concatenate([first, second], axis=0), from_left]


def dp_gather_2d(t, n):
    assert n == 8
    me = lax.axis_index("dp")
    x, l, nx = me // 2, me % 2, n // 2
    partner = lax.ppermute(t, "dp", _y_pair(n))
    stacked = jnp.stack(x_ring_gather(t, n) + x_ring_gather(partner, n))
    p = jnp.arange(n, dtype=jnp.int32)
    order = (p // 2 - x) % nx + nx * (p % 2 != l).astype(jnp.int32)
    return jnp.take(stacked, order, axis=0)


def x_ring_scatter(blocks, n):
    h = blocks[0].shape[0] // 2
    low = lax.ppermute(blocks[2][:h].astype(jnp.bfloat16), "dp", _x_shift(n, 1))
    high = lax.ppermute(blocks[2][h:].astype(jnp.bfloat16), "dp", _x_shift(n, -1))
    to_right = jnp.concatenate([blocks[1][:h] + low.astype(jnp.float32), blocks[1][h:]], axis=0)
    to_left = jnp.concatenate([blocks[3][:h], blocks[3][h:] + high.astype(jnp.float32)], axis=0)
    from_left = lax.ppermute(to_right.astype(jnp.bfloat16), "dp", _x_shift(n, 1))
    from_right = lax.ppermute(to_left.astype(jnp.bfloat16), "dp", _x_shift(n, -1))
    return blocks[0] + from_left.astype(jnp.float32) + from_right.astype(jnp.float32)


def dp_scatter_2d(partial, n):
    assert n == 8
    me = lax.axis_index("dp")
    x, l, nx = me // 2, me % 2, n // 2
    blocks = partial.reshape((n, partial.shape[0] // n) + partial.shape[1:])

    def pick(m, side):
        index = 2 * ((x + m) % nx) + side
        return lax.dynamic_index_in_dim(blocks, index, 0, keepdims=False).astype(jnp.float32)

    partner_sum = x_ring_scatter([pick(m, 1 - l) for m in range(nx)], n)
    sent = lax.ppermute(partner_sum.astype(jnp.bfloat16), "dp", _y_pair(n))
    own_sum = x_ring_scatter([pick(m, l) for m in range(nx)], n)
    return own_sum + sent.astype(jnp.float32)


def _ring_gather_kernel(n, *refs):
    count = (len(refs) - 3) // 2
    shards, outs = refs[:count], refs[count : 2 * count]
    send_sem, recv_sem, local_sem = refs[2 * count :]
    me = lax.axis_index("dp")
    ex = lax.axis_index("expert")
    right, left, partner = lax.rem(me + 2, n), lax.rem(me + n - 2, n), me + 1 - 2 * lax.rem(me, 2)
    barrier = pltpu.get_barrier_semaphore()
    for peer in (right, left, partner):
        pl.semaphore_signal(barrier, inc=1, device_id=(peer, ex), device_id_type=MESH)
    pl.semaphore_wait(barrier, 3)

    def send(a, role, src, slot, rows, peer):
        copy = pltpu.make_async_remote_copy(
            src_ref=src,
            dst_ref=outs[a].at[slot, rows],
            send_sem=send_sem.at[a, role],
            recv_sem=recv_sem.at[a, role],
            device_id=(peer, ex),
            device_id_type=MESH,
        )
        copy.start()
        return copy

    spans = []
    for a in range(count):
        half = shards[a].shape[0] // 2
        spans.append((pl.ds(0, 2 * half), pl.ds(0, half), pl.ds(half, half)))
    locals_, first, second, third = [], [], [], []
    for a in range(count):
        local = pltpu.make_async_copy(shards[a], outs[a].at[me], local_sem.at[a])
        local.start()
        locals_.append(local)
        whole = spans[a][0]
        first += [
            send(a, 0, shards[a], me, whole, right),
            send(a, 1, shards[a], me, whole, left),
            send(a, 2, shards[a], me, whole, partner),
        ]
    for copy in first:
        copy.wait_recv()
    mate = partner
    for a in range(count):
        whole, low, high = spans[a]
        second += [
            send(a, 3, outs[a].at[left, low], left, low, right),
            send(a, 4, outs[a].at[right, high], right, high, left),
            send(a, 5, outs[a].at[mate], mate, whole, right),
            send(a, 6, outs[a].at[mate], mate, whole, left),
        ]
    for a in range(count):
        second[4 * a + 2].wait_recv()
        second[4 * a + 3].wait_recv()
    mate_left, mate_right = lax.rem(mate + n - 2, n), lax.rem(mate + 2, n)
    for a in range(count):
        whole, low, high = spans[a]
        third += [
            send(a, 7, outs[a].at[mate_left, low], mate_left, low, right),
            send(a, 8, outs[a].at[mate_right, high], mate_right, high, left),
        ]
    for copy in first:
        copy.wait_send()
    for a in range(count):
        second[4 * a].wait_recv()
        second[4 * a + 1].wait_recv()
    for copy in second:
        copy.wait_send()
    for copy in third:
        copy.wait_recv()
        copy.wait_send()
    for local in locals_:
        local.wait()


def dp_gather_kernel(shards, n):
    assert n == 8
    count = len(shards)
    return pl.pallas_call(
        functools.partial(_ring_gather_kernel, n),
        out_shape=[jax.ShapeDtypeStruct((n,) + s.shape, s.dtype) for s in shards],
        in_specs=[pl.BlockSpec(memory_space=pl.ANY)] * count,
        out_specs=[pl.BlockSpec(memory_space=pl.ANY)] * count,
        scratch_shapes=[
            pltpu.SemaphoreType.DMA((count, 9)),
            pltpu.SemaphoreType.DMA((count, 9)),
            pltpu.SemaphoreType.DMA((count,)),
        ],
        compiler_params=pltpu.CompilerParams(collective_id=2, has_side_effects=True),
    )(*shards)


def to_blocks(slot_array, num_blocks, pick_count):
    expert_count = slot_array.shape[0]
    trailing = slot_array.shape[2:]
    grouped = slot_array.reshape((expert_count, num_blocks, pick_count) + trailing)
    axis_order = (1, 0, 2) + tuple(range(3, 3 + len(trailing)))
    return jnp.transpose(grouped, axis_order).reshape(
        (num_blocks, expert_count * pick_count) + trailing
    )


def weight_grads(expert_rows, hidden, expert_cot, d_pre_gate, d_pre_up, n):
    hidden_activations = hidden.shape[2]
    out_part = jnp.einsum(
        "erc,erd->cd", hidden, expert_cot, preferred_element_type=jnp.float32
    ).astype(jnp.bfloat16)
    both_grads = jnp.concatenate([d_pre_gate, d_pre_up], axis=2)
    in_part = jnp.einsum(
        "erc,erk->ck", expert_rows, both_grads, preferred_element_type=jnp.float32
    ).astype(jnp.bfloat16)
    out_rows, in_rows = out_part.shape[0] // n, in_part.shape[0] // n
    out_size = out_rows * out_part.shape[1]
    packed = jnp.concatenate([out_part.reshape(n, -1), in_part.reshape(n, -1)], axis=1)
    share = dp_scatter_2d(packed.reshape(-1, hidden_activations), n).reshape(-1)
    out_share = share[:out_size].reshape(out_rows, out_part.shape[1])
    in_share = share[out_size:].reshape(in_rows, in_part.shape[1])
    grad_gate = in_share[None, :, :hidden_activations]
    grad_up = in_share[None, :, hidden_activations:]
    down_weight_gradient = out_share[None]
    return (grad_gate, grad_up, down_weight_gradient)


def body(tokens, cotangent, chosen, w_router, w_gate, w_up, w_down):
    tok_rows, model_width = tokens.shape
    num_blocks, expert_count, pick_count = chosen.shape
    block_rows = tok_rows // num_blocks
    slot_count = num_blocks * pick_count
    logits = jnp.dot(tokens, w_router, preferred_element_type=jnp.float32)
    gate_values = jax.nn.sigmoid(logits)
    offsets = (jnp.arange(num_blocks, dtype=jnp.int32) * block_rows)[:, None, None]
    slot_rows = jnp.transpose(chosen + offsets, (1, 0, 2)).reshape(expert_count, slot_count)
    picked = tokens[slot_rows]
    slot_gate_values = jnp.take_along_axis(gate_values.T, slot_rows, axis=1)
    cot_rows = cotangent[slot_rows]
    scaled_cot = (slot_gate_values[:, :, None] * cot_rows.astype(jnp.float32)).astype(jnp.bfloat16)
    n = lax.axis_size("dp")
    full_gate, full_up, full_down = (
        g.reshape((1, -1) + g.shape[2:])
        for g in dp_gather_kernel([w_gate[0], w_up[0], w_down[0]], n)
    )
    expert_count_axis = lax.axis_size("expert")
    dispatched = lax.all_to_all(
        jnp.concatenate([picked, scaled_cot], axis=1), "expert", 0, 0, tiled=True
    )
    slot_width = picked.shape[1]
    expert_rows = dispatched[:, :slot_width].reshape(1, -1, model_width)
    pre_gate = jnp.einsum(
        "erd,edh->erh", expert_rows, full_gate, preferred_element_type=jnp.float32
    )
    pre_up = jnp.einsum("erd,edh->erh", expert_rows, full_up, preferred_element_type=jnp.float32)
    silu_gate = jax.nn.silu(pre_gate)
    hidden = (silu_gate * pre_up).astype(jnp.bfloat16)
    expert_out = jnp.einsum(
        "erh,ehd->erd", hidden, full_down, preferred_element_type=jnp.float32
    ).astype(jnp.bfloat16)
    returned = lax.all_to_all(
        expert_out.reshape(expert_count_axis, -1, model_width), "expert", 0, 0, tiled=True
    )
    expert_cot = dispatched[:, slot_width:].reshape(1, -1, model_width)
    back_gate, back_up, back_down = (full_gate, full_up, full_down)
    d_hidden = jnp.einsum("erd,ehd->erh", expert_cot, back_down, preferred_element_type=jnp.float32)
    gate_sigmoid = jax.nn.sigmoid(pre_gate)
    d_pre_gate = (
        d_hidden * pre_up * gate_sigmoid * (1.0 + pre_gate * (1.0 - gate_sigmoid))
    ).astype(jnp.bfloat16)
    d_pre_up = (d_hidden * silu_gate).astype(jnp.bfloat16)
    d_rows = (
        jnp.einsum("erh,edh->erd", d_pre_gate, back_gate, preferred_element_type=jnp.float32)
        + jnp.einsum("erh,edh->erd", d_pre_up, back_up, preferred_element_type=jnp.float32)
    ).astype(jnp.bfloat16)
    row_grads = lax.all_to_all(
        d_rows.reshape(expert_count_axis, -1, model_width), "expert", 0, 0, tiled=True
    )
    position_hits = chosen[:, :, :, None] == jnp.arange(block_rows, dtype=jnp.int32)
    indicator_matrix = position_hits.reshape(num_blocks, expert_count * pick_count, block_rows)
    gate_weighted_rows = to_blocks(slot_gate_values, num_blocks, pick_count)[
        :, :, None
    ] * to_blocks(returned, num_blocks, pick_count).astype(jnp.float32)
    mixed = (
        jnp.einsum(
            "wze,wzi->wei",
            indicator_matrix.astype(jnp.float32),
            gate_weighted_rows,
            precision=lax.Precision.HIGHEST,
        )
        .reshape(tok_rows, model_width)
        .astype(jnp.bfloat16)
    )
    slot_dots = jnp.sum(cot_rows.astype(jnp.float32) * returned.astype(jnp.float32), axis=2)
    dgate = jnp.einsum(
        "bept,ebp->bte",
        position_hits.astype(jnp.float32),
        slot_dots.reshape(expert_count, num_blocks, pick_count),
        precision=lax.Precision.HIGHEST,
    ).reshape(tok_rows, expert_count)
    d_logit = (dgate * gate_values * (1.0 - gate_values)).astype(jnp.bfloat16)
    gathered_grads = jnp.einsum(
        "wze,wzi->wei",
        indicator_matrix.astype(jnp.bfloat16),
        to_blocks(row_grads, num_blocks, pick_count),
        preferred_element_type=jnp.float32,
    ).reshape(tok_rows, model_width)
    grad_tokens = (
        gathered_grads + jnp.dot(d_logit, w_router.T, preferred_element_type=jnp.float32)
    ).astype(jnp.bfloat16)
    router_full = jnp.dot(tokens.T, d_logit, preferred_element_type=jnp.float32)
    devices = n * expert_count_axis
    router_part = jnp.sum(
        lax.all_to_all(router_full.reshape(devices, -1), ("dp", "expert"), 0, 0, tiled=True),
        axis=0,
    )
    grad_gate, grad_up, down_weight_gradient = weight_grads(
        expert_rows, hidden, expert_cot, d_pre_gate, d_pre_up, n
    )
    grad_router = lax.all_to_all(
        jnp.broadcast_to(router_part[None], (devices,) + router_part.shape),
        ("dp", "expert"),
        0,
        0,
        tiled=True,
    ).reshape(router_full.shape)
    return (mixed, grad_tokens, grad_gate, grad_up, down_weight_gradient, grad_router)


def solution(mesh):
    placed = (
        P(("dp", "expert"), None),
        P(("dp", "expert"), None),
        P(("dp", "expert"), None, None),
        P(),
        P("expert", "dp", None),
        P("expert", "dp", None),
        P("expert", "dp", None),
    )
    return jax.shard_map(
        body,
        mesh=mesh,
        in_specs=placed,
        out_specs=(
            P(("dp", "expert"), None),
            P(("dp", "expert"), None),
            P("expert", "dp", None),
            P("expert", "dp", None),
            P("expert", "dp", None),
            P(),
        ),
        check_vma=False,
    )
```

```python
import functools

import jax
import jax.numpy as jnp
from jax import lax
from jax.experimental import pallas as pl
from jax.experimental.pallas import tpu as pltpu
from jax.sharding import PartitionSpec as P

MESH = pl.DeviceIdType.MESH


def _gather_kernel(n, *refs):
    count = (len(refs) - 3) // 2
    srcs, dsts = refs[:count], refs[count : 2 * count]
    send_sem, recv_sem, local_sem = refs[2 * count :]
    me = lax.axis_index("dp")
    ex = lax.axis_index("expert")
    barrier = pltpu.get_barrier_semaphore()
    for k in range(1, n):
        pl.semaphore_signal(barrier, inc=1, device_id=(lax.rem(me + k, n), ex), device_id_type=MESH)
    pl.semaphore_wait(barrier, n - 1)
    copies = []
    for a in range(count):
        rows = srcs[a].shape[0]
        slot = dsts[a].at[pl.ds(me * rows, rows)]
        local = pltpu.make_async_copy(srcs[a], slot, local_sem.at[a])
        local.start()
        copies.append(local)
        for k in range(1, n):
            remote = pltpu.make_async_remote_copy(
                src_ref=srcs[a],
                dst_ref=slot,
                send_sem=send_sem.at[a, k],
                recv_sem=recv_sem.at[a, k],
                device_id=(lax.rem(me + k, n), ex),
                device_id_type=MESH,
            )
            remote.start()
            copies.append(remote)
    for c in copies:
        c.wait()


def dp_all_gather(shards, n):
    count = len(shards)
    return pl.pallas_call(
        functools.partial(_gather_kernel, n),
        out_shape=[jax.ShapeDtypeStruct((n * s.shape[0],) + s.shape[1:], s.dtype) for s in shards],
        in_specs=[pl.BlockSpec(memory_space=pl.ANY)] * count,
        out_specs=[pl.BlockSpec(memory_space=pl.ANY)] * count,
        scratch_shapes=[
            pltpu.SemaphoreType.DMA((count, n)),
            pltpu.SemaphoreType.DMA((count, n)),
            pltpu.SemaphoreType.DMA((count,)),
        ],
        compiler_params=pltpu.CompilerParams(collective_id=0, has_side_effects=True),
    )(*shards)


def _exchange_kernel(n, n_scatter, *refs):
    count = (len(refs) - 3) // 2
    srcs, dsts = refs[:count], refs[count : 2 * count]
    send_sem, recv_sem, local_sem = refs[2 * count :]
    me = lax.axis_index("dp")
    ex = lax.axis_index("expert")
    barrier = pltpu.get_barrier_semaphore()
    for k in range(1, n):
        pl.semaphore_signal(barrier, inc=1, device_id=(lax.rem(me + k, n), ex), device_id_type=MESH)
    pl.semaphore_wait(barrier, n - 1)
    copies = []
    for a in range(count):
        rows = dsts[a].shape[1]
        if a < n_scatter:
            mine = srcs[a].at[pl.ds(me * rows, rows)]
        else:
            mine = srcs[a]
        local = pltpu.make_async_copy(mine, dsts[a].at[me], local_sem.at[a])
        local.start()
        copies.append(local)
        for k in range(1, n):
            peer = lax.rem(me + k, n)
            if a < n_scatter:
                part = srcs[a].at[pl.ds(peer * rows, rows)]
            else:
                part = srcs[a]
            remote = pltpu.make_async_remote_copy(
                src_ref=part,
                dst_ref=dsts[a].at[me],
                send_sem=send_sem.at[a, k],
                recv_sem=recv_sem.at[a, k],
                device_id=(peer, ex),
                device_id_type=MESH,
            )
            remote.start()
            copies.append(remote)
    for c in copies:
        c.wait()


def dp_exchange(partials, replicas, n):
    arrays = list(partials) + list(replicas)
    count = len(arrays)
    shapes = [(n, p.shape[0] // n) + p.shape[1:] for p in partials]
    shapes += [(n,) + r.shape for r in replicas]
    received = pl.pallas_call(
        functools.partial(_exchange_kernel, n, len(partials)),
        out_shape=[jax.ShapeDtypeStruct(s, a.dtype) for s, a in zip(shapes, arrays)],
        in_specs=[pl.BlockSpec(memory_space=pl.ANY)] * count,
        out_specs=[pl.BlockSpec(memory_space=pl.ANY)] * count,
        scratch_shapes=[
            pltpu.SemaphoreType.DMA((count, n)),
            pltpu.SemaphoreType.DMA((count, n)),
            pltpu.SemaphoreType.DMA((count,)),
        ],
        compiler_params=pltpu.CompilerParams(collective_id=1, has_side_effects=True),
    )(*arrays)
    return [jnp.sum(r.astype(jnp.float32), axis=0) for r in received]


def _shift_pairs(n, k):
    return [(i, (i + k) % n) for i in range(n)]


def dp_gather_permute(shard, n):
    me = lax.axis_index("dp")
    full = jnp.zeros((n,) + shard.shape, shard.dtype)
    full = lax.dynamic_update_index_in_dim(full, shard, me, 0)
    for k in range(1, n):
        got = lax.ppermute(shard, "dp", perm=_shift_pairs(n, k))
        full = lax.dynamic_update_index_in_dim(full, got, lax.rem(me + n - k, n), 0)
    return full


def dp_scatter_permute(partial, n):
    me = lax.axis_index("dp")
    blocks = partial.reshape((n, partial.shape[0] // n) + partial.shape[1:])
    total = lax.dynamic_index_in_dim(blocks, me, 0, keepdims=False).astype(jnp.float32)
    for k in range(1, n):
        piece = lax.dynamic_index_in_dim(blocks, lax.rem(me + k, n), 0, keepdims=False)
        got = lax.ppermute(piece, "dp", perm=_shift_pairs(n, k))
        total = total + got.astype(jnp.float32)
    return total


def _x_shift(n, d):
    return [(i, (i + 2 * d) % n) for i in range(n)]


def _y_pair(n):
    return [(i, i ^ 1) for i in range(n)]


def x_ring_gather(t, n):
    from_left = lax.ppermute(t, "dp", _x_shift(n, 1))
    from_right = lax.ppermute(t, "dp", _x_shift(n, -1))
    h = t.shape[0] // 2
    first = lax.ppermute(from_left[:h], "dp", _x_shift(n, 1))
    second = lax.ppermute(from_right[h:], "dp", _x_shift(n, -1))
    return [t, from_right, jnp.concatenate([first, second], axis=0), from_left]


def dp_gather_2d(t, n):
    assert n == 8
    me = lax.axis_index("dp")
    x, l, nx = me // 2, me % 2, n // 2
    partner = lax.ppermute(t, "dp", _y_pair(n))
    stacked = jnp.stack(x_ring_gather(t, n) + x_ring_gather(partner, n))
    p = jnp.arange(n, dtype=jnp.int32)
    order = (p // 2 - x) % nx + nx * (p % 2 != l).astype(jnp.int32)
    return jnp.take(stacked, order, axis=0)


def x_ring_scatter(blocks, n):
    h = blocks[0].shape[0] // 2
    low = lax.ppermute(blocks[2][:h].astype(jnp.bfloat16), "dp", _x_shift(n, 1))
    high = lax.ppermute(blocks[2][h:].astype(jnp.bfloat16), "dp", _x_shift(n, -1))
    to_right = jnp.concatenate([blocks[1][:h] + low.astype(jnp.float32), blocks[1][h:]], axis=0)
    to_left = jnp.concatenate([blocks[3][:h], blocks[3][h:] + high.astype(jnp.float32)], axis=0)
    from_left = lax.ppermute(to_right.astype(jnp.bfloat16), "dp", _x_shift(n, 1))
    from_right = lax.ppermute(to_left.astype(jnp.bfloat16), "dp", _x_shift(n, -1))
    return blocks[0] + from_left.astype(jnp.float32) + from_right.astype(jnp.float32)


def dp_scatter_2d(partial, n):
    assert n == 8
    me = lax.axis_index("dp")
    x, l, nx = me // 2, me % 2, n // 2
    blocks = partial.reshape((n, partial.shape[0] // n) + partial.shape[1:])

    def pick(m, side):
        index = 2 * ((x + m) % nx) + side
        return lax.dynamic_index_in_dim(blocks, index, 0, keepdims=False).astype(jnp.float32)

    partner_sum = x_ring_scatter([pick(m, 1 - l) for m in range(nx)], n)
    sent = lax.ppermute(partner_sum.astype(jnp.bfloat16), "dp", _y_pair(n))
    own_sum = x_ring_scatter([pick(m, l) for m in range(nx)], n)
    return own_sum + sent.astype(jnp.float32)


def _ring_gather_kernel(n, *refs):
    count = (len(refs) - 3) // 2
    shards, outs = refs[:count], refs[count : 2 * count]
    send_sem, recv_sem, local_sem = refs[2 * count :]
    me = lax.axis_index("dp")
    ex = lax.axis_index("expert")
    right, left, partner = lax.rem(me + 2, n), lax.rem(me + n - 2, n), me + 1 - 2 * lax.rem(me, 2)
    barrier = pltpu.get_barrier_semaphore()
    for peer in (right, left, partner):
        pl.semaphore_signal(barrier, inc=1, device_id=(peer, ex), device_id_type=MESH)
    pl.semaphore_wait(barrier, 3)

    def send(a, role, src, slot, rows, peer):
        copy = pltpu.make_async_remote_copy(
            src_ref=src,
            dst_ref=outs[a].at[slot, rows],
            send_sem=send_sem.at[a, role],
            recv_sem=recv_sem.at[a, role],
            device_id=(peer, ex),
            device_id_type=MESH,
        )
        copy.start()
        return copy

    spans = []
    for a in range(count):
        half = shards[a].shape[0] // 2
        spans.append((pl.ds(0, 2 * half), pl.ds(0, half), pl.ds(half, half)))
    locals_, first, second, third = [], [], [], []
    for a in range(count):
        local = pltpu.make_async_copy(shards[a], outs[a].at[me], local_sem.at[a])
        local.start()
        locals_.append(local)
        whole = spans[a][0]
        first += [
            send(a, 0, shards[a], me, whole, right),
            send(a, 1, shards[a], me, whole, left),
            send(a, 2, shards[a], me, whole, partner),
        ]
    for copy in first:
        copy.wait_recv()
    mate = partner
    for a in range(count):
        whole, low, high = spans[a]
        second += [
            send(a, 3, outs[a].at[left, low], left, low, right),
            send(a, 4, outs[a].at[right, high], right, high, left),
            send(a, 5, outs[a].at[mate], mate, whole, right),
            send(a, 6, outs[a].at[mate], mate, whole, left),
        ]
    for a in range(count):
        second[4 * a + 2].wait_recv()
        second[4 * a + 3].wait_recv()
    mate_left, mate_right = lax.rem(mate + n - 2, n), lax.rem(mate + 2, n)
    for a in range(count):
        whole, low, high = spans[a]
        third += [
            send(a, 7, outs[a].at[mate_left, low], mate_left, low, right),
            send(a, 8, outs[a].at[mate_right, high], mate_right, high, left),
        ]
    for copy in first:
        copy.wait_send()
    for a in range(count):
        second[4 * a].wait_recv()
        second[4 * a + 1].wait_recv()
    for copy in second:
        copy.wait_send()
    for copy in third:
        copy.wait_recv()
        copy.wait_send()
    for local in locals_:
        local.wait()


def dp_gather_kernel(shards, n):
    assert n == 8
    count = len(shards)
    return pl.pallas_call(
        functools.partial(_ring_gather_kernel, n),
        out_shape=[jax.ShapeDtypeStruct((n,) + s.shape, s.dtype) for s in shards],
        in_specs=[pl.BlockSpec(memory_space=pl.ANY)] * count,
        out_specs=[pl.BlockSpec(memory_space=pl.ANY)] * count,
        scratch_shapes=[
            pltpu.SemaphoreType.DMA((count, 9)),
            pltpu.SemaphoreType.DMA((count, 9)),
            pltpu.SemaphoreType.DMA((count,)),
        ],
        compiler_params=pltpu.CompilerParams(collective_id=2, has_side_effects=True),
    )(*shards)


def to_blocks(slot_array, num_blocks, pick_count):
    expert_count = slot_array.shape[0]
    trailing = slot_array.shape[2:]
    grouped = slot_array.reshape((expert_count, num_blocks, pick_count) + trailing)
    axis_order = (1, 0, 2) + tuple(range(3, 3 + len(trailing)))
    return jnp.transpose(grouped, axis_order).reshape(
        (num_blocks, expert_count * pick_count) + trailing
    )


def weight_grads(expert_rows, hidden, expert_cot, d_pre_gate, d_pre_up, n):
    hidden_activations = hidden.shape[2]
    out_part = jnp.einsum(
        "erc,erd->cd", hidden, expert_cot, preferred_element_type=jnp.float32
    ).astype(jnp.bfloat16)
    out_share = dp_scatter_2d(out_part, n)
    both_grads = jnp.concatenate([d_pre_gate, d_pre_up], axis=2)
    in_part = jnp.einsum(
        "erc,erk->ck", expert_rows, both_grads, preferred_element_type=jnp.float32
    ).astype(jnp.bfloat16)
    in_share = dp_scatter_2d(in_part, n)
    grad_gate = in_share[None, :, :hidden_activations]
    grad_up = in_share[None, :, hidden_activations:]
    down_weight_gradient = out_share[None]
    return (grad_gate, grad_up, down_weight_gradient)


def body(tokens, cotangent, chosen, w_router, w_gate, w_up, w_down):
    tok_rows, model_width = tokens.shape
    num_blocks, expert_count, pick_count = chosen.shape
    block_rows = tok_rows // num_blocks
    slot_count = num_blocks * pick_count
    logits = jnp.dot(tokens, w_router, preferred_element_type=jnp.float32)
    gate_values = jax.nn.sigmoid(logits)
    offsets = (jnp.arange(num_blocks, dtype=jnp.int32) * block_rows)[:, None, None]
    slot_rows = jnp.transpose(chosen + offsets, (1, 0, 2)).reshape(expert_count, slot_count)
    picked = tokens[slot_rows]
    slot_gate_values = jnp.take_along_axis(gate_values.T, slot_rows, axis=1)
    cot_rows = cotangent[slot_rows]
    scaled_cot = (slot_gate_values[:, :, None] * cot_rows.astype(jnp.float32)).astype(jnp.bfloat16)
    n = lax.axis_size("dp")
    full_gate, full_up, full_down = (
        g.reshape((1, -1) + g.shape[2:])
        for g in dp_gather_kernel([w_gate[0], w_up[0], w_down[0]], n)
    )
    expert_count_axis = lax.axis_size("expert")
    dispatched = lax.all_to_all(
        jnp.concatenate([picked, scaled_cot], axis=1), "expert", 0, 0, tiled=True
    )
    slot_width = picked.shape[1]
    expert_rows = dispatched[:, :slot_width].reshape(1, -1, model_width)
    pre_gate = jnp.einsum(
        "erd,edh->erh", expert_rows, full_gate, preferred_element_type=jnp.float32
    )
    pre_up = jnp.einsum("erd,edh->erh", expert_rows, full_up, preferred_element_type=jnp.float32)
    silu_gate = jax.nn.silu(pre_gate)
    hidden = (silu_gate * pre_up).astype(jnp.bfloat16)
    expert_out = jnp.einsum(
        "erh,ehd->erd", hidden, full_down, preferred_element_type=jnp.float32
    ).astype(jnp.bfloat16)
    returned = lax.all_to_all(
        expert_out.reshape(expert_count_axis, -1, model_width), "expert", 0, 0, tiled=True
    )
    expert_cot = dispatched[:, slot_width:].reshape(1, -1, model_width)
    back_gate, back_up, back_down = (full_gate, full_up, full_down)
    d_hidden = jnp.einsum("erd,ehd->erh", expert_cot, back_down, preferred_element_type=jnp.float32)
    position_hits = chosen[:, :, :, None] == jnp.arange(block_rows, dtype=jnp.int32)
    slot_dots = jnp.sum(cot_rows.astype(jnp.float32) * returned.astype(jnp.float32), axis=2)
    dgate = jnp.einsum(
        "bept,ebp->bte",
        position_hits.astype(jnp.float32),
        slot_dots.reshape(expert_count, num_blocks, pick_count),
        precision=lax.Precision.HIGHEST,
    ).reshape(tok_rows, expert_count)
    d_logit = (dgate * gate_values * (1.0 - gate_values)).astype(jnp.bfloat16)
    router_full = jnp.dot(tokens.T, d_logit, preferred_element_type=jnp.float32)
    devices = n * expert_count_axis
    router_part = jnp.sum(
        lax.all_to_all(router_full.reshape(devices, -1), ("dp", "expert"), 0, 0, tiled=True),
        axis=0,
    )
    router_full, d_hidden = lax.optimization_barrier((router_full, d_hidden))
    gate_sigmoid = jax.nn.sigmoid(pre_gate)
    d_pre_gate = (
        d_hidden * pre_up * gate_sigmoid * (1.0 + pre_gate * (1.0 - gate_sigmoid))
    ).astype(jnp.bfloat16)
    d_pre_up = (d_hidden * silu_gate).astype(jnp.bfloat16)
    d_rows = (
        jnp.einsum("erh,edh->erd", d_pre_gate, back_gate, preferred_element_type=jnp.float32)
        + jnp.einsum("erh,edh->erd", d_pre_up, back_up, preferred_element_type=jnp.float32)
    ).astype(jnp.bfloat16)
    row_grads = lax.all_to_all(
        d_rows.reshape(expert_count_axis, -1, model_width), "expert", 0, 0, tiled=True
    )
    indicator_matrix = position_hits.reshape(num_blocks, expert_count * pick_count, block_rows)
    gate_weighted_rows = to_blocks(slot_gate_values, num_blocks, pick_count)[
        :, :, None
    ] * to_blocks(returned, num_blocks, pick_count).astype(jnp.float32)
    mixed = (
        jnp.einsum(
            "wze,wzi->wei",
            indicator_matrix.astype(jnp.float32),
            gate_weighted_rows,
            precision=lax.Precision.HIGHEST,
        )
        .reshape(tok_rows, model_width)
        .astype(jnp.bfloat16)
    )
    gathered_grads = jnp.einsum(
        "wze,wzi->wei",
        indicator_matrix.astype(jnp.bfloat16),
        to_blocks(row_grads, num_blocks, pick_count),
        preferred_element_type=jnp.float32,
    ).reshape(tok_rows, model_width)
    grad_tokens = (
        gathered_grads + jnp.dot(d_logit, w_router.T, preferred_element_type=jnp.float32)
    ).astype(jnp.bfloat16)
    grad_gate, grad_up, down_weight_gradient = weight_grads(
        expert_rows, hidden, expert_cot, d_pre_gate, d_pre_up, n
    )
    grad_router = lax.all_to_all(
        jnp.broadcast_to(router_part[None], (devices,) + router_part.shape),
        ("dp", "expert"),
        0,
        0,
        tiled=True,
    ).reshape(router_full.shape)
    return (mixed, grad_tokens, grad_gate, grad_up, down_weight_gradient, grad_router)


def solution(mesh):
    placed = (
        P(("dp", "expert"), None),
        P(("dp", "expert"), None),
        P(("dp", "expert"), None, None),
        P(),
        P("expert", "dp", None),
        P("expert", "dp", None),
        P("expert", "dp", None),
    )
    return jax.shard_map(
        body,
        mesh=mesh,
        in_specs=placed,
        out_specs=(
            P(("dp", "expert"), None),
            P(("dp", "expert"), None),
            P("expert", "dp", None),
            P("expert", "dp", None),
            P("expert", "dp", None),
            P(),
        ),
        check_vma=False,
    )
```

```python
import functools

import jax
import jax.numpy as jnp
from jax import lax
from jax.experimental import pallas as pl
from jax.experimental.pallas import tpu as pltpu
from jax.sharding import PartitionSpec as P

MESH = pl.DeviceIdType.MESH


def _gather_kernel(n, *refs):
    count = (len(refs) - 3) // 2
    srcs, dsts = refs[:count], refs[count : 2 * count]
    send_sem, recv_sem, local_sem = refs[2 * count :]
    me = lax.axis_index("dp")
    ex = lax.axis_index("expert")
    barrier = pltpu.get_barrier_semaphore()
    for k in range(1, n):
        pl.semaphore_signal(barrier, inc=1, device_id=(lax.rem(me + k, n), ex), device_id_type=MESH)
    pl.semaphore_wait(barrier, n - 1)
    copies = []
    for a in range(count):
        rows = srcs[a].shape[0]
        slot = dsts[a].at[pl.ds(me * rows, rows)]
        local = pltpu.make_async_copy(srcs[a], slot, local_sem.at[a])
        local.start()
        copies.append(local)
        for k in range(1, n):
            remote = pltpu.make_async_remote_copy(
                src_ref=srcs[a],
                dst_ref=slot,
                send_sem=send_sem.at[a, k],
                recv_sem=recv_sem.at[a, k],
                device_id=(lax.rem(me + k, n), ex),
                device_id_type=MESH,
            )
            remote.start()
            copies.append(remote)
    for c in copies:
        c.wait()


def dp_all_gather(shards, n):
    count = len(shards)
    return pl.pallas_call(
        functools.partial(_gather_kernel, n),
        out_shape=[jax.ShapeDtypeStruct((n * s.shape[0],) + s.shape[1:], s.dtype) for s in shards],
        in_specs=[pl.BlockSpec(memory_space=pl.ANY)] * count,
        out_specs=[pl.BlockSpec(memory_space=pl.ANY)] * count,
        scratch_shapes=[
            pltpu.SemaphoreType.DMA((count, n)),
            pltpu.SemaphoreType.DMA((count, n)),
            pltpu.SemaphoreType.DMA((count,)),
        ],
        compiler_params=pltpu.CompilerParams(collective_id=0, has_side_effects=True),
    )(*shards)


def _exchange_kernel(n, n_scatter, *refs):
    count = (len(refs) - 3) // 2
    srcs, dsts = refs[:count], refs[count : 2 * count]
    send_sem, recv_sem, local_sem = refs[2 * count :]
    me = lax.axis_index("dp")
    ex = lax.axis_index("expert")
    barrier = pltpu.get_barrier_semaphore()
    for k in range(1, n):
        pl.semaphore_signal(barrier, inc=1, device_id=(lax.rem(me + k, n), ex), device_id_type=MESH)
    pl.semaphore_wait(barrier, n - 1)
    copies = []
    for a in range(count):
        rows = dsts[a].shape[1]
        if a < n_scatter:
            mine = srcs[a].at[pl.ds(me * rows, rows)]
        else:
            mine = srcs[a]
        local = pltpu.make_async_copy(mine, dsts[a].at[me], local_sem.at[a])
        local.start()
        copies.append(local)
        for k in range(1, n):
            peer = lax.rem(me + k, n)
            if a < n_scatter:
                part = srcs[a].at[pl.ds(peer * rows, rows)]
            else:
                part = srcs[a]
            remote = pltpu.make_async_remote_copy(
                src_ref=part,
                dst_ref=dsts[a].at[me],
                send_sem=send_sem.at[a, k],
                recv_sem=recv_sem.at[a, k],
                device_id=(peer, ex),
                device_id_type=MESH,
            )
            remote.start()
            copies.append(remote)
    for c in copies:
        c.wait()


def dp_exchange(partials, replicas, n):
    arrays = list(partials) + list(replicas)
    count = len(arrays)
    shapes = [(n, p.shape[0] // n) + p.shape[1:] for p in partials]
    shapes += [(n,) + r.shape for r in replicas]
    received = pl.pallas_call(
        functools.partial(_exchange_kernel, n, len(partials)),
        out_shape=[jax.ShapeDtypeStruct(s, a.dtype) for s, a in zip(shapes, arrays)],
        in_specs=[pl.BlockSpec(memory_space=pl.ANY)] * count,
        out_specs=[pl.BlockSpec(memory_space=pl.ANY)] * count,
        scratch_shapes=[
            pltpu.SemaphoreType.DMA((count, n)),
            pltpu.SemaphoreType.DMA((count, n)),
            pltpu.SemaphoreType.DMA((count,)),
        ],
        compiler_params=pltpu.CompilerParams(collective_id=1, has_side_effects=True),
    )(*arrays)
    return [jnp.sum(r.astype(jnp.float32), axis=0) for r in received]


def _shift_pairs(n, k):
    return [(i, (i + k) % n) for i in range(n)]


def dp_gather_permute(shard, n):
    me = lax.axis_index("dp")
    full = jnp.zeros((n,) + shard.shape, shard.dtype)
    full = lax.dynamic_update_index_in_dim(full, shard, me, 0)
    for k in range(1, n):
        got = lax.ppermute(shard, "dp", perm=_shift_pairs(n, k))
        full = lax.dynamic_update_index_in_dim(full, got, lax.rem(me + n - k, n), 0)
    return full


def dp_scatter_permute(partial, n):
    me = lax.axis_index("dp")
    blocks = partial.reshape((n, partial.shape[0] // n) + partial.shape[1:])
    total = lax.dynamic_index_in_dim(blocks, me, 0, keepdims=False).astype(jnp.float32)
    for k in range(1, n):
        piece = lax.dynamic_index_in_dim(blocks, lax.rem(me + k, n), 0, keepdims=False)
        got = lax.ppermute(piece, "dp", perm=_shift_pairs(n, k))
        total = total + got.astype(jnp.float32)
    return total


def _x_shift(n, d):
    return [(i, (i + 2 * d) % n) for i in range(n)]


def _y_pair(n):
    return [(i, i ^ 1) for i in range(n)]


def x_ring_gather(t, n):
    from_left = lax.ppermute(t, "dp", _x_shift(n, 1))
    from_right = lax.ppermute(t, "dp", _x_shift(n, -1))
    h = t.shape[0] // 2
    first = lax.ppermute(from_left[:h], "dp", _x_shift(n, 1))
    second = lax.ppermute(from_right[h:], "dp", _x_shift(n, -1))
    return [t, from_right, jnp.concatenate([first, second], axis=0), from_left]


def dp_gather_2d(t, n):
    assert n == 8
    me = lax.axis_index("dp")
    x, l, nx = me // 2, me % 2, n // 2
    partner = lax.ppermute(t, "dp", _y_pair(n))
    stacked = jnp.stack(x_ring_gather(t, n) + x_ring_gather(partner, n))
    p = jnp.arange(n, dtype=jnp.int32)
    order = (p // 2 - x) % nx + nx * (p % 2 != l).astype(jnp.int32)
    return jnp.take(stacked, order, axis=0)


def x_ring_scatter(blocks, n):
    h = blocks[0].shape[0] // 2
    low = lax.ppermute(blocks[2][:h].astype(jnp.bfloat16), "dp", _x_shift(n, 1))
    high = lax.ppermute(blocks[2][h:].astype(jnp.bfloat16), "dp", _x_shift(n, -1))
    to_right = jnp.concatenate([blocks[1][:h] + low.astype(jnp.float32), blocks[1][h:]], axis=0)
    to_left = jnp.concatenate([blocks[3][:h], blocks[3][h:] + high.astype(jnp.float32)], axis=0)
    from_left = lax.ppermute(to_right.astype(jnp.bfloat16), "dp", _x_shift(n, 1))
    from_right = lax.ppermute(to_left.astype(jnp.bfloat16), "dp", _x_shift(n, -1))
    return blocks[0] + from_left.astype(jnp.float32) + from_right.astype(jnp.float32)


def dp_scatter_2d(partial, n):
    assert n == 8
    me = lax.axis_index("dp")
    x, l, nx = me // 2, me % 2, n // 2
    blocks = partial.reshape((n, partial.shape[0] // n) + partial.shape[1:])

    def pick(m, side):
        index = 2 * ((x + m) % nx) + side
        return lax.dynamic_index_in_dim(blocks, index, 0, keepdims=False).astype(jnp.float32)

    partner_sum = x_ring_scatter([pick(m, 1 - l) for m in range(nx)], n)
    sent = lax.ppermute(partner_sum.astype(jnp.bfloat16), "dp", _y_pair(n))
    own_sum = x_ring_scatter([pick(m, l) for m in range(nx)], n)
    return own_sum + sent.astype(jnp.float32)


def _ring_gather_kernel(n, *refs):
    count = (len(refs) - 3) // 2
    shards, outs = refs[:count], refs[count : 2 * count]
    send_sem, recv_sem, local_sem = refs[2 * count :]
    me = lax.axis_index("dp")
    ex = lax.axis_index("expert")
    right, left, partner = lax.rem(me + 2, n), lax.rem(me + n - 2, n), me + 1 - 2 * lax.rem(me, 2)
    barrier = pltpu.get_barrier_semaphore()
    for peer in (right, left, partner):
        pl.semaphore_signal(barrier, inc=1, device_id=(peer, ex), device_id_type=MESH)
    pl.semaphore_wait(barrier, 3)

    def send(a, role, src, slot, rows, peer):
        copy = pltpu.make_async_remote_copy(
            src_ref=src,
            dst_ref=outs[a].at[slot, rows],
            send_sem=send_sem.at[a, role],
            recv_sem=recv_sem.at[a, role],
            device_id=(peer, ex),
            device_id_type=MESH,
        )
        copy.start()
        return copy

    spans = []
    for a in range(count):
        half = shards[a].shape[0] // 2
        spans.append((pl.ds(0, 2 * half), pl.ds(0, half), pl.ds(half, half)))
    locals_, first, second, third = [], [], [], []
    for a in range(count):
        local = pltpu.make_async_copy(shards[a], outs[a].at[me], local_sem.at[a])
        local.start()
        locals_.append(local)
        whole = spans[a][0]
        first += [
            send(a, 0, shards[a], me, whole, right),
            send(a, 1, shards[a], me, whole, left),
            send(a, 2, shards[a], me, whole, partner),
        ]
    mate = partner
    for a in range(count):
        whole, low, high = spans[a]
        first[3 * a].wait_recv()
        to_right = send(a, 3, outs[a].at[left, low], left, low, right)
        first[3 * a + 1].wait_recv()
        to_left = send(a, 4, outs[a].at[right, high], right, high, left)
        second += [to_right, to_left]
    for a in range(count):
        whole = spans[a][0]
        first[3 * a + 2].wait_recv()
        second += [
            send(a, 5, outs[a].at[mate], mate, whole, right),
            send(a, 6, outs[a].at[mate], mate, whole, left),
        ]
    forwards, mates = second[: 2 * count], second[2 * count :]
    for copy in mates:
        copy.wait_recv()
    mate_left, mate_right = lax.rem(mate + n - 2, n), lax.rem(mate + 2, n)
    for a in range(count):
        whole, low, high = spans[a]
        third += [
            send(a, 7, outs[a].at[mate_left, low], mate_left, low, right),
            send(a, 8, outs[a].at[mate_right, high], mate_right, high, left),
        ]
    for copy in first:
        copy.wait_send()
    for copy in forwards:
        copy.wait_recv()
    for copy in second:
        copy.wait_send()
    for copy in third:
        copy.wait_recv()
        copy.wait_send()
    for local in locals_:
        local.wait()


def dp_gather_kernel(shards, n):
    assert n == 8
    count = len(shards)
    return pl.pallas_call(
        functools.partial(_ring_gather_kernel, n),
        out_shape=[jax.ShapeDtypeStruct((n,) + s.shape, s.dtype) for s in shards],
        in_specs=[pl.BlockSpec(memory_space=pl.ANY)] * count,
        out_specs=[pl.BlockSpec(memory_space=pl.ANY)] * count,
        scratch_shapes=[
            pltpu.SemaphoreType.DMA((count, 9)),
            pltpu.SemaphoreType.DMA((count, 9)),
            pltpu.SemaphoreType.DMA((count,)),
        ],
        compiler_params=pltpu.CompilerParams(collective_id=2, has_side_effects=True),
    )(*shards)


def to_blocks(slot_array, num_blocks, pick_count):
    expert_count = slot_array.shape[0]
    trailing = slot_array.shape[2:]
    grouped = slot_array.reshape((expert_count, num_blocks, pick_count) + trailing)
    axis_order = (1, 0, 2) + tuple(range(3, 3 + len(trailing)))
    return jnp.transpose(grouped, axis_order).reshape(
        (num_blocks, expert_count * pick_count) + trailing
    )


def weight_grads(expert_rows, hidden, expert_cot, d_pre_gate, d_pre_up, n):
    hidden_activations = hidden.shape[2]
    out_part = jnp.einsum(
        "erc,erd->cd", hidden, expert_cot, preferred_element_type=jnp.float32
    ).astype(jnp.bfloat16)
    out_share = dp_scatter_2d(out_part, n)
    both_grads = jnp.concatenate([d_pre_gate, d_pre_up], axis=2)
    in_part = jnp.einsum(
        "erc,erk->ck", expert_rows, both_grads, preferred_element_type=jnp.float32
    ).astype(jnp.bfloat16)
    in_share = dp_scatter_2d(in_part, n)
    grad_gate = in_share[None, :, :hidden_activations]
    grad_up = in_share[None, :, hidden_activations:]
    down_weight_gradient = out_share[None]
    return (grad_gate, grad_up, down_weight_gradient)


def body(tokens, cotangent, chosen, w_router, w_gate, w_up, w_down):
    tok_rows, model_width = tokens.shape
    num_blocks, expert_count, pick_count = chosen.shape
    block_rows = tok_rows // num_blocks
    slot_count = num_blocks * pick_count
    logits = jnp.dot(tokens, w_router, preferred_element_type=jnp.float32)
    gate_values = jax.nn.sigmoid(logits)
    offsets = (jnp.arange(num_blocks, dtype=jnp.int32) * block_rows)[:, None, None]
    slot_rows = jnp.transpose(chosen + offsets, (1, 0, 2)).reshape(expert_count, slot_count)
    picked = tokens[slot_rows]
    slot_gate_values = jnp.take_along_axis(gate_values.T, slot_rows, axis=1)
    cot_rows = cotangent[slot_rows]
    scaled_cot = (slot_gate_values[:, :, None] * cot_rows.astype(jnp.float32)).astype(jnp.bfloat16)
    n = lax.axis_size("dp")
    full_gate, full_up, full_down = (
        g.reshape((1, -1) + g.shape[2:])
        for g in dp_gather_kernel([w_gate[0], w_up[0], w_down[0]], n)
    )
    expert_count_axis = lax.axis_size("expert")
    dispatched = lax.all_to_all(
        jnp.concatenate([picked, scaled_cot], axis=1), "expert", 0, 0, tiled=True
    )
    slot_width = picked.shape[1]
    expert_rows = dispatched[:, :slot_width].reshape(1, -1, model_width)
    pre_gate = jnp.einsum(
        "erd,edh->erh", expert_rows, full_gate, preferred_element_type=jnp.float32
    )
    pre_up = jnp.einsum("erd,edh->erh", expert_rows, full_up, preferred_element_type=jnp.float32)
    silu_gate = jax.nn.silu(pre_gate)
    hidden = (silu_gate * pre_up).astype(jnp.bfloat16)
    expert_out = jnp.einsum(
        "erh,ehd->erd", hidden, full_down, preferred_element_type=jnp.float32
    ).astype(jnp.bfloat16)
    returned = lax.all_to_all(
        expert_out.reshape(expert_count_axis, -1, model_width), "expert", 0, 0, tiled=True
    )
    expert_cot = dispatched[:, slot_width:].reshape(1, -1, model_width)
    back_gate, back_up, back_down = (full_gate, full_up, full_down)
    d_hidden = jnp.einsum("erd,ehd->erh", expert_cot, back_down, preferred_element_type=jnp.float32)
    gate_sigmoid = jax.nn.sigmoid(pre_gate)
    d_pre_gate = (
        d_hidden * pre_up * gate_sigmoid * (1.0 + pre_gate * (1.0 - gate_sigmoid))
    ).astype(jnp.bfloat16)
    d_pre_up = (d_hidden * silu_gate).astype(jnp.bfloat16)
    d_rows = (
        jnp.einsum("erh,edh->erd", d_pre_gate, back_gate, preferred_element_type=jnp.float32)
        + jnp.einsum("erh,edh->erd", d_pre_up, back_up, preferred_element_type=jnp.float32)
    ).astype(jnp.bfloat16)
    row_grads = lax.all_to_all(
        d_rows.reshape(expert_count_axis, -1, model_width), "expert", 0, 0, tiled=True
    )
    position_hits = chosen[:, :, :, None] == jnp.arange(block_rows, dtype=jnp.int32)
    indicator_matrix = position_hits.reshape(num_blocks, expert_count * pick_count, block_rows)
    gate_weighted_rows = to_blocks(slot_gate_values, num_blocks, pick_count)[
        :, :, None
    ] * to_blocks(returned, num_blocks, pick_count).astype(jnp.float32)
    mixed = (
        jnp.einsum(
            "wze,wzi->wei",
            indicator_matrix.astype(jnp.float32),
            gate_weighted_rows,
            precision=lax.Precision.HIGHEST,
        )
        .reshape(tok_rows, model_width)
        .astype(jnp.bfloat16)
    )
    slot_dots = jnp.sum(cot_rows.astype(jnp.float32) * returned.astype(jnp.float32), axis=2)
    dgate = jnp.einsum(
        "bept,ebp->bte",
        position_hits.astype(jnp.float32),
        slot_dots.reshape(expert_count, num_blocks, pick_count),
        precision=lax.Precision.HIGHEST,
    ).reshape(tok_rows, expert_count)
    d_logit = (dgate * gate_values * (1.0 - gate_values)).astype(jnp.bfloat16)
    gathered_grads = jnp.einsum(
        "wze,wzi->wei",
        indicator_matrix.astype(jnp.bfloat16),
        to_blocks(row_grads, num_blocks, pick_count),
        preferred_element_type=jnp.float32,
    ).reshape(tok_rows, model_width)
    grad_tokens = (
        gathered_grads + jnp.dot(d_logit, w_router.T, preferred_element_type=jnp.float32)
    ).astype(jnp.bfloat16)
    router_full = jnp.dot(tokens.T, d_logit, preferred_element_type=jnp.float32)
    devices = n * expert_count_axis
    router_part = jnp.sum(
        lax.all_to_all(router_full.reshape(devices, -1), ("dp", "expert"), 0, 0, tiled=True),
        axis=0,
    )
    grad_gate, grad_up, down_weight_gradient = weight_grads(
        expert_rows, hidden, expert_cot, d_pre_gate, d_pre_up, n
    )
    grad_router = lax.all_to_all(
        jnp.broadcast_to(router_part[None], (devices,) + router_part.shape),
        ("dp", "expert"),
        0,
        0,
        tiled=True,
    ).reshape(router_full.shape)
    return (mixed, grad_tokens, grad_gate, grad_up, down_weight_gradient, grad_router)


def solution(mesh):
    placed = (
        P(("dp", "expert"), None),
        P(("dp", "expert"), None),
        P(("dp", "expert"), None, None),
        P(),
        P("expert", "dp", None),
        P("expert", "dp", None),
        P("expert", "dp", None),
    )
    return jax.shard_map(
        body,
        mesh=mesh,
        in_specs=placed,
        out_specs=(
            P(("dp", "expert"), None),
            P(("dp", "expert"), None),
            P("expert", "dp", None),
            P("expert", "dp", None),
            P("expert", "dp", None),
            P(),
        ),
        check_vma=False,
    )
```

```python
import functools

import jax
import jax.numpy as jnp
from jax import lax
from jax.experimental import pallas as pl
from jax.experimental.pallas import tpu as pltpu
from jax.sharding import PartitionSpec as P

MESH = pl.DeviceIdType.MESH


def _gather_kernel(n, *refs):
    count = (len(refs) - 3) // 2
    srcs, dsts = refs[:count], refs[count : 2 * count]
    send_sem, recv_sem, local_sem = refs[2 * count :]
    me = lax.axis_index("dp")
    ex = lax.axis_index("expert")
    barrier = pltpu.get_barrier_semaphore()
    for k in range(1, n):
        pl.semaphore_signal(barrier, inc=1, device_id=(lax.rem(me + k, n), ex), device_id_type=MESH)
    pl.semaphore_wait(barrier, n - 1)
    copies = []
    for a in range(count):
        rows = srcs[a].shape[0]
        slot = dsts[a].at[pl.ds(me * rows, rows)]
        local = pltpu.make_async_copy(srcs[a], slot, local_sem.at[a])
        local.start()
        copies.append(local)
        for k in range(1, n):
            remote = pltpu.make_async_remote_copy(
                src_ref=srcs[a],
                dst_ref=slot,
                send_sem=send_sem.at[a, k],
                recv_sem=recv_sem.at[a, k],
                device_id=(lax.rem(me + k, n), ex),
                device_id_type=MESH,
            )
            remote.start()
            copies.append(remote)
    for c in copies:
        c.wait()


def dp_all_gather(shards, n):
    count = len(shards)
    return pl.pallas_call(
        functools.partial(_gather_kernel, n),
        out_shape=[jax.ShapeDtypeStruct((n * s.shape[0],) + s.shape[1:], s.dtype) for s in shards],
        in_specs=[pl.BlockSpec(memory_space=pl.ANY)] * count,
        out_specs=[pl.BlockSpec(memory_space=pl.ANY)] * count,
        scratch_shapes=[
            pltpu.SemaphoreType.DMA((count, n)),
            pltpu.SemaphoreType.DMA((count, n)),
            pltpu.SemaphoreType.DMA((count,)),
        ],
        compiler_params=pltpu.CompilerParams(collective_id=0, has_side_effects=True),
    )(*shards)


def _exchange_kernel(n, n_scatter, *refs):
    count = (len(refs) - 3) // 2
    srcs, dsts = refs[:count], refs[count : 2 * count]
    send_sem, recv_sem, local_sem = refs[2 * count :]
    me = lax.axis_index("dp")
    ex = lax.axis_index("expert")
    barrier = pltpu.get_barrier_semaphore()
    for k in range(1, n):
        pl.semaphore_signal(barrier, inc=1, device_id=(lax.rem(me + k, n), ex), device_id_type=MESH)
    pl.semaphore_wait(barrier, n - 1)
    copies = []
    for a in range(count):
        rows = dsts[a].shape[1]
        if a < n_scatter:
            mine = srcs[a].at[pl.ds(me * rows, rows)]
        else:
            mine = srcs[a]
        local = pltpu.make_async_copy(mine, dsts[a].at[me], local_sem.at[a])
        local.start()
        copies.append(local)
        for k in range(1, n):
            peer = lax.rem(me + k, n)
            if a < n_scatter:
                part = srcs[a].at[pl.ds(peer * rows, rows)]
            else:
                part = srcs[a]
            remote = pltpu.make_async_remote_copy(
                src_ref=part,
                dst_ref=dsts[a].at[me],
                send_sem=send_sem.at[a, k],
                recv_sem=recv_sem.at[a, k],
                device_id=(peer, ex),
                device_id_type=MESH,
            )
            remote.start()
            copies.append(remote)
    for c in copies:
        c.wait()


def dp_exchange(partials, replicas, n):
    arrays = list(partials) + list(replicas)
    count = len(arrays)
    shapes = [(n, p.shape[0] // n) + p.shape[1:] for p in partials]
    shapes += [(n,) + r.shape for r in replicas]
    received = pl.pallas_call(
        functools.partial(_exchange_kernel, n, len(partials)),
        out_shape=[jax.ShapeDtypeStruct(s, a.dtype) for s, a in zip(shapes, arrays)],
        in_specs=[pl.BlockSpec(memory_space=pl.ANY)] * count,
        out_specs=[pl.BlockSpec(memory_space=pl.ANY)] * count,
        scratch_shapes=[
            pltpu.SemaphoreType.DMA((count, n)),
            pltpu.SemaphoreType.DMA((count, n)),
            pltpu.SemaphoreType.DMA((count,)),
        ],
        compiler_params=pltpu.CompilerParams(collective_id=1, has_side_effects=True),
    )(*arrays)
    return [jnp.sum(r.astype(jnp.float32), axis=0) for r in received]


def _shift_pairs(n, k):
    return [(i, (i + k) % n) for i in range(n)]


def dp_gather_permute(shard, n):
    me = lax.axis_index("dp")
    full = jnp.zeros((n,) + shard.shape, shard.dtype)
    full = lax.dynamic_update_index_in_dim(full, shard, me, 0)
    for k in range(1, n):
        got = lax.ppermute(shard, "dp", perm=_shift_pairs(n, k))
        full = lax.dynamic_update_index_in_dim(full, got, lax.rem(me + n - k, n), 0)
    return full


def dp_scatter_permute(partial, n):
    me = lax.axis_index("dp")
    blocks = partial.reshape((n, partial.shape[0] // n) + partial.shape[1:])
    total = lax.dynamic_index_in_dim(blocks, me, 0, keepdims=False).astype(jnp.float32)
    for k in range(1, n):
        piece = lax.dynamic_index_in_dim(blocks, lax.rem(me + k, n), 0, keepdims=False)
        got = lax.ppermute(piece, "dp", perm=_shift_pairs(n, k))
        total = total + got.astype(jnp.float32)
    return total


def _x_shift(n, d):
    return [(i, (i + 2 * d) % n) for i in range(n)]


def _y_pair(n):
    return [(i, i ^ 1) for i in range(n)]


def x_ring_gather(t, n):
    from_left = lax.ppermute(t, "dp", _x_shift(n, 1))
    from_right = lax.ppermute(t, "dp", _x_shift(n, -1))
    h = t.shape[0] // 2
    first = lax.ppermute(from_left[:h], "dp", _x_shift(n, 1))
    second = lax.ppermute(from_right[h:], "dp", _x_shift(n, -1))
    return [t, from_right, jnp.concatenate([first, second], axis=0), from_left]


def dp_gather_2d(t, n):
    assert n == 8
    me = lax.axis_index("dp")
    x, l, nx = me // 2, me % 2, n // 2
    partner = lax.ppermute(t, "dp", _y_pair(n))
    stacked = jnp.stack(x_ring_gather(t, n) + x_ring_gather(partner, n))
    p = jnp.arange(n, dtype=jnp.int32)
    order = (p // 2 - x) % nx + nx * (p % 2 != l).astype(jnp.int32)
    return jnp.take(stacked, order, axis=0)


def x_ring_scatter(blocks, n):
    h = blocks[0].shape[0] // 2
    low = lax.ppermute(blocks[2][:h].astype(jnp.bfloat16), "dp", _x_shift(n, 1))
    high = lax.ppermute(blocks[2][h:].astype(jnp.bfloat16), "dp", _x_shift(n, -1))
    to_right = jnp.concatenate([blocks[1][:h] + low.astype(jnp.float32), blocks[1][h:]], axis=0)
    to_left = jnp.concatenate([blocks[3][:h], blocks[3][h:] + high.astype(jnp.float32)], axis=0)
    from_left = lax.ppermute(to_right.astype(jnp.bfloat16), "dp", _x_shift(n, 1))
    from_right = lax.ppermute(to_left.astype(jnp.bfloat16), "dp", _x_shift(n, -1))
    return blocks[0] + from_left.astype(jnp.float32) + from_right.astype(jnp.float32)


def dp_scatter_2d(partial, n):
    assert n == 8
    me = lax.axis_index("dp")
    x, l, nx = me // 2, me % 2, n // 2
    blocks = partial.reshape((n, partial.shape[0] // n) + partial.shape[1:])

    def pick(m, side):
        index = 2 * ((x + m) % nx) + side
        return lax.dynamic_index_in_dim(blocks, index, 0, keepdims=False).astype(jnp.float32)

    partner_sum = x_ring_scatter([pick(m, 1 - l) for m in range(nx)], n)
    sent = lax.ppermute(partner_sum.astype(jnp.bfloat16), "dp", _y_pair(n))
    own_sum = x_ring_scatter([pick(m, l) for m in range(nx)], n)
    return own_sum + sent.astype(jnp.float32)


def _ring_gather_kernel(n, *refs):
    count = (len(refs) - 3) // 2
    shards, outs = refs[:count], refs[count : 2 * count]
    send_sem, recv_sem, local_sem = refs[2 * count :]
    me = lax.axis_index("dp")
    ex = lax.axis_index("expert")
    right, left, partner = lax.rem(me + 2, n), lax.rem(me + n - 2, n), me + 1 - 2 * lax.rem(me, 2)
    barrier = pltpu.get_barrier_semaphore()
    for peer in (right, left, partner):
        pl.semaphore_signal(barrier, inc=1, device_id=(peer, ex), device_id_type=MESH)
    pl.semaphore_wait(barrier, 3)

    def send(a, role, src, slot, rows, peer):
        copy = pltpu.make_async_remote_copy(
            src_ref=src,
            dst_ref=outs[a].at[slot, rows],
            send_sem=send_sem.at[a, role],
            recv_sem=recv_sem.at[a, role],
            device_id=(peer, ex),
            device_id_type=MESH,
        )
        copy.start()
        return copy

    spans = []
    for a in range(count):
        half = shards[a].shape[0] // 2
        spans.append((pl.ds(0, 2 * half), pl.ds(0, half), pl.ds(half, half)))
    locals_, first, second, third = [], [], [], []
    for a in range(count):
        local = pltpu.make_async_copy(shards[a], outs[a].at[me], local_sem.at[a])
        local.start()
        locals_.append(local)
        whole = spans[a][0]
        first += [
            send(a, 0, shards[a], me, whole, right),
            send(a, 1, shards[a], me, whole, left),
            send(a, 2, shards[a], me, whole, partner),
        ]
    mate = partner
    for a in range(count):
        whole, low, high = spans[a]
        first[3 * a].wait_recv()
        to_right = send(a, 3, outs[a].at[left, low], left, low, right)
        first[3 * a + 1].wait_recv()
        to_left = send(a, 4, outs[a].at[right, high], right, high, left)
        second += [to_right, to_left]
    for a in range(count):
        whole = spans[a][0]
        first[3 * a + 2].wait_recv()
        second += [
            send(a, 5, outs[a].at[mate], mate, whole, right),
            send(a, 6, outs[a].at[mate], mate, whole, left),
        ]
    forwards, mates = second[: 2 * count], second[2 * count :]
    mate_left, mate_right = lax.rem(mate + n - 2, n), lax.rem(mate + 2, n)
    for a in range(count):
        whole, low, high = spans[a]
        mates[2 * a].wait_recv()
        third.append(send(a, 7, outs[a].at[mate_left, low], mate_left, low, right))
        mates[2 * a + 1].wait_recv()
        third.append(send(a, 8, outs[a].at[mate_right, high], mate_right, high, left))
    for copy in first:
        copy.wait_send()
    for copy in forwards:
        copy.wait_recv()
    for copy in second:
        copy.wait_send()
    for copy in third:
        copy.wait_recv()
        copy.wait_send()
    for local in locals_:
        local.wait()


def dp_gather_kernel(shards, n):
    assert n == 8
    count = len(shards)
    return pl.pallas_call(
        functools.partial(_ring_gather_kernel, n),
        out_shape=[jax.ShapeDtypeStruct((n,) + s.shape, s.dtype) for s in shards],
        in_specs=[pl.BlockSpec(memory_space=pl.ANY)] * count,
        out_specs=[pl.BlockSpec(memory_space=pl.ANY)] * count,
        scratch_shapes=[
            pltpu.SemaphoreType.DMA((count, 9)),
            pltpu.SemaphoreType.DMA((count, 9)),
            pltpu.SemaphoreType.DMA((count,)),
        ],
        compiler_params=pltpu.CompilerParams(collective_id=2, has_side_effects=True),
    )(*shards)


def to_blocks(slot_array, num_blocks, pick_count):
    expert_count = slot_array.shape[0]
    trailing = slot_array.shape[2:]
    grouped = slot_array.reshape((expert_count, num_blocks, pick_count) + trailing)
    axis_order = (1, 0, 2) + tuple(range(3, 3 + len(trailing)))
    return jnp.transpose(grouped, axis_order).reshape(
        (num_blocks, expert_count * pick_count) + trailing
    )


def weight_grads(expert_rows, hidden, expert_cot, d_pre_gate, d_pre_up, n):
    hidden_activations = hidden.shape[2]
    out_part = jnp.einsum(
        "erc,erd->cd", hidden, expert_cot, preferred_element_type=jnp.float32
    ).astype(jnp.bfloat16)
    out_share = dp_scatter_2d(out_part, n)
    both_grads = jnp.concatenate([d_pre_gate, d_pre_up], axis=2)
    in_part = jnp.einsum(
        "erc,erk->ck", expert_rows, both_grads, preferred_element_type=jnp.float32
    ).astype(jnp.bfloat16)
    in_share = dp_scatter_2d(in_part, n)
    grad_gate = in_share[None, :, :hidden_activations]
    grad_up = in_share[None, :, hidden_activations:]
    down_weight_gradient = out_share[None]
    return (grad_gate, grad_up, down_weight_gradient)


def body(tokens, cotangent, chosen, w_router, w_gate, w_up, w_down):
    tok_rows, model_width = tokens.shape
    num_blocks, expert_count, pick_count = chosen.shape
    block_rows = tok_rows // num_blocks
    slot_count = num_blocks * pick_count
    logits = jnp.dot(tokens, w_router, preferred_element_type=jnp.float32)
    gate_values = jax.nn.sigmoid(logits)
    offsets = (jnp.arange(num_blocks, dtype=jnp.int32) * block_rows)[:, None, None]
    slot_rows = jnp.transpose(chosen + offsets, (1, 0, 2)).reshape(expert_count, slot_count)
    picked = tokens[slot_rows]
    slot_gate_values = jnp.take_along_axis(gate_values.T, slot_rows, axis=1)
    cot_rows = cotangent[slot_rows]
    scaled_cot = (slot_gate_values[:, :, None] * cot_rows.astype(jnp.float32)).astype(jnp.bfloat16)
    n = lax.axis_size("dp")
    full_gate, full_up, full_down = (
        g.reshape((1, -1) + g.shape[2:])
        for g in dp_gather_kernel([w_gate[0], w_up[0], w_down[0]], n)
    )
    expert_count_axis = lax.axis_size("expert")
    dispatched = lax.all_to_all(
        jnp.concatenate([picked, scaled_cot], axis=1), "expert", 0, 0, tiled=True
    )
    slot_width = picked.shape[1]
    expert_rows = dispatched[:, :slot_width].reshape(1, -1, model_width)
    pre_gate = jnp.einsum(
        "erd,edh->erh", expert_rows, full_gate, preferred_element_type=jnp.float32
    )
    pre_up = jnp.einsum("erd,edh->erh", expert_rows, full_up, preferred_element_type=jnp.float32)
    silu_gate = jax.nn.silu(pre_gate)
    hidden = (silu_gate * pre_up).astype(jnp.bfloat16)
    expert_out = jnp.einsum(
        "erh,ehd->erd", hidden, full_down, preferred_element_type=jnp.float32
    ).astype(jnp.bfloat16)
    returned = lax.all_to_all(
        expert_out.reshape(expert_count_axis, -1, model_width), "expert", 0, 0, tiled=True
    )
    expert_cot = dispatched[:, slot_width:].reshape(1, -1, model_width)
    back_gate, back_up, back_down = (full_gate, full_up, full_down)
    d_hidden = jnp.einsum("erd,ehd->erh", expert_cot, back_down, preferred_element_type=jnp.float32)
    gate_sigmoid = jax.nn.sigmoid(pre_gate)
    d_pre_gate = (
        d_hidden * pre_up * gate_sigmoid * (1.0 + pre_gate * (1.0 - gate_sigmoid))
    ).astype(jnp.bfloat16)
    d_pre_up = (d_hidden * silu_gate).astype(jnp.bfloat16)
    d_rows = (
        jnp.einsum("erh,edh->erd", d_pre_gate, back_gate, preferred_element_type=jnp.float32)
        + jnp.einsum("erh,edh->erd", d_pre_up, back_up, preferred_element_type=jnp.float32)
    ).astype(jnp.bfloat16)
    row_grads = lax.all_to_all(
        d_rows.reshape(expert_count_axis, -1, model_width), "expert", 0, 0, tiled=True
    )
    position_hits = chosen[:, :, :, None] == jnp.arange(block_rows, dtype=jnp.int32)
    indicator_matrix = position_hits.reshape(num_blocks, expert_count * pick_count, block_rows)
    gate_weighted_rows = to_blocks(slot_gate_values, num_blocks, pick_count)[
        :, :, None
    ] * to_blocks(returned, num_blocks, pick_count).astype(jnp.float32)
    mixed = (
        jnp.einsum(
            "wze,wzi->wei",
            indicator_matrix.astype(jnp.float32),
            gate_weighted_rows,
            precision=lax.Precision.HIGHEST,
        )
        .reshape(tok_rows, model_width)
        .astype(jnp.bfloat16)
    )
    slot_dots = jnp.sum(cot_rows.astype(jnp.float32) * returned.astype(jnp.float32), axis=2)
    dgate = jnp.einsum(
        "bept,ebp->bte",
        position_hits.astype(jnp.float32),
        slot_dots.reshape(expert_count, num_blocks, pick_count),
        precision=lax.Precision.HIGHEST,
    ).reshape(tok_rows, expert_count)
    d_logit = (dgate * gate_values * (1.0 - gate_values)).astype(jnp.bfloat16)
    gathered_grads = jnp.einsum(
        "wze,wzi->wei",
        indicator_matrix.astype(jnp.bfloat16),
        to_blocks(row_grads, num_blocks, pick_count),
        preferred_element_type=jnp.float32,
    ).reshape(tok_rows, model_width)
    grad_tokens = (
        gathered_grads + jnp.dot(d_logit, w_router.T, preferred_element_type=jnp.float32)
    ).astype(jnp.bfloat16)
    router_full = jnp.dot(tokens.T, d_logit, preferred_element_type=jnp.float32)
    devices = n * expert_count_axis
    router_part = jnp.sum(
        lax.all_to_all(router_full.reshape(devices, -1), ("dp", "expert"), 0, 0, tiled=True),
        axis=0,
    )
    grad_gate, grad_up, down_weight_gradient = weight_grads(
        expert_rows, hidden, expert_cot, d_pre_gate, d_pre_up, n
    )
    grad_router = lax.all_to_all(
        jnp.broadcast_to(router_part[None], (devices,) + router_part.shape),
        ("dp", "expert"),
        0,
        0,
        tiled=True,
    ).reshape(router_full.shape)
    return (mixed, grad_tokens, grad_gate, grad_up, down_weight_gradient, grad_router)


def solution(mesh):
    placed = (
        P(("dp", "expert"), None),
        P(("dp", "expert"), None),
        P(("dp", "expert"), None, None),
        P(),
        P("expert", "dp", None),
        P("expert", "dp", None),
        P("expert", "dp", None),
    )
    return jax.shard_map(
        body,
        mesh=mesh,
        in_specs=placed,
        out_specs=(
            P(("dp", "expert"), None),
            P(("dp", "expert"), None),
            P("expert", "dp", None),
            P("expert", "dp", None),
            P("expert", "dp", None),
            P(),
        ),
        check_vma=False,
    )
```

```python
import functools

import jax
import jax.numpy as jnp
from jax import lax
from jax.experimental import pallas as pl
from jax.experimental.pallas import tpu as pltpu
from jax.sharding import PartitionSpec as P

MESH = pl.DeviceIdType.MESH


def _gather_kernel(n, *refs):
    count = (len(refs) - 3) // 2
    srcs, dsts = refs[:count], refs[count : 2 * count]
    send_sem, recv_sem, local_sem = refs[2 * count :]
    me = lax.axis_index("dp")
    ex = lax.axis_index("expert")
    barrier = pltpu.get_barrier_semaphore()
    for k in range(1, n):
        pl.semaphore_signal(barrier, inc=1, device_id=(lax.rem(me + k, n), ex), device_id_type=MESH)
    pl.semaphore_wait(barrier, n - 1)
    copies = []
    for a in range(count):
        rows = srcs[a].shape[0]
        slot = dsts[a].at[pl.ds(me * rows, rows)]
        local = pltpu.make_async_copy(srcs[a], slot, local_sem.at[a])
        local.start()
        copies.append(local)
        for k in range(1, n):
            remote = pltpu.make_async_remote_copy(
                src_ref=srcs[a],
                dst_ref=slot,
                send_sem=send_sem.at[a, k],
                recv_sem=recv_sem.at[a, k],
                device_id=(lax.rem(me + k, n), ex),
                device_id_type=MESH,
            )
            remote.start()
            copies.append(remote)
    for c in copies:
        c.wait()


def dp_all_gather(shards, n):
    count = len(shards)
    return pl.pallas_call(
        functools.partial(_gather_kernel, n),
        out_shape=[jax.ShapeDtypeStruct((n * s.shape[0],) + s.shape[1:], s.dtype) for s in shards],
        in_specs=[pl.BlockSpec(memory_space=pl.ANY)] * count,
        out_specs=[pl.BlockSpec(memory_space=pl.ANY)] * count,
        scratch_shapes=[
            pltpu.SemaphoreType.DMA((count, n)),
            pltpu.SemaphoreType.DMA((count, n)),
            pltpu.SemaphoreType.DMA((count,)),
        ],
        compiler_params=pltpu.CompilerParams(collective_id=0, has_side_effects=True),
    )(*shards)


def _exchange_kernel(n, n_scatter, *refs):
    count = (len(refs) - 3) // 2
    srcs, dsts = refs[:count], refs[count : 2 * count]
    send_sem, recv_sem, local_sem = refs[2 * count :]
    me = lax.axis_index("dp")
    ex = lax.axis_index("expert")
    barrier = pltpu.get_barrier_semaphore()
    for k in range(1, n):
        pl.semaphore_signal(barrier, inc=1, device_id=(lax.rem(me + k, n), ex), device_id_type=MESH)
    pl.semaphore_wait(barrier, n - 1)
    copies = []
    for a in range(count):
        rows = dsts[a].shape[1]
        if a < n_scatter:
            mine = srcs[a].at[pl.ds(me * rows, rows)]
        else:
            mine = srcs[a]
        local = pltpu.make_async_copy(mine, dsts[a].at[me], local_sem.at[a])
        local.start()
        copies.append(local)
        for k in range(1, n):
            peer = lax.rem(me + k, n)
            if a < n_scatter:
                part = srcs[a].at[pl.ds(peer * rows, rows)]
            else:
                part = srcs[a]
            remote = pltpu.make_async_remote_copy(
                src_ref=part,
                dst_ref=dsts[a].at[me],
                send_sem=send_sem.at[a, k],
                recv_sem=recv_sem.at[a, k],
                device_id=(peer, ex),
                device_id_type=MESH,
            )
            remote.start()
            copies.append(remote)
    for c in copies:
        c.wait()


def dp_exchange(partials, replicas, n):
    arrays = list(partials) + list(replicas)
    count = len(arrays)
    shapes = [(n, p.shape[0] // n) + p.shape[1:] for p in partials]
    shapes += [(n,) + r.shape for r in replicas]
    received = pl.pallas_call(
        functools.partial(_exchange_kernel, n, len(partials)),
        out_shape=[jax.ShapeDtypeStruct(s, a.dtype) for s, a in zip(shapes, arrays)],
        in_specs=[pl.BlockSpec(memory_space=pl.ANY)] * count,
        out_specs=[pl.BlockSpec(memory_space=pl.ANY)] * count,
        scratch_shapes=[
            pltpu.SemaphoreType.DMA((count, n)),
            pltpu.SemaphoreType.DMA((count, n)),
            pltpu.SemaphoreType.DMA((count,)),
        ],
        compiler_params=pltpu.CompilerParams(collective_id=1, has_side_effects=True),
    )(*arrays)
    return [jnp.sum(r.astype(jnp.float32), axis=0) for r in received]


def _shift_pairs(n, k):
    return [(i, (i + k) % n) for i in range(n)]


def dp_gather_permute(shard, n):
    me = lax.axis_index("dp")
    full = jnp.zeros((n,) + shard.shape, shard.dtype)
    full = lax.dynamic_update_index_in_dim(full, shard, me, 0)
    for k in range(1, n):
        got = lax.ppermute(shard, "dp", perm=_shift_pairs(n, k))
        full = lax.dynamic_update_index_in_dim(full, got, lax.rem(me + n - k, n), 0)
    return full


def dp_scatter_permute(partial, n):
    me = lax.axis_index("dp")
    blocks = partial.reshape((n, partial.shape[0] // n) + partial.shape[1:])
    total = lax.dynamic_index_in_dim(blocks, me, 0, keepdims=False).astype(jnp.float32)
    for k in range(1, n):
        piece = lax.dynamic_index_in_dim(blocks, lax.rem(me + k, n), 0, keepdims=False)
        got = lax.ppermute(piece, "dp", perm=_shift_pairs(n, k))
        total = total + got.astype(jnp.float32)
    return total


def _x_shift(n, d):
    return [(i, (i + 2 * d) % n) for i in range(n)]


def _y_pair(n):
    return [(i, i ^ 1) for i in range(n)]


def x_ring_gather(t, n):
    from_left = lax.ppermute(t, "dp", _x_shift(n, 1))
    from_right = lax.ppermute(t, "dp", _x_shift(n, -1))
    h = t.shape[0] // 2
    first = lax.ppermute(from_left[:h], "dp", _x_shift(n, 1))
    second = lax.ppermute(from_right[h:], "dp", _x_shift(n, -1))
    return [t, from_right, jnp.concatenate([first, second], axis=0), from_left]


def dp_gather_2d(t, n):
    assert n == 8
    me = lax.axis_index("dp")
    x, l, nx = me // 2, me % 2, n // 2
    partner = lax.ppermute(t, "dp", _y_pair(n))
    stacked = jnp.stack(x_ring_gather(t, n) + x_ring_gather(partner, n))
    p = jnp.arange(n, dtype=jnp.int32)
    order = (p // 2 - x) % nx + nx * (p % 2 != l).astype(jnp.int32)
    return jnp.take(stacked, order, axis=0)


def x_ring_scatter(blocks, n):
    h = blocks[0].shape[0] // 2
    low = lax.ppermute(blocks[2][:h].astype(jnp.bfloat16), "dp", _x_shift(n, 1))
    high = lax.ppermute(blocks[2][h:].astype(jnp.bfloat16), "dp", _x_shift(n, -1))
    to_right = jnp.concatenate([blocks[1][:h] + low.astype(jnp.float32), blocks[1][h:]], axis=0)
    to_left = jnp.concatenate([blocks[3][:h], blocks[3][h:] + high.astype(jnp.float32)], axis=0)
    from_left = lax.ppermute(to_right.astype(jnp.bfloat16), "dp", _x_shift(n, 1))
    from_right = lax.ppermute(to_left.astype(jnp.bfloat16), "dp", _x_shift(n, -1))
    return blocks[0] + from_left.astype(jnp.float32) + from_right.astype(jnp.float32)


def dp_scatter_2d(partial, n):
    assert n == 8
    me = lax.axis_index("dp")
    x, l, nx = me // 2, me % 2, n // 2
    blocks = partial.reshape((n, partial.shape[0] // n) + partial.shape[1:])

    def pick(m, side):
        index = 2 * ((x + m) % nx) + side
        return lax.dynamic_index_in_dim(blocks, index, 0, keepdims=False).astype(jnp.float32)

    partner_sum = x_ring_scatter([pick(m, 1 - l) for m in range(nx)], n)
    sent = lax.ppermute(partner_sum.astype(jnp.bfloat16), "dp", _y_pair(n))
    own_sum = x_ring_scatter([pick(m, l) for m in range(nx)], n)
    return own_sum + sent.astype(jnp.float32)


def _ring_gather_kernel(n, *refs):
    count = (len(refs) - 3) // 2
    shards, outs = refs[:count], refs[count : 2 * count]
    send_sem, recv_sem, local_sem = refs[2 * count :]
    me = lax.axis_index("dp")
    ex = lax.axis_index("expert")
    right, left, partner = lax.rem(me + 2, n), lax.rem(me + n - 2, n), me + 1 - 2 * lax.rem(me, 2)
    barrier = pltpu.get_barrier_semaphore()
    for peer in (right, left, partner):
        pl.semaphore_signal(barrier, inc=1, device_id=(peer, ex), device_id_type=MESH)
    pl.semaphore_wait(barrier, 3)

    def send(a, role, src, slot, rows, peer):
        copy = pltpu.make_async_remote_copy(
            src_ref=src,
            dst_ref=outs[a].at[slot, rows],
            send_sem=send_sem.at[a, role],
            recv_sem=recv_sem.at[a, role],
            device_id=(peer, ex),
            device_id_type=MESH,
        )
        copy.start()
        return copy

    spans = []
    for a in range(count):
        half = shards[a].shape[0] // 2
        spans.append((pl.ds(0, 2 * half), pl.ds(0, half), pl.ds(half, half)))
    locals_, first, second, third = [], [], [], []
    for a in range(count):
        local = pltpu.make_async_copy(shards[a], outs[a].at[me], local_sem.at[a])
        local.start()
        locals_.append(local)
    across = [send(a, 2, shards[a], me, spans[a][0], partner) for a in range(count)]
    for a in range(count):
        whole = spans[a][0]
        first += [
            send(a, 0, shards[a], me, whole, right),
            send(a, 1, shards[a], me, whole, left),
            across[a],
        ]
    mate = partner
    for a in range(count):
        whole, low, high = spans[a]
        first[3 * a].wait_recv()
        to_right = send(a, 3, outs[a].at[left, low], left, low, right)
        first[3 * a + 1].wait_recv()
        to_left = send(a, 4, outs[a].at[right, high], right, high, left)
        second += [to_right, to_left]
    for a in range(count):
        whole = spans[a][0]
        first[3 * a + 2].wait_recv()
        second += [
            send(a, 5, outs[a].at[mate], mate, whole, right),
            send(a, 6, outs[a].at[mate], mate, whole, left),
        ]
    forwards, mates = second[: 2 * count], second[2 * count :]
    mate_left, mate_right = lax.rem(mate + n - 2, n), lax.rem(mate + 2, n)
    for a in range(count):
        whole, low, high = spans[a]
        mates[2 * a].wait_recv()
        third.append(send(a, 7, outs[a].at[mate_left, low], mate_left, low, right))
        mates[2 * a + 1].wait_recv()
        third.append(send(a, 8, outs[a].at[mate_right, high], mate_right, high, left))
    for copy in first:
        copy.wait_send()
    for copy in forwards:
        copy.wait_recv()
    for copy in second:
        copy.wait_send()
    for copy in third:
        copy.wait_recv()
        copy.wait_send()
    for local in locals_:
        local.wait()


def dp_gather_kernel(shards, n):
    assert n == 8
    count = len(shards)
    return pl.pallas_call(
        functools.partial(_ring_gather_kernel, n),
        out_shape=[jax.ShapeDtypeStruct((n,) + s.shape, s.dtype) for s in shards],
        in_specs=[pl.BlockSpec(memory_space=pl.ANY)] * count,
        out_specs=[pl.BlockSpec(memory_space=pl.ANY)] * count,
        scratch_shapes=[
            pltpu.SemaphoreType.DMA((count, 9)),
            pltpu.SemaphoreType.DMA((count, 9)),
            pltpu.SemaphoreType.DMA((count,)),
        ],
        compiler_params=pltpu.CompilerParams(collective_id=2, has_side_effects=True),
    )(*shards)


def to_blocks(slot_array, num_blocks, pick_count):
    expert_count = slot_array.shape[0]
    trailing = slot_array.shape[2:]
    grouped = slot_array.reshape((expert_count, num_blocks, pick_count) + trailing)
    axis_order = (1, 0, 2) + tuple(range(3, 3 + len(trailing)))
    return jnp.transpose(grouped, axis_order).reshape(
        (num_blocks, expert_count * pick_count) + trailing
    )


def weight_grads(expert_rows, hidden, expert_cot, d_pre_gate, d_pre_up, n):
    hidden_activations = hidden.shape[2]
    out_part = jnp.einsum(
        "erc,erd->cd", hidden, expert_cot, preferred_element_type=jnp.float32
    ).astype(jnp.bfloat16)
    out_share = dp_scatter_2d(out_part, n)
    both_grads = jnp.concatenate([d_pre_gate, d_pre_up], axis=2)
    in_part = jnp.einsum(
        "erc,erk->ck", expert_rows, both_grads, preferred_element_type=jnp.float32
    ).astype(jnp.bfloat16)
    in_share = dp_scatter_2d(in_part, n)
    grad_gate = in_share[None, :, :hidden_activations]
    grad_up = in_share[None, :, hidden_activations:]
    down_weight_gradient = out_share[None]
    return (grad_gate, grad_up, down_weight_gradient)


def body(tokens, cotangent, chosen, w_router, w_gate, w_up, w_down):
    tok_rows, model_width = tokens.shape
    num_blocks, expert_count, pick_count = chosen.shape
    block_rows = tok_rows // num_blocks
    slot_count = num_blocks * pick_count
    logits = jnp.dot(tokens, w_router, preferred_element_type=jnp.float32)
    gate_values = jax.nn.sigmoid(logits)
    offsets = (jnp.arange(num_blocks, dtype=jnp.int32) * block_rows)[:, None, None]
    slot_rows = jnp.transpose(chosen + offsets, (1, 0, 2)).reshape(expert_count, slot_count)
    picked = tokens[slot_rows]
    slot_gate_values = jnp.take_along_axis(gate_values.T, slot_rows, axis=1)
    cot_rows = cotangent[slot_rows]
    scaled_cot = (slot_gate_values[:, :, None] * cot_rows.astype(jnp.float32)).astype(jnp.bfloat16)
    n = lax.axis_size("dp")
    full_gate, full_up, full_down = (
        g.reshape((1, -1) + g.shape[2:])
        for g in dp_gather_kernel([w_gate[0], w_up[0], w_down[0]], n)
    )
    expert_count_axis = lax.axis_size("expert")
    dispatched = lax.all_to_all(
        jnp.concatenate([picked, scaled_cot], axis=1), "expert", 0, 0, tiled=True
    )
    slot_width = picked.shape[1]
    expert_rows = dispatched[:, :slot_width].reshape(1, -1, model_width)
    pre_gate = jnp.einsum(
        "erd,edh->erh", expert_rows, full_gate, preferred_element_type=jnp.float32
    )
    pre_up = jnp.einsum("erd,edh->erh", expert_rows, full_up, preferred_element_type=jnp.float32)
    silu_gate = jax.nn.silu(pre_gate)
    hidden = (silu_gate * pre_up).astype(jnp.bfloat16)
    expert_out = jnp.einsum(
        "erh,ehd->erd", hidden, full_down, preferred_element_type=jnp.float32
    ).astype(jnp.bfloat16)
    returned = lax.all_to_all(
        expert_out.reshape(expert_count_axis, -1, model_width), "expert", 0, 0, tiled=True
    )
    expert_cot = dispatched[:, slot_width:].reshape(1, -1, model_width)
    back_gate, back_up, back_down = (full_gate, full_up, full_down)
    d_hidden = jnp.einsum("erd,ehd->erh", expert_cot, back_down, preferred_element_type=jnp.float32)
    gate_sigmoid = jax.nn.sigmoid(pre_gate)
    d_pre_gate = (
        d_hidden * pre_up * gate_sigmoid * (1.0 + pre_gate * (1.0 - gate_sigmoid))
    ).astype(jnp.bfloat16)
    d_pre_up = (d_hidden * silu_gate).astype(jnp.bfloat16)
    d_rows = (
        jnp.einsum("erh,edh->erd", d_pre_gate, back_gate, preferred_element_type=jnp.float32)
        + jnp.einsum("erh,edh->erd", d_pre_up, back_up, preferred_element_type=jnp.float32)
    ).astype(jnp.bfloat16)
    row_grads = lax.all_to_all(
        d_rows.reshape(expert_count_axis, -1, model_width), "expert", 0, 0, tiled=True
    )
    position_hits = chosen[:, :, :, None] == jnp.arange(block_rows, dtype=jnp.int32)
    indicator_matrix = position_hits.reshape(num_blocks, expert_count * pick_count, block_rows)
    gate_weighted_rows = to_blocks(slot_gate_values, num_blocks, pick_count)[
        :, :, None
    ] * to_blocks(returned, num_blocks, pick_count).astype(jnp.float32)
    mixed = (
        jnp.einsum(
            "wze,wzi->wei",
            indicator_matrix.astype(jnp.float32),
            gate_weighted_rows,
            precision=lax.Precision.HIGHEST,
        )
        .reshape(tok_rows, model_width)
        .astype(jnp.bfloat16)
    )
    slot_dots = jnp.sum(cot_rows.astype(jnp.float32) * returned.astype(jnp.float32), axis=2)
    dgate = jnp.einsum(
        "bept,ebp->bte",
        position_hits.astype(jnp.float32),
        slot_dots.reshape(expert_count, num_blocks, pick_count),
        precision=lax.Precision.HIGHEST,
    ).reshape(tok_rows, expert_count)
    d_logit = (dgate * gate_values * (1.0 - gate_values)).astype(jnp.bfloat16)
    gathered_grads = jnp.einsum(
        "wze,wzi->wei",
        indicator_matrix.astype(jnp.bfloat16),
        to_blocks(row_grads, num_blocks, pick_count),
        preferred_element_type=jnp.float32,
    ).reshape(tok_rows, model_width)
    grad_tokens = (
        gathered_grads + jnp.dot(d_logit, w_router.T, preferred_element_type=jnp.float32)
    ).astype(jnp.bfloat16)
    router_full = jnp.dot(tokens.T, d_logit, preferred_element_type=jnp.float32)
    devices = n * expert_count_axis
    router_part = jnp.sum(
        lax.all_to_all(router_full.reshape(devices, -1), ("dp", "expert"), 0, 0, tiled=True),
        axis=0,
    )
    grad_gate, grad_up, down_weight_gradient = weight_grads(
        expert_rows, hidden, expert_cot, d_pre_gate, d_pre_up, n
    )
    grad_router = lax.all_to_all(
        jnp.broadcast_to(router_part[None], (devices,) + router_part.shape),
        ("dp", "expert"),
        0,
        0,
        tiled=True,
    ).reshape(router_full.shape)
    return (mixed, grad_tokens, grad_gate, grad_up, down_weight_gradient, grad_router)


def solution(mesh):
    placed = (
        P(("dp", "expert"), None),
        P(("dp", "expert"), None),
        P(("dp", "expert"), None, None),
        P(),
        P("expert", "dp", None),
        P("expert", "dp", None),
        P("expert", "dp", None),
    )
    return jax.shard_map(
        body,
        mesh=mesh,
        in_specs=placed,
        out_specs=(
            P(("dp", "expert"), None),
            P(("dp", "expert"), None),
            P("expert", "dp", None),
            P("expert", "dp", None),
            P("expert", "dp", None),
            P(),
        ),
        check_vma=False,
    )
```

```python
import functools

import jax
import jax.numpy as jnp
from jax import lax
from jax.experimental import pallas as pl
from jax.experimental.pallas import tpu as pltpu
from jax.sharding import PartitionSpec as P

MESH = pl.DeviceIdType.MESH


def _gather_kernel(n, *refs):
    count = (len(refs) - 3) // 2
    srcs, dsts = refs[:count], refs[count : 2 * count]
    send_sem, recv_sem, local_sem = refs[2 * count :]
    me = lax.axis_index("dp")
    ex = lax.axis_index("expert")
    barrier = pltpu.get_barrier_semaphore()
    for k in range(1, n):
        pl.semaphore_signal(barrier, inc=1, device_id=(lax.rem(me + k, n), ex), device_id_type=MESH)
    pl.semaphore_wait(barrier, n - 1)
    copies = []
    for a in range(count):
        rows = srcs[a].shape[0]
        slot = dsts[a].at[pl.ds(me * rows, rows)]
        local = pltpu.make_async_copy(srcs[a], slot, local_sem.at[a])
        local.start()
        copies.append(local)
        for k in range(1, n):
            remote = pltpu.make_async_remote_copy(
                src_ref=srcs[a],
                dst_ref=slot,
                send_sem=send_sem.at[a, k],
                recv_sem=recv_sem.at[a, k],
                device_id=(lax.rem(me + k, n), ex),
                device_id_type=MESH,
            )
            remote.start()
            copies.append(remote)
    for c in copies:
        c.wait()


def dp_all_gather(shards, n):
    count = len(shards)
    return pl.pallas_call(
        functools.partial(_gather_kernel, n),
        out_shape=[jax.ShapeDtypeStruct((n * s.shape[0],) + s.shape[1:], s.dtype) for s in shards],
        in_specs=[pl.BlockSpec(memory_space=pl.ANY)] * count,
        out_specs=[pl.BlockSpec(memory_space=pl.ANY)] * count,
        scratch_shapes=[
            pltpu.SemaphoreType.DMA((count, n)),
            pltpu.SemaphoreType.DMA((count, n)),
            pltpu.SemaphoreType.DMA((count,)),
        ],
        compiler_params=pltpu.CompilerParams(collective_id=0, has_side_effects=True),
    )(*shards)


def _exchange_kernel(n, n_scatter, *refs):
    count = (len(refs) - 3) // 2
    srcs, dsts = refs[:count], refs[count : 2 * count]
    send_sem, recv_sem, local_sem = refs[2 * count :]
    me = lax.axis_index("dp")
    ex = lax.axis_index("expert")
    barrier = pltpu.get_barrier_semaphore()
    for k in range(1, n):
        pl.semaphore_signal(barrier, inc=1, device_id=(lax.rem(me + k, n), ex), device_id_type=MESH)
    pl.semaphore_wait(barrier, n - 1)
    copies = []
    for a in range(count):
        rows = dsts[a].shape[1]
        if a < n_scatter:
            mine = srcs[a].at[pl.ds(me * rows, rows)]
        else:
            mine = srcs[a]
        local = pltpu.make_async_copy(mine, dsts[a].at[me], local_sem.at[a])
        local.start()
        copies.append(local)
        for k in range(1, n):
            peer = lax.rem(me + k, n)
            if a < n_scatter:
                part = srcs[a].at[pl.ds(peer * rows, rows)]
            else:
                part = srcs[a]
            remote = pltpu.make_async_remote_copy(
                src_ref=part,
                dst_ref=dsts[a].at[me],
                send_sem=send_sem.at[a, k],
                recv_sem=recv_sem.at[a, k],
                device_id=(peer, ex),
                device_id_type=MESH,
            )
            remote.start()
            copies.append(remote)
    for c in copies:
        c.wait()


def dp_exchange(partials, replicas, n):
    arrays = list(partials) + list(replicas)
    count = len(arrays)
    shapes = [(n, p.shape[0] // n) + p.shape[1:] for p in partials]
    shapes += [(n,) + r.shape for r in replicas]
    received = pl.pallas_call(
        functools.partial(_exchange_kernel, n, len(partials)),
        out_shape=[jax.ShapeDtypeStruct(s, a.dtype) for s, a in zip(shapes, arrays)],
        in_specs=[pl.BlockSpec(memory_space=pl.ANY)] * count,
        out_specs=[pl.BlockSpec(memory_space=pl.ANY)] * count,
        scratch_shapes=[
            pltpu.SemaphoreType.DMA((count, n)),
            pltpu.SemaphoreType.DMA((count, n)),
            pltpu.SemaphoreType.DMA((count,)),
        ],
        compiler_params=pltpu.CompilerParams(collective_id=1, has_side_effects=True),
    )(*arrays)
    return [jnp.sum(r.astype(jnp.float32), axis=0) for r in received]


def _shift_pairs(n, k):
    return [(i, (i + k) % n) for i in range(n)]


def dp_gather_permute(shard, n):
    me = lax.axis_index("dp")
    full = jnp.zeros((n,) + shard.shape, shard.dtype)
    full = lax.dynamic_update_index_in_dim(full, shard, me, 0)
    for k in range(1, n):
        got = lax.ppermute(shard, "dp", perm=_shift_pairs(n, k))
        full = lax.dynamic_update_index_in_dim(full, got, lax.rem(me + n - k, n), 0)
    return full


def dp_scatter_permute(partial, n):
    me = lax.axis_index("dp")
    blocks = partial.reshape((n, partial.shape[0] // n) + partial.shape[1:])
    total = lax.dynamic_index_in_dim(blocks, me, 0, keepdims=False).astype(jnp.float32)
    for k in range(1, n):
        piece = lax.dynamic_index_in_dim(blocks, lax.rem(me + k, n), 0, keepdims=False)
        got = lax.ppermute(piece, "dp", perm=_shift_pairs(n, k))
        total = total + got.astype(jnp.float32)
    return total


def _x_shift(n, d):
    return [(i, (i + 2 * d) % n) for i in range(n)]


def _y_pair(n):
    return [(i, i ^ 1) for i in range(n)]


def x_ring_gather(t, n):
    from_left = lax.ppermute(t, "dp", _x_shift(n, 1))
    from_right = lax.ppermute(t, "dp", _x_shift(n, -1))
    h = t.shape[0] // 2
    first = lax.ppermute(from_left[:h], "dp", _x_shift(n, 1))
    second = lax.ppermute(from_right[h:], "dp", _x_shift(n, -1))
    return [t, from_right, jnp.concatenate([first, second], axis=0), from_left]


def dp_gather_2d(t, n):
    assert n == 8
    me = lax.axis_index("dp")
    x, l, nx = me // 2, me % 2, n // 2
    partner = lax.ppermute(t, "dp", _y_pair(n))
    stacked = jnp.stack(x_ring_gather(t, n) + x_ring_gather(partner, n))
    p = jnp.arange(n, dtype=jnp.int32)
    order = (p // 2 - x) % nx + nx * (p % 2 != l).astype(jnp.int32)
    return jnp.take(stacked, order, axis=0)


def x_ring_scatter(blocks, n):
    h = blocks[0].shape[0] // 2
    low = lax.ppermute(blocks[2][:h].astype(jnp.bfloat16), "dp", _x_shift(n, 1))
    high = lax.ppermute(blocks[2][h:].astype(jnp.bfloat16), "dp", _x_shift(n, -1))
    to_right = jnp.concatenate([blocks[1][:h] + low.astype(jnp.float32), blocks[1][h:]], axis=0)
    to_left = jnp.concatenate([blocks[3][:h], blocks[3][h:] + high.astype(jnp.float32)], axis=0)
    from_left = lax.ppermute(to_right.astype(jnp.bfloat16), "dp", _x_shift(n, 1))
    from_right = lax.ppermute(to_left.astype(jnp.bfloat16), "dp", _x_shift(n, -1))
    return blocks[0] + from_left.astype(jnp.float32) + from_right.astype(jnp.float32)


def dp_scatter_2d(partial, n):
    assert n == 8
    me = lax.axis_index("dp")
    x, l, nx = me // 2, me % 2, n // 2
    blocks = partial.reshape((n, partial.shape[0] // n) + partial.shape[1:])

    def pick(m, side):
        index = 2 * ((x + m) % nx) + side
        return lax.dynamic_index_in_dim(blocks, index, 0, keepdims=False).astype(jnp.float32)

    partner_sum = x_ring_scatter([pick(m, 1 - l) for m in range(nx)], n)
    sent = lax.ppermute(partner_sum.astype(jnp.bfloat16), "dp", _y_pair(n))
    own_sum = x_ring_scatter([pick(m, l) for m in range(nx)], n)
    return own_sum + sent.astype(jnp.float32)


def _ring_gather_kernel(n, *refs):
    count = (len(refs) - 3) // 2
    shards, outs = refs[:count], refs[count : 2 * count]
    send_sem, recv_sem, local_sem = refs[2 * count :]
    me = lax.axis_index("dp")
    ex = lax.axis_index("expert")
    right, left, partner = lax.rem(me + 2, n), lax.rem(me + n - 2, n), me + 1 - 2 * lax.rem(me, 2)
    barrier = pltpu.get_barrier_semaphore()
    for peer in (right, left, partner):
        pl.semaphore_signal(barrier, inc=1, device_id=(peer, ex), device_id_type=MESH)
    pl.semaphore_wait(barrier, 3)

    def send(a, role, src, slot, rows, peer):
        copy = pltpu.make_async_remote_copy(
            src_ref=src,
            dst_ref=outs[a].at[slot, rows],
            send_sem=send_sem.at[a, role],
            recv_sem=recv_sem.at[a, role],
            device_id=(peer, ex),
            device_id_type=MESH,
        )
        copy.start()
        return copy

    spans = []
    for a in range(count):
        half = shards[a].shape[0] // 2
        spans.append((pl.ds(0, 2 * half), pl.ds(0, half), pl.ds(half, half)))
    locals_, first, second, third = [], [], [], []
    for a in range(count):
        local = pltpu.make_async_copy(shards[a], outs[a].at[me], local_sem.at[a])
        local.start()
        locals_.append(local)
        whole = spans[a][0]
        first += [
            send(a, 0, shards[a], me, whole, right),
            send(a, 1, shards[a], me, whole, left),
            send(a, 2, shards[a], me, whole, partner),
        ]
    mate = partner
    forwards, mates = [], []
    for a in range(count):
        whole, low, high = spans[a]
        first[3 * a].wait_recv()
        forwards.append(send(a, 3, outs[a].at[left, low], left, low, right))
        first[3 * a + 1].wait_recv()
        forwards.append(send(a, 4, outs[a].at[right, high], right, high, left))
        first[3 * a + 2].wait_recv()
        mates.append(send(a, 5, outs[a].at[mate], mate, whole, right))
        mates.append(send(a, 6, outs[a].at[mate], mate, whole, left))
    second = forwards + mates
    mate_left, mate_right = lax.rem(mate + n - 2, n), lax.rem(mate + 2, n)
    for a in range(count):
        whole, low, high = spans[a]
        mates[2 * a].wait_recv()
        third.append(send(a, 7, outs[a].at[mate_left, low], mate_left, low, right))
        mates[2 * a + 1].wait_recv()
        third.append(send(a, 8, outs[a].at[mate_right, high], mate_right, high, left))
    for copy in first:
        copy.wait_send()
    for copy in forwards:
        copy.wait_recv()
    for copy in second:
        copy.wait_send()
    for copy in third:
        copy.wait_recv()
        copy.wait_send()
    for local in locals_:
        local.wait()


def dp_gather_kernel(shards, n):
    assert n == 8
    count = len(shards)
    return pl.pallas_call(
        functools.partial(_ring_gather_kernel, n),
        out_shape=[jax.ShapeDtypeStruct((n,) + s.shape, s.dtype) for s in shards],
        in_specs=[pl.BlockSpec(memory_space=pl.ANY)] * count,
        out_specs=[pl.BlockSpec(memory_space=pl.ANY)] * count,
        scratch_shapes=[
            pltpu.SemaphoreType.DMA((count, 9)),
            pltpu.SemaphoreType.DMA((count, 9)),
            pltpu.SemaphoreType.DMA((count,)),
        ],
        compiler_params=pltpu.CompilerParams(collective_id=2, has_side_effects=True),
    )(*shards)


def to_blocks(slot_array, num_blocks, pick_count):
    expert_count = slot_array.shape[0]
    trailing = slot_array.shape[2:]
    grouped = slot_array.reshape((expert_count, num_blocks, pick_count) + trailing)
    axis_order = (1, 0, 2) + tuple(range(3, 3 + len(trailing)))
    return jnp.transpose(grouped, axis_order).reshape(
        (num_blocks, expert_count * pick_count) + trailing
    )


def weight_grads(expert_rows, hidden, expert_cot, d_pre_gate, d_pre_up, n):
    hidden_activations = hidden.shape[2]
    out_part = jnp.einsum(
        "erc,erd->cd", hidden, expert_cot, preferred_element_type=jnp.float32
    ).astype(jnp.bfloat16)
    out_share = dp_scatter_2d(out_part, n)
    both_grads = jnp.concatenate([d_pre_gate, d_pre_up], axis=2)
    in_part = jnp.einsum(
        "erc,erk->ck", expert_rows, both_grads, preferred_element_type=jnp.float32
    ).astype(jnp.bfloat16)
    in_share = dp_scatter_2d(in_part, n)
    grad_gate = in_share[None, :, :hidden_activations]
    grad_up = in_share[None, :, hidden_activations:]
    down_weight_gradient = out_share[None]
    return (grad_gate, grad_up, down_weight_gradient)


def body(tokens, cotangent, chosen, w_router, w_gate, w_up, w_down):
    tok_rows, model_width = tokens.shape
    num_blocks, expert_count, pick_count = chosen.shape
    block_rows = tok_rows // num_blocks
    slot_count = num_blocks * pick_count
    logits = jnp.dot(tokens, w_router, preferred_element_type=jnp.float32)
    gate_values = jax.nn.sigmoid(logits)
    offsets = (jnp.arange(num_blocks, dtype=jnp.int32) * block_rows)[:, None, None]
    slot_rows = jnp.transpose(chosen + offsets, (1, 0, 2)).reshape(expert_count, slot_count)
    picked = tokens[slot_rows]
    slot_gate_values = jnp.take_along_axis(gate_values.T, slot_rows, axis=1)
    cot_rows = cotangent[slot_rows]
    scaled_cot = (slot_gate_values[:, :, None] * cot_rows.astype(jnp.float32)).astype(jnp.bfloat16)
    n = lax.axis_size("dp")
    full_gate, full_up, full_down = (
        g.reshape((1, -1) + g.shape[2:])
        for g in dp_gather_kernel([w_gate[0], w_up[0], w_down[0]], n)
    )
    expert_count_axis = lax.axis_size("expert")
    dispatched = lax.all_to_all(
        jnp.concatenate([picked, scaled_cot], axis=1), "expert", 0, 0, tiled=True
    )
    slot_width = picked.shape[1]
    expert_rows = dispatched[:, :slot_width].reshape(1, -1, model_width)
    pre_gate = jnp.einsum(
        "erd,edh->erh", expert_rows, full_gate, preferred_element_type=jnp.float32
    )
    pre_up = jnp.einsum("erd,edh->erh", expert_rows, full_up, preferred_element_type=jnp.float32)
    silu_gate = jax.nn.silu(pre_gate)
    hidden = (silu_gate * pre_up).astype(jnp.bfloat16)
    expert_out = jnp.einsum(
        "erh,ehd->erd", hidden, full_down, preferred_element_type=jnp.float32
    ).astype(jnp.bfloat16)
    returned = lax.all_to_all(
        expert_out.reshape(expert_count_axis, -1, model_width), "expert", 0, 0, tiled=True
    )
    expert_cot = dispatched[:, slot_width:].reshape(1, -1, model_width)
    back_gate, back_up, back_down = (full_gate, full_up, full_down)
    d_hidden = jnp.einsum("erd,ehd->erh", expert_cot, back_down, preferred_element_type=jnp.float32)
    gate_sigmoid = jax.nn.sigmoid(pre_gate)
    d_pre_gate = (
        d_hidden * pre_up * gate_sigmoid * (1.0 + pre_gate * (1.0 - gate_sigmoid))
    ).astype(jnp.bfloat16)
    d_pre_up = (d_hidden * silu_gate).astype(jnp.bfloat16)
    d_rows = (
        jnp.einsum("erh,edh->erd", d_pre_gate, back_gate, preferred_element_type=jnp.float32)
        + jnp.einsum("erh,edh->erd", d_pre_up, back_up, preferred_element_type=jnp.float32)
    ).astype(jnp.bfloat16)
    row_grads = lax.all_to_all(
        d_rows.reshape(expert_count_axis, -1, model_width), "expert", 0, 0, tiled=True
    )
    position_hits = chosen[:, :, :, None] == jnp.arange(block_rows, dtype=jnp.int32)
    indicator_matrix = position_hits.reshape(num_blocks, expert_count * pick_count, block_rows)
    gate_weighted_rows = to_blocks(slot_gate_values, num_blocks, pick_count)[
        :, :, None
    ] * to_blocks(returned, num_blocks, pick_count).astype(jnp.float32)
    mixed = (
        jnp.einsum(
            "wze,wzi->wei",
            indicator_matrix.astype(jnp.float32),
            gate_weighted_rows,
            precision=lax.Precision.HIGHEST,
        )
        .reshape(tok_rows, model_width)
        .astype(jnp.bfloat16)
    )
    slot_dots = jnp.sum(cot_rows.astype(jnp.float32) * returned.astype(jnp.float32), axis=2)
    dgate = jnp.einsum(
        "bept,ebp->bte",
        position_hits.astype(jnp.float32),
        slot_dots.reshape(expert_count, num_blocks, pick_count),
        precision=lax.Precision.HIGHEST,
    ).reshape(tok_rows, expert_count)
    d_logit = (dgate * gate_values * (1.0 - gate_values)).astype(jnp.bfloat16)
    gathered_grads = jnp.einsum(
        "wze,wzi->wei",
        indicator_matrix.astype(jnp.bfloat16),
        to_blocks(row_grads, num_blocks, pick_count),
        preferred_element_type=jnp.float32,
    ).reshape(tok_rows, model_width)
    grad_tokens = (
        gathered_grads + jnp.dot(d_logit, w_router.T, preferred_element_type=jnp.float32)
    ).astype(jnp.bfloat16)
    router_full = jnp.dot(tokens.T, d_logit, preferred_element_type=jnp.float32)
    devices = n * expert_count_axis
    router_part = jnp.sum(
        lax.all_to_all(router_full.reshape(devices, -1), ("dp", "expert"), 0, 0, tiled=True),
        axis=0,
    )
    grad_gate, grad_up, down_weight_gradient = weight_grads(
        expert_rows, hidden, expert_cot, d_pre_gate, d_pre_up, n
    )
    grad_router = lax.all_to_all(
        jnp.broadcast_to(router_part[None], (devices,) + router_part.shape),
        ("dp", "expert"),
        0,
        0,
        tiled=True,
    ).reshape(router_full.shape)
    return (mixed, grad_tokens, grad_gate, grad_up, down_weight_gradient, grad_router)


def solution(mesh):
    placed = (
        P(("dp", "expert"), None),
        P(("dp", "expert"), None),
        P(("dp", "expert"), None, None),
        P(),
        P("expert", "dp", None),
        P("expert", "dp", None),
        P("expert", "dp", None),
    )
    return jax.shard_map(
        body,
        mesh=mesh,
        in_specs=placed,
        out_specs=(
            P(("dp", "expert"), None),
            P(("dp", "expert"), None),
            P("expert", "dp", None),
            P("expert", "dp", None),
            P("expert", "dp", None),
            P(),
        ),
        check_vma=False,
    )
```
